32 devices in a mesh: pass: 16 (over z, y, core), qry: 2 (over x).
Axes of the slice: x: 2, y: 2, z: 4, core: 2. Of those that a mesh axis runs over, the one named last changes fastest.
Arguments:
- tokens: bfloat16 [4096, 1024], P(('pass', 'qry')), may hold values from -6 to 6
- w_query: bfloat16 [1024, 1024], P(None, 'qry'), may hold values from -0.1875 to 0.1875
- w_key: bfloat16 [1024, 1024], P(None, 'qry'), may hold values from -0.1875 to 0.1875
- w_value: bfloat16 [1024, 1024], P(None, 'qry'), may hold values from -0.1875 to 0.1875
- w_out: bfloat16 [1024, 1024], P('qry'), may hold values from -6 to 6
- gain_attn: float32 [1024], replicated, may hold values from 0.5 to 1.5
- shift_attn: float32 [1024], replicated, may hold values from -1.25 to 1.25
- w_up: bfloat16 [1024, 4096], P(None, 'qry'), may hold values from -0.1875 to 0.1875
- w_down: bfloat16 [4096, 1024], P('qry'), may hold values from -0.09375 to 0.09375
- gain_ffn: float32 [1024], replicated, may hold values from 0.5 to 1.5
- shift_ffn: float32 [1024], replicated, may hold values from -1.25 to 1.25
- w_colbert: bfloat16 [1024, 1024], replicated, may hold values from -0.1875 to 0.1875
- query_vecs: bfloat16 [2048, 1024], P('qry'), may hold values from -0.75 to 0.75
- match_index: int32 [2048, 4], P('qry'), may hold values from 0 to 2047
- passage_of: int32 [16], replicated, may hold values from 0 to 3, never falling along the last dimension, each value on 1 to 8 neighbouring positions
- cot_act: bfloat16 [4096, 1024], P(('pass', 'qry')), may hold values from -6 to 6
- cot_scores: float32 [32, 4], P('qry'), may hold values from -6 to 6
Outputs:
- activations: bfloat16 [4096, 1024], P(('pass', 'qry'))
- scores: float32 [32, 4], replicated
- grad_tokens: float32 [4096, 1024], P(('pass', 'qry'))
- grad_query: float32 [1024, 1024], P('pass', 'qry')
- grad_key: float32 [1024, 1024], P('pass', 'qry')
- grad_value: float32 [1024, 1024], P('pass', 'qry')
- grad_out: float32 [1024, 1024], P('qry', 'pass')
- grad_up: float32 [1024, 4096], P('pass', 'qry')
- grad_down: float32 [4096, 1024], P('qry', 'pass')
- grad_colbert: float32 [1024, 1024], replicated
- grad_gain_attn: float32 [1024], replicated
- grad_shift_attn: float32 [1024], replicated
- grad_gain_ffn: float32 [1024], replicated
- grad_shift_ffn: float32 [1024], replicated
The draws below stay inside these ranges and needn't reach their ends.
Inputs may be any that keep to these rules, and one draw needn't show every extreme that they name: `passage_of`: entry p is the passage of the 256 tokens of pass index p; numbers never fall along p, every passage 0 to 3 holds 1 to 8 consecutive indices, and one holds exactly 8.
All inputs are finite; a program needn't handle non-finite values.
Results may differ from the reference program's by a relative error of at most 0.023.
Values may be sent and summed in bfloat16 or wider, within the bound.
No kernel may reach another device: no remote copies, remote signals or barrier semaphores. Data moves between devices by JAX's collectives and lax.ppermute only.
A program may use at most 192 MiB of HBM per device.

```python
import math
import jax
import jax.numpy as jnp
import numpy as np
from jax import lax

D = 1024
HEADS = 16
HD = 64
FF = 4096
TOK_PASS = 256
QLEN = 64
SPAN = 8
TOKENS = 4096
NSEQ = 4
NQ = 32
QTOK = 2048
N_PASS = 16


def set_ends(values, stream_key, least, top_value):
    longest = values.shape.index(max(values.shape))
    spots = []
    for shift in (0, 1):
        where = [jax.random.randint(jax.random.fold_in(stream_key, axis), (), 0, length) for axis, length in enumerate(values.shape)]
        where[longest] = (where[longest] + shift) % values.shape[longest]
        spots.append(tuple(where))
    return values.at[spots[0]].set(least).at[spots[1]].set(top_value)


def levels(key, shape, cuts, least, largest):
    def one(dim, parts):
        heights = jax.random.uniform(jax.random.fold_in(jax.random.fold_in(key, 6), dim), (parts,), jnp.float32, least / len(cuts), largest / len(cuts))
        return jnp.repeat(jnp.exp(heights), shape[dim] // parts).reshape((-1,) + (1,) * (len(shape) - dim - 1))

    loudness = one(*cuts[0])
    for cut in cuts[1:]:
        loudness = loudness * one(*cut)
    return loudness


def split_up(number_of, total, bound, lean):
    loads = [(1 << 20) // math.isqrt(grade ** lean) + 1 for grade in range(2, number_of + 1)]
    spare, holding = total - bound - (number_of - 1), [1] * (number_of - 1)
    while spare > 0:
        movable = [i for i in range(number_of - 1) if holding[i] < bound]
        mass, left = sum([loads[i] for i in movable]), spare
        for i in movable:
            extra = min(bound - holding[i], max(1, left * loads[i] // mass), spare)
            holding[i] = holding[i] + extra
            spare = spare - extra
    return np.array([bound] + holding)


def uneven_parts(rng, count, total, limit, slope):
    if count == 2:
        one = jax.random.randint(rng, (), max(1, total - limit), min(limit, total - 1) + 1)
        return jnp.stack([one, total - one])
    sizes = jnp.asarray(split_up(count, total, limit, slope), jnp.int32)
    couples = (count - 1) // 2
    giver, sink = sizes[1:1 + 2 * couples:2], sizes[2:2 + 2 * couples:2]
    room = jnp.minimum(giver - 1, limit - sink)
    moved = jax.random.randint(jax.random.fold_in(rng, 1), (couples,), 0, 1 << 20) % (room + 1)
    sizes = sizes.at[1:1 + 2 * couples:2].set(giver - moved).at[2:2 + 2 * couples:2].set(sink + moved)
    return sizes[jax.random.permutation(jax.random.fold_in(rng, 2), count)]


def normal_values(rng, extent, width, limit, cuts=(), kind=jnp.bfloat16):
    result = width * jax.random.normal(rng, extent, jnp.float32)
    if cuts:
        result = result * levels(rng, extent, cuts, -0.22, 0.18)
    return jnp.clip(result, -limit, limit).astype(kind)


def setup_inputs(seed: int = 0) -> dict:
    arg_keys = jax.random.split(jax.random.key(seed), 18)
    tokens = normal_values(arg_keys[0], (TOKENS, D), 1.0, 6.0, ((0, 32),))
    w_query = normal_values(arg_keys[1], (D, D), D ** -0.5, 0.1875, ((1, 2),))
    w_key = normal_values(arg_keys[2], (D, D), D ** -0.5, 0.1875, ((1, 2),))
    w_value = normal_values(arg_keys[3], (D, D), D ** -0.5, 0.1875, ((1, 2),))
    w_out = normal_values(arg_keys[4], (D, D), (max(1, D // (4 * TOK_PASS))) ** -0.5, 6.0, ((0, 2),))
    gain_attn = jnp.clip(1.0 + 0.1 * jax.random.normal(arg_keys[5], (D,), jnp.float32), 0.5, 1.5)
    shift_attn = normal_values(arg_keys[6], (D,), 0.2, 1.25, (), jnp.float32)
    w_up = normal_values(arg_keys[7], (D, FF), D ** -0.5, 0.1875, ((1, 2),))
    w_down = normal_values(arg_keys[8], (FF, D), FF ** -0.5, 0.09375, ((0, 2),))
    gain_ffn = jnp.clip(1.0 + 0.1 * jax.random.normal(arg_keys[9], (D,), jnp.float32), 0.5, 1.5)
    shift_ffn = normal_values(arg_keys[10], (D,), 0.2, 1.25, (), jnp.float32)
    w_colbert = normal_values(arg_keys[11], (D, D), D ** -0.5, 0.1875)
    query_vecs = normal_values(arg_keys[12], (QTOK, D), 0.125, 0.75, ((0, 2),))
    match_index = set_ends(jax.random.randint(arg_keys[13], (QTOK, NSEQ), 0, SPAN * TOK_PASS), jax.random.fold_in(arg_keys[13], 1), 0, (SPAN * TOK_PASS) - 1).astype(jnp.int32)
    passage_of = jnp.searchsorted(jnp.cumsum(uneven_parts(arg_keys[14], NSEQ, N_PASS, SPAN, 2)), jnp.arange(N_PASS), side="right").astype(jnp.int32)
    cot_act = normal_values(arg_keys[15], (TOKENS, D), 1.0, 6.0, ((0, 32),))
    cot_scores = normal_values(arg_keys[16], (NQ, NSEQ), 1.0, 6.0, ((0, 2),), jnp.float32)
    return {"tokens": tokens, "w_query": w_query, "w_key": w_key, "w_value": w_value, "w_out": w_out, "gain_attn": gain_attn, "shift_attn": shift_attn, "w_up": w_up, "w_down": w_down, "gain_ffn": gain_ffn, "shift_ffn": shift_ffn, "w_colbert": w_colbert, "query_vecs": query_vecs, "match_index": match_index, "passage_of": passage_of, "cot_act": cot_act, "cot_scores": cot_scores}


@jax.custom_vjp
def low(v):
    return lax.optimization_barrier(v.astype(jnp.bfloat16)).astype(jnp.float32)

@jax.custom_vjp
def low_back(v):
    return v

def low_keep(v):
    return (low(v), None)

def low_pass(kept, grad):
    return (grad,)

def back_keep(v):
    return (v, None)

def back_low(kept, grad):
    return (low(grad),)
low.defvjp(low_keep, low_pass)
low_back.defvjp(back_keep, back_low)
HIGHEST_PRECISION = lax.Precision.HIGHEST

def matmul(left, right):
    return jnp.dot(left, right, precision=HIGHEST_PRECISION, preferred_element_type=jnp.float32)

def layer_norm(values, gain, shift):
    row_mean = lax.optimization_barrier(jnp.mean(values, axis=-1, keepdims=True))
    centred = values - row_mean
    variance = lax.optimization_barrier(jnp.mean(centred * centred, axis=-1, keepdims=True))
    return centred * lax.rsqrt(variance + 1e-05) * gain + shift

def gelu_exact(values):
    return 0.5 * values * (1.0 + jax.scipy.special.erf(values * 0.7071067811865476))

def passage_table(passage_of):
    numbers = jnp.arange(NSEQ, dtype=jnp.int32)
    counts = lax.optimization_barrier(jnp.sum((passage_of[None, :] == numbers[:, None]).astype(jnp.int32), axis=1))
    before = lax.optimization_barrier(jnp.sum((passage_of[None, :] < numbers[:, None]).astype(jnp.int32), axis=1))
    return (before * TOK_PASS, counts * TOK_PASS)

def attention(queries, key_rows, value_rows, passage_of):
    blocks = N_PASS
    groups = HEADS // 4
    margin = (SPAN - 1) * TOK_PASS
    window = (2 * SPAN - 1) * TOK_PASS
    key_pad = jnp.pad(key_rows.reshape(TOKENS, HEADS, HD), ((margin, margin), (0, 0), (0, 0)))
    value_pad = jnp.pad(value_rows.reshape(TOKENS, HEADS, HD), ((margin, margin), (0, 0), (0, 0)))
    edge_ids = jnp.full((SPAN - 1,), -1, jnp.int32)
    ids_pad = jnp.concatenate([edge_ids, passage_of.astype(jnp.int32), edge_ids])
    query_items = queries.reshape(blocks, TOK_PASS, groups, 4, HD).transpose(0, 2, 1, 3, 4)
    query_items = query_items.reshape(blocks * groups, TOK_PASS, 4, HD)
    zero_index = jnp.zeros((), jnp.int32)

    def one_item(item_pair):
        item_index, query_block = item_pair
        block_index = (item_index // groups).astype(jnp.int32)
        group_index = (item_index % groups).astype(jnp.int32)
        first_row = (block_index * TOK_PASS).astype(jnp.int32)
        key_block = lax.dynamic_slice(key_pad, (first_row, group_index * 4, zero_index), (window, 4, HD))
        value_block = lax.dynamic_slice(value_pad, (first_row, group_index * 4, zero_index), (window, 4, HD))
        window_ids = jnp.repeat(lax.dynamic_slice(ids_pad, (block_index,), (2 * SPAN - 1,)), TOK_PASS)
        allowed = window_ids == passage_of[block_index]
        raw_scores = low_back(jnp.einsum('qhd,khd->hqk', query_block, key_block, precision=HIGHEST_PRECISION))
        scaled = jnp.where(allowed[None, None, :], raw_scores * 0.125, -1e+30)
        log_total = jax.nn.logsumexp(scaled, axis=2, keepdims=True)
        weights = low(jnp.exp(scaled - log_total))
        return jnp.einsum('hqk,khd->qhd', weights, value_block, precision=HIGHEST_PRECISION)
    results = lax.map(jax.checkpoint(one_item), (jnp.arange(blocks * groups, dtype=jnp.int32), query_items))
    results = results.reshape(blocks, groups, TOK_PASS, 4, HD).transpose(0, 2, 1, 3, 4)
    return results.reshape(TOKENS, HEADS * HD)

def forward(tokens, w_query, w_key, w_value, w_out, gain_attn, shift_attn, w_up, w_down, gain_ffn, shift_ffn, w_colbert, query_vecs, match_index, passage_of):
    queries = low_back(low(matmul(tokens, w_query)))
    key_rows = low_back(low(matmul(tokens, w_key)))
    value_rows = low_back(low(matmul(tokens, w_value)))
    context = low_back(low(attention(queries, key_rows, value_rows, passage_of)))
    attn_rows = low_back(matmul(context, w_out))
    hidden = layer_norm(tokens + attn_rows, gain_attn, shift_attn)
    inner_pre = low_back(matmul(low(hidden), w_up))
    gated_low = low(gelu_exact(inner_pre))
    ffn_rows = low_back(matmul(gated_low, w_down))
    output = layer_norm(hidden + ffn_rows, gain_ffn, shift_ffn)
    proj_rows = low_back(matmul(low(output), w_colbert))
    unit_vecs = low(proj_rows * lax.rsqrt(lax.optimization_barrier(jnp.sum(proj_rows * proj_rows, axis=1, keepdims=True)) + 1e-06))
    starts, lengths = passage_table(passage_of)
    pick_rows = starts[None, :] + match_index % lengths[None, :]

    def one_passage(columns):
        picked = low_back(unit_vecs[columns])
        return lax.optimization_barrier(jnp.sum(query_vecs * picked, axis=1))
    match_vals = lax.map(one_passage, pick_rows.T)
    scores = lax.optimization_barrier(jnp.sum(match_vals.reshape(NSEQ, NQ, QLEN), axis=2)).T
    return (output, scores)

def reference(tokens, w_query, w_key, w_value, w_out, gain_attn, shift_attn, w_up, w_down, gain_ffn, shift_ffn, w_colbert, query_vecs, match_index, passage_of, cot_act, cot_scores):
    floats = [tokens, w_query, w_key, w_value, w_out, gain_attn, shift_attn, w_up, w_down, gain_ffn, shift_ffn, w_colbert]
    floats = [entry.astype(jnp.float32) for entry in floats]
    query_float = query_vecs.astype(jnp.float32)

    def closed(*params):
        return forward(*params, query_float, match_index, passage_of)
    (output, scores), pullback = jax.vjp(closed, *floats)
    gradients = pullback((cot_act.astype(jnp.float32), cot_scores.astype(jnp.float32)))
    return (output.astype(jnp.bfloat16), scores, gradients[0], gradients[1], gradients[2], gradients[3], gradients[4], gradients[7], gradients[8], gradients[11], gradients[5], gradients[6], gradients[9], gradients[10])
```

```python
import functools
import math

import jax
import jax.numpy as jnp
from jax import lax
from jax.experimental import pallas as pl
from jax.experimental.pallas import tpu as pltpu
from jax.sharding import PartitionSpec as P

HD = 64
SPAN = 8
LANES = 128
VMEM_LIMIT = 56 << 20
LOG2E = math.log2(math.e)


def passed_along(value, axis, steps):
    count = lax.axis_size(axis)
    first, last = (max(0, -steps), min(count, count - steps))
    return lax.ppermute(value, axis, [(source, source + steps) for source in range(first, last)])


def layer_norm(values, gain, shift):
    row_mean = jnp.mean(values, axis=-1, keepdims=True)
    centred = values - row_mean
    variance = jnp.mean(centred * centred, axis=-1, keepdims=True)
    return centred * lax.rsqrt(variance + 1e-05) * gain + shift


def gelu_exact(values):
    return 0.5 * values * (1.0 + jax.scipy.special.erf(values * 0.7071067811865476))


def normalize_rows(proj_rows):
    return proj_rows * lax.rsqrt(jnp.sum(proj_rows * proj_rows, axis=1, keepdims=True) + 1e-06)


def head_split(array):
    return array.reshape(array.shape[0], array.shape[1] // HD, HD)


def block_scores(queries, key_rows):
    return jnp.einsum("qhd,khd->hqk", queries, key_rows, preferred_element_type=jnp.float32) * 0.125


def grad_block(queries, ctx_grad, log_total, row_delta, key_rows, value_rows):
    scaled = block_scores(queries, key_rows)
    probs = jnp.exp(scaled - log_total[:, :, None])
    dprob = jnp.einsum("qhd,khd->hqk", ctx_grad, value_rows, preferred_element_type=jnp.float32)
    dscore = (0.125 * probs * (dprob - row_delta[:, :, None])).astype(jnp.bfloat16)
    dquery = jnp.einsum("hqk,khd->qhd", dscore, key_rows, preferred_element_type=jnp.float32)
    dkey = jnp.einsum("hqk,qhd->khd", dscore, queries, preferred_element_type=jnp.float32)
    dvalue = jnp.einsum(
        "hqk,qhd->khd", probs.astype(jnp.bfloat16), ctx_grad, preferred_element_type=jnp.float32
    )
    return (dquery, jnp.stack([dkey, dvalue]))


def contract_rows(left, right):
    return lax.dot_general(
        left, right, (((0,), (0,)), ((), ())), preferred_element_type=jnp.float32
    )


def contract_cols(left, right):
    return lax.dot_general(
        left, right, (((1,), (1,)), ((), ())), preferred_element_type=jnp.float32
    )


def local_general(
    tokens,
    w_query,
    w_key,
    w_value,
    w_out,
    gain_attn,
    shift_attn,
    w_up,
    w_down,
    gain_ffn,
    shift_ffn,
    w_colbert,
    query_vecs,
    match_index,
    passage_of,
    cot_act,
    cot_scores,
):
    pass_count = lax.axis_size("pass")
    qry_count = lax.axis_size("qry")
    pass_index = lax.axis_index("pass")
    qry_index = lax.axis_index("qry")
    own_id = passage_of[pass_index]

    def source_valid(offset):
        source = pass_index - offset
        inside = (source >= 0) & (source < pass_count)
        return inside & (passage_of[jnp.clip(source, 0, pass_count - 1)] == own_id)

    gathered = lax.all_gather(tokens, "qry", axis=0, tiled=True)
    block_rows = gathered.shape[0]
    local_width = w_query.shape[1]
    w_qkv = jnp.concatenate([w_query, w_key, w_value], axis=1)
    qkv_rows = jnp.dot(gathered, w_qkv, preferred_element_type=jnp.float32).astype(jnp.bfloat16)
    query_flat = qkv_rows[:, :local_width]
    key_flat = qkv_rows[:, local_width : 2 * local_width]
    value_flat = qkv_rows[:, 2 * local_width :]
    queries = head_split(query_flat)
    heads = queries.shape[1]
    own_pair = jnp.stack([key_flat, value_flat])
    offsets = [distance for distance in range(1, SPAN)] + [-distance for distance in range(1, SPAN)]

    def fetch_keys():
        received = []
        for offset in offsets:
            received.append(passed_along(own_pair, "pass", offset))
        return received

    remote = fetch_keys()

    def stat_of(kv_pair):
        return jax.nn.logsumexp(block_scores(queries, head_split(kv_pair[0])), axis=2)

    log_total = stat_of(own_pair)
    for offset, kv_pair in zip(offsets, remote):
        log_total = lax.cond(
            source_valid(offset),
            lambda current, kv_pair=kv_pair: jnp.logaddexp(current, stat_of(kv_pair)),
            lambda current: current,
            log_total,
        )

    def weighted(kv_pair):
        probs = jnp.exp(
            block_scores(queries, head_split(kv_pair[0])) - log_total[:, :, None]
        ).astype(jnp.bfloat16)
        return jnp.einsum(
            "hqk,khd->qhd", probs, head_split(kv_pair[1]), preferred_element_type=jnp.float32
        )

    context = weighted(own_pair)
    for offset, kv_pair in zip(offsets, remote):
        context = lax.cond(
            source_valid(offset),
            lambda running, kv_pair=kv_pair: running + weighted(kv_pair),
            lambda running: running,
            context,
        )
    context_low = context.reshape(block_rows, local_width).astype(jnp.bfloat16)
    piece_rows = context_low
    attn_rows = lax.psum_scatter(
        jnp.dot(piece_rows, w_out, preferred_element_type=jnp.float32).astype(jnp.bfloat16),
        "qry",
        scatter_dimension=0,
        tiled=True,
    ).astype(jnp.float32)
    hidden, norm_attn_back = jax.vjp(
        layer_norm, tokens.astype(jnp.float32) + attn_rows, gain_attn, shift_attn
    )
    hidden_all = lax.all_gather(hidden.astype(jnp.bfloat16), "qry", axis=0, tiled=True)
    inner_pre = jnp.dot(hidden_all, w_up, preferred_element_type=jnp.float32)
    gated_float, gelu_back = jax.vjp(gelu_exact, inner_pre)
    gated_low = gated_float.astype(jnp.bfloat16)
    piece_rows = gated_low
    ffn_rows = lax.psum_scatter(
        jnp.dot(piece_rows, w_down, preferred_element_type=jnp.float32).astype(jnp.bfloat16),
        "qry",
        scatter_dimension=0,
        tiled=True,
    ).astype(jnp.float32)
    output, norm_ffn_back = jax.vjp(layer_norm, hidden + ffn_rows, gain_ffn, shift_ffn)
    output_low = output.astype(jnp.bfloat16)
    proj_rows = jnp.dot(output_low, w_colbert, preferred_element_type=jnp.float32)
    unit_vecs, unit_back = jax.vjp(normalize_rows, proj_rows)
    unit_all = lax.all_gather(unit_vecs.astype(jnp.bfloat16), "qry", axis=0, tiled=True)
    seq_count = match_index.shape[1]
    query_rows = cot_scores.shape[0]
    numbers = jnp.arange(seq_count, dtype=jnp.int32)
    pick_col = numbers == own_id
    span_count = jnp.sum((passage_of == own_id).astype(jnp.int32))
    first_index = jnp.sum((passage_of < own_id).astype(jnp.int32))
    length = span_count * block_rows
    raw_pick = jnp.sum(jnp.where(pick_col[None, :], match_index, 0), axis=1)
    local_row = raw_pick % length - (pass_index - first_index) * block_rows
    one_hot = (local_row[:, None] == jnp.arange(block_rows, dtype=jnp.int32)[None, :]).astype(
        jnp.bfloat16
    )
    picked = jnp.dot(one_hot, unit_all, preferred_element_type=jnp.float32)
    query_float = query_vecs.astype(jnp.float32)
    match_vals = jnp.sum(query_float * picked, axis=1)
    per_query = jnp.sum(match_vals.reshape(query_rows, -1), axis=1)
    score_block = per_query[:, None] * pick_col.astype(jnp.float32)[None, :]
    score_part = lax.dynamic_update_slice(
        jnp.zeros((query_rows * qry_count, seq_count), jnp.float32),
        score_block,
        (qry_index * query_rows, jnp.zeros((), jnp.int32)),
    )
    cot_pick = jnp.sum(jnp.where(pick_col[None, :], cot_scores, 0.0), axis=1)
    token_weight = jnp.repeat(cot_pick, query_vecs.shape[0] // query_rows)
    weighted_queries = (token_weight[:, None] * query_float).astype(jnp.bfloat16)
    piece_rows = one_hot
    unit_grad = lax.psum_scatter(
        contract_rows(piece_rows, weighted_queries).astype(jnp.bfloat16),
        "qry",
        scatter_dimension=0,
        tiled=True,
    ).astype(jnp.float32)
    (proj_grad,) = unit_back(unit_grad)
    proj_low = proj_grad.astype(jnp.bfloat16)
    grad_colbert = contract_rows(output_low, proj_low)
    out_grad = cot_act.astype(jnp.float32) + contract_cols(proj_low, w_colbert)
    pre_grad, grad_gain_ffn, grad_shift_ffn = norm_ffn_back(out_grad)
    ffn_all = lax.all_gather(pre_grad.astype(jnp.bfloat16), "qry", axis=0, tiled=True)
    gated_grad = contract_cols(ffn_all, w_down)
    grad_down = contract_rows(gated_low, ffn_all)
    (inner_grad,) = gelu_back(gated_grad)
    inner_low = inner_grad.astype(jnp.bfloat16)
    grad_up = contract_rows(hidden_all, inner_low)
    piece_rows = inner_low
    hidden_grad = pre_grad + lax.psum_scatter(
        contract_cols(piece_rows, w_up).astype(jnp.bfloat16), "qry", scatter_dimension=0, tiled=True
    ).astype(jnp.float32)
    attn_pre_grad, grad_gain_attn, grad_shift_attn = norm_attn_back(hidden_grad)
    attn_all = lax.all_gather(attn_pre_grad.astype(jnp.bfloat16), "qry", axis=0, tiled=True)
    grad_out = contract_rows(context_low, attn_all)
    ctx_grad = head_split(contract_cols(attn_all, w_out).astype(jnp.bfloat16))
    row_delta = jnp.einsum("qhd,qhd->hq", ctx_grad.astype(jnp.float32), context)
    remote_back = fetch_keys()
    dquery, dkv_own = grad_block(
        queries, ctx_grad, log_total, row_delta, head_split(key_flat), head_split(value_flat)
    )
    key_value_grad = dkv_own
    zero_query = jnp.zeros_like(dquery)
    zero_pair = jnp.zeros((2, block_rows, heads, HD), jnp.float32)
    for offset, kv_pair in zip(offsets, remote_back):
        query_part, pair_part = lax.cond(
            source_valid(offset),
            lambda incoming: grad_block(
                queries,
                ctx_grad,
                log_total,
                row_delta,
                head_split(incoming[0]),
                head_split(incoming[1]),
            ),
            lambda incoming: (zero_query, zero_pair),
            kv_pair,
        )
        dquery = dquery + query_part
        returned = passed_along(
            pair_part.reshape(2, block_rows, local_width).astype(jnp.bfloat16), "pass", -offset
        ).astype(jnp.float32)
        key_value_grad = key_value_grad + returned.reshape(2, block_rows, heads, HD)
    dqkv_low = jnp.concatenate(
        [
            dquery.reshape(block_rows, local_width),
            key_value_grad[0].reshape(block_rows, local_width),
            key_value_grad[1].reshape(block_rows, local_width),
        ],
        axis=1,
    ).astype(jnp.bfloat16)
    grad_qkv = contract_rows(gathered, dqkv_low)
    piece_rows = dqkv_low
    grad_tokens = attn_pre_grad + lax.psum_scatter(
        contract_cols(piece_rows, w_qkv).astype(jnp.bfloat16),
        "qry",
        scatter_dimension=0,
        tiled=True,
    ).astype(jnp.float32)
    summed = (
        lax.psum_scatter(
            grad_qkv[:, :local_width].astype(jnp.bfloat16), "pass", scatter_dimension=0, tiled=True
        ).astype(jnp.float32),
        lax.psum_scatter(
            grad_qkv[:, local_width : 2 * local_width].astype(jnp.bfloat16),
            "pass",
            scatter_dimension=0,
            tiled=True,
        ).astype(jnp.float32),
        lax.psum_scatter(
            grad_qkv[:, 2 * local_width :].astype(jnp.bfloat16),
            "pass",
            scatter_dimension=0,
            tiled=True,
        ).astype(jnp.float32),
        lax.psum_scatter(
            grad_out.astype(jnp.bfloat16), "pass", scatter_dimension=1, tiled=True
        ).astype(jnp.float32),
        lax.psum_scatter(
            grad_up.astype(jnp.bfloat16), "pass", scatter_dimension=0, tiled=True
        ).astype(jnp.float32),
        lax.psum_scatter(
            grad_down.astype(jnp.bfloat16), "pass", scatter_dimension=1, tiled=True
        ).astype(jnp.float32),
    )
    shared = lax.psum(
        (grad_colbert, grad_gain_attn, grad_shift_attn, grad_gain_ffn, grad_shift_ffn, score_part),
        ("pass", "qry"),
    )
    return (
        output_low,
        shared[5],
        grad_tokens,
        summed[0],
        summed[1],
        summed[2],
        summed[3],
        summed[4],
        summed[5],
        shared[0],
        shared[1],
        shared[2],
        shared[3],
        shared[4],
    )


def swap_over(value, axis, mask):
    count = lax.axis_size(axis)
    return lax.ppermute(value, axis, [(index, index ^ mask) for index in range(count)])


def ring_chips(chips):
    layers = chips // 2
    return [2 * z for z in range(layers)] + [2 * z + 1 for z in reversed(range(layers))]


def low_lanes(rows):
    return lax.broadcasted_iota(jnp.int32, (rows, LANES), 1) < HD


def split_lanes(first, second):
    low = low_lanes(first.shape[0])
    return (
        jnp.where(low, first, pltpu.roll(second, HD, 1)),
        jnp.where(low, pltpu.roll(first, HD, 1), second),
    )


def dot_nn(left, right):
    return jnp.dot(left, right, preferred_element_type=jnp.float32)


def dot_nt(left, right):
    return contract_cols(left, right)


def params(*semantics):
    return pltpu.CompilerParams(
        dimension_semantics=semantics or None, vmem_limit_bytes=VMEM_LIMIT
    )


def cost(flops, moved, transcendentals=0):
    return pl.CostEstimate(
        flops=int(flops), bytes_accessed=int(moved), transcendentals=int(transcendentals)
    )


def project_body(x_ref, wq_ref, wk_ref, wv_ref, out_ref):
    x = x_ref[...]
    rows = x.shape[0]
    half = rows // 2
    query = dot_nn(x, wq_ref[...])
    key = dot_nn(x, wk_ref[...])
    value = dot_nn(x, wv_ref[...])
    for pair in range(query.shape[1] // LANES):
        cols = slice(pair * LANES, (pair + 1) * LANES)
        first, second = split_lanes(key[:, cols], value[:, cols])
        out_ref[2 * pair, 0:rows] = first.astype(jnp.bfloat16)
        out_ref[2 * pair + 1, 0:rows] = second.astype(jnp.bfloat16)
        first, second = split_lanes(query[:half, cols], query[half:, cols])
        out_ref[2 * pair, rows : rows + half] = first.astype(jnp.bfloat16)
        out_ref[2 * pair + 1, rows : rows + half] = second.astype(jnp.bfloat16)


def project(x, wq, wk, wv):
    rows, depth = x.shape
    width = wq.shape[1]
    heads = width // HD
    steps = 2
    weight = pl.BlockSpec((depth, width // steps), lambda i: (0, i))
    return pl.pallas_call(
        project_body,
        grid=(steps,),
        in_specs=[pl.BlockSpec((rows, depth), lambda i: (0, 0)), weight, weight, weight],
        out_specs=pl.BlockSpec((heads // steps, rows * 3 // 2, LANES), lambda i: (i, 0, 0)),
        out_shape=jax.ShapeDtypeStruct((heads, rows * 3 // 2, LANES), jnp.bfloat16),
        compiler_params=params("arbitrary"),
        cost_estimate=cost(2 * rows * depth * width * 3, 2 * (3 * depth * width + 4 * rows * depth)),
        name="project",
    )(x, wq, wk, wv)


def load_query(packed):
    wide = packed.astype(jnp.float32)
    low = low_lanes(wide.shape[0])
    top = jnp.where(low, wide, 0.0)
    bottom = jnp.where(low, pltpu.roll(wide, HD, 1), 0.0)
    return jnp.concatenate([top, bottom], axis=0).astype(jnp.bfloat16)


def pack_transposed(columns):
    half = columns.shape[1] // 2
    return jnp.concatenate([columns[:, :half], columns[:, half:]], axis=0).T


def attend_body(info_ref, own_ref, sib_ref, ctx_ref, ctxt_ref, lse_ref, kv_s, vt_s, score_s):
    chips = own_ref.shape[0]
    blocks = 2 * chips
    rows = kv_s.shape[1]
    parity = info_ref[2 * blocks]
    scale = 0.125 * LOG2E
    ones_rows = lax.broadcasted_iota(jnp.int32, (LANES, rows), 0) < HD

    def gather(chip, carry):
        for ref, which in ((own_ref, parity), (sib_ref, 1 - parity)):
            block = ref[chip, 0:rows]
            kv_s[2 * chip + which] = block
            turned = block.astype(jnp.float32).T
            vt_s[2 * chip + which] = jnp.where(ones_rows, 1.0, turned).astype(jnp.bfloat16)
        return carry

    lax.fori_loop(0, chips, gather, 0)

    def one_block(item, carry):
        block = 2 * item + parity
        first = info_ref[block]
        count = info_ref[blocks + block]
        query = load_query(own_ref[item, rows : rows + rows // 2])

        def scores(step, top):
            score = dot_nt(kv_s[first + step], query) * scale
            score_s[step] = score
            return jnp.maximum(top, jnp.max(score.reshape(rows // 8, 8, rows), axis=0))

        top = lax.fori_loop(0, count, scores, jnp.full((8, rows), -jnp.inf, jnp.float32))
        top = jnp.max(top, axis=0, keepdims=True)

        def weigh(step, total):
            prob = jnp.exp2(score_s[step] - top).astype(jnp.bfloat16)
            return total + dot_nn(vt_s[first + step], prob)

        total = lax.fori_loop(0, count, weigh, jnp.zeros((LANES, rows), jnp.float32))
        weight = total[0:1]
        context = total[HD:] / weight
        ctxt_ref[item] = context
        lse_ref[item] = jnp.broadcast_to(top + jnp.log2(weight), (8, rows))
        ctx_ref[item] = pack_transposed(context).astype(jnp.bfloat16)
        return carry

    lax.fori_loop(0, chips, one_block, 0)


def whole():
    return pl.BlockSpec(memory_space=pltpu.VMEM)


def attend(info, own, sib):
    chips, packed, _ = own.shape
    rows = packed * 2 // 3
    blocks = 2 * chips
    return pl.pallas_call(
        attend_body,
        in_specs=[pl.BlockSpec(memory_space=pltpu.SMEM), whole(), whole()],
        out_specs=[whole(), whole(), whole()],
        out_shape=[
            jax.ShapeDtypeStruct((chips, rows // 2, LANES), jnp.bfloat16),
            jax.ShapeDtypeStruct((chips, HD, rows), jnp.float32),
            jax.ShapeDtypeStruct((chips, 8, rows), jnp.float32),
        ],
        scratch_shapes=[
            pltpu.VMEM((blocks, rows, LANES), jnp.bfloat16),
            pltpu.VMEM((blocks, LANES, rows), jnp.bfloat16),
            pltpu.VMEM((SPAN, rows, rows), jnp.float32),
        ],
        compiler_params=params(),
        cost_estimate=cost(2 * 2 * 40 * rows * rows * LANES, 4 << 20, 40 * rows * rows),
        name="attend",
    )(info, own, sib)


def attend_back_body(
    info_ref, own_ref, sib_ref, dctx_ref, ctxt_ref, lse_ref, dkv_ref, dq_ref, kv_s, kt_s, acc_s
):
    chips = own_ref.shape[0]
    blocks = 2 * chips
    rows = kv_s.shape[1]
    half = rows // 2
    parity = info_ref[2 * blocks]
    scale = 0.125 * LOG2E

    def gather(chip, carry):
        for ref, which in ((own_ref, parity), (sib_ref, 1 - parity)):
            block = ref[chip, 0:rows]
            kv_s[2 * chip + which] = block
            turned = block.astype(jnp.float32).T
            kt_s[2 * chip + which] = turned[0:HD].astype(jnp.bfloat16)
            acc_s[2 * chip + which] = jnp.zeros((rows, LANES), jnp.float32)
        return carry

    lax.fori_loop(0, chips, gather, 0)
    low = low_lanes(half)

    def one_block(item, carry):
        block = 2 * item + parity
        first = info_ref[block]
        count = info_ref[blocks + block]
        query = load_query(own_ref[item, rows : rows + half])
        packed = dctx_ref[item].astype(jnp.float32)
        top = jnp.where(low, 0.0, pltpu.roll(packed, HD, 1))
        bottom = jnp.where(low, 0.0, packed)
        dctx = jnp.concatenate([top, bottom], axis=0).astype(jnp.bfloat16)
        turned = packed.T
        dctx_t = jnp.concatenate([turned[:HD], turned[HD:]], axis=1)
        delta = jnp.sum(dctx_t * ctxt_ref[item], axis=0, keepdims=True)
        lse = lse_ref[item, 0:1]
        both = jnp.concatenate([query, dctx], axis=0)

        def step_block(step, dq):
            kv = kv_s[first + step]
            prob = jnp.exp2(dot_nt(kv, query) * scale - lse)
            dprob = dot_nt(kv, dctx)
            dscore = (0.125 * prob * (dprob - delta)).astype(jnp.bfloat16)
            pair = jnp.concatenate([dscore, prob.astype(jnp.bfloat16)], axis=1)
            acc_s[first + step] += dot_nn(pair, both)
            return dq + dot_nn(kt_s[first + step], dscore)

        dq = lax.fori_loop(0, count, step_block, jnp.zeros((HD, rows), jnp.float32))
        dq_ref[item] = pack_transposed(dq).astype(jnp.bfloat16)
        return carry

    lax.fori_loop(0, chips, one_block, 0)

    def finish(index, carry):
        dkv_ref[index] = acc_s[index].astype(jnp.bfloat16)
        return carry

    lax.fori_loop(0, blocks, finish, 0)


def attend_back(info, own, sib, dctx, ctxt, lse):
    chips, packed, _ = own.shape
    rows = packed * 2 // 3
    blocks = 2 * chips
    return pl.pallas_call(
        attend_back_body,
        in_specs=[pl.BlockSpec(memory_space=pltpu.SMEM)] + [whole()] * 5,
        out_specs=[whole(), whole()],
        out_shape=[
            jax.ShapeDtypeStruct((blocks, rows, LANES), jnp.bfloat16),
            jax.ShapeDtypeStruct((chips, rows // 2, LANES), jnp.bfloat16),
        ],
        scratch_shapes=[
            pltpu.VMEM((blocks, rows, LANES), jnp.bfloat16),
            pltpu.VMEM((blocks, HD, rows), jnp.bfloat16),
            pltpu.VMEM((blocks, rows, LANES), jnp.float32),
        ],
        compiler_params=params(),
        cost_estimate=cost(2 * 5 * 40 * rows * rows * LANES, 5 << 20, 40 * rows * rows),
        name="attend_back",
    )(info, own, sib, dctx, ctxt, lse)


def out_project_body(in_ref, w_ref, ctx_ref, own_ref, send_ref):
    heads, half, _ = in_ref.shape
    for pair in range(heads // 2):
        cols = slice(pair * LANES, (pair + 1) * LANES)
        top, bottom = split_lanes(
            in_ref[2 * pair].astype(jnp.float32), in_ref[2 * pair + 1].astype(jnp.float32)
        )
        ctx_ref[0:half, cols] = top.astype(jnp.bfloat16)
        ctx_ref[half:, cols] = bottom.astype(jnp.bfloat16)
    rows = dot_nn(ctx_ref[...], w_ref[...])
    own_ref[...] = rows[:half]
    send_ref[...] = rows[half:].astype(jnp.bfloat16)


def out_project(packed, w_out):
    heads, half, _ = packed.shape
    width, depth = w_out.shape
    return pl.pallas_call(
        out_project_body,
        in_specs=[whole()] * 2,
        out_specs=[whole()] * 3,
        out_shape=[
            jax.ShapeDtypeStruct((2 * half, width), jnp.bfloat16),
            jax.ShapeDtypeStruct((half, depth), jnp.float32),
            jax.ShapeDtypeStruct((half, depth), jnp.bfloat16),
        ],
        compiler_params=params(),
        cost_estimate=cost(4 * half * width * depth, 3 << 20),
        name="out_project",
    )(packed, w_out)


def ctx_grad_body(g_ref, w_ref, out_ref):
    half = out_ref.shape[1]
    grad = dot_nt(g_ref[...], w_ref[...])
    for pair in range(grad.shape[1] // LANES):
        cols = slice(pair * LANES, (pair + 1) * LANES)
        first, second = split_lanes(grad[:half, cols], grad[half:, cols])
        out_ref[2 * pair] = first.astype(jnp.bfloat16)
        out_ref[2 * pair + 1] = second.astype(jnp.bfloat16)


def ctx_grad_packed(grad_all, w_out):
    rows, depth = grad_all.shape
    width = w_out.shape[0]
    return pl.pallas_call(
        ctx_grad_body,
        in_specs=[whole()] * 2,
        out_specs=whole(),
        out_shape=jax.ShapeDtypeStruct((width // HD, rows // 2, LANES), jnp.bfloat16),
        compiler_params=params(),
        cost_estimate=cost(2 * rows * width * depth, 2 << 20),
        name="ctx_grad",
    )(grad_all, w_out)


def head_grad_body(
    info_ref, tok_ref, dkv_ref, dkv_sib_ref, dq_ref, dq_sib_ref, out_ref, acc_s, grad_s
):
    step = pl.program_id(0)
    steps = pl.num_programs(0)
    chips, half, _ = dq_ref.shape
    blocks = 2 * chips
    rows = 2 * half
    parity = info_ref[2 * blocks]
    chip = jnp.where(step < chips // 2, 2 * step, 2 * chips - 1 - 2 * step)

    @pl.when(step == 0)
    def _():
        acc_s[...] = jnp.zeros_like(acc_s)

    for core in range(2):
        block = 2 * chip + core
        total = dkv_ref[block].astype(jnp.float32) + dkv_sib_ref[block].astype(jnp.float32)
        own = (parity == core).astype(jnp.int32)
        dq = jnp.where(
            own == 1, dq_ref[chip].astype(jnp.float32), dq_sib_ref[chip].astype(jnp.float32)
        )
        dq_t = dq.T
        dq_t = jnp.concatenate([dq_t[:HD], dq_t[HD:]], axis=1)
        left = jnp.concatenate([total.T, dq_t], axis=0).astype(jnp.bfloat16)
        acc_s[...] += dot_nn(left, tok_ref[core * rows : (core + 1) * rows])

        @pl.when(own == 1)
        def _():
            out_ref[chip, 0:rows] = total.astype(jnp.bfloat16)
            out_ref[chip, rows : rows + half] = dq_ref[chip]

    @pl.when(step == steps - 1)
    def _():
        grad = acc_s[...]
        depth = grad.shape[1] // blocks
        wide = jnp.concatenate([grad[: 2 * HD], grad[2 * HD :], jnp.zeros_like(grad[:HD])], axis=0)
        turned = wide.T
        grad_s[...] = turned.reshape(blocks, depth, 2 * LANES)

        def pack(index, carry):
            part = grad_s[2 * index + parity]
            base = rows + half
            out_ref[index, base : base + depth] = part[:, :LANES].astype(jnp.bfloat16)
            query = part[:, LANES:]
            low = low_lanes(depth // 2)
            mixed = jnp.where(low, query[: depth // 2], pltpu.roll(query[depth // 2 :], HD, 1))
            out_ref[index, base + depth : base + depth + depth // 2] = mixed.astype(jnp.bfloat16)
            return carry

        lax.fori_loop(0, chips, pack, 0)


def head_grad(info, tokens_all, dkv, dkv_sib, dq, dq_sib):
    blocks, rows, _ = dkv.shape
    chips = blocks // 2
    depth = tokens_all.shape[1]
    piece = depth // blocks
    height = rows + rows // 2 + piece + piece // 2
    full = lambda shape: pl.BlockSpec(shape, lambda i: (0,) * len(shape))
    return pl.pallas_call(
        head_grad_body,
        grid=(chips,),
        in_specs=[
            pl.BlockSpec(memory_space=pltpu.SMEM),
            pl.BlockSpec((2 * rows, depth), lambda i: (i, 0)),
            full(dkv.shape),
            full(dkv.shape),
            full(dq.shape),
            full(dq.shape),
        ],
        out_specs=full((chips, height, LANES)),
        out_shape=jax.ShapeDtypeStruct((chips, height, LANES), jnp.bfloat16),
        scratch_shapes=[
            pltpu.VMEM((3 * HD, depth), jnp.float32),
            pltpu.VMEM((blocks, piece, 2 * LANES), jnp.float32),
        ],
        compiler_params=params("arbitrary"),
        cost_estimate=cost(2 * blocks * rows * depth * 3 * HD, blocks * rows * depth * 2),
        name="head_grad",
    )(info, tokens_all, dkv, dkv_sib, dq, dq_sib)


def token_grad_body(in_ref, wq_ref, wk_ref, wv_ref, own_ref, send_ref, gq_ref, gk_ref, gv_ref, d_s):
    heads = in_ref.shape[0]
    rows, width = d_s.shape[1:]
    half = rows // 2
    piece = gq_ref.shape[0]
    base = rows + half
    load = lambda head, lo, hi: in_ref[head, lo:hi].astype(jnp.float32)
    for pair in range(heads // 2):
        cols = slice(pair * LANES, (pair + 1) * LANES)
        a, b = 2 * pair, 2 * pair + 1
        key, value = split_lanes(load(a, 0, rows), load(b, 0, rows))
        d_s[1, :, cols] = key.astype(jnp.bfloat16)
        d_s[2, :, cols] = value.astype(jnp.bfloat16)
        top, bottom = split_lanes(load(a, rows, base), load(b, rows, base))
        d_s[0, :half, cols] = top.astype(jnp.bfloat16)
        d_s[0, half:, cols] = bottom.astype(jnp.bfloat16)
        key, value = split_lanes(load(a, base, base + piece), load(b, base, base + piece))
        gk_ref[:, cols] = key
        gv_ref[:, cols] = value
        last = base + piece + piece // 2
        top, bottom = split_lanes(load(a, base + piece, last), load(b, base + piece, last))
        gq_ref[: piece // 2, cols] = top
        gq_ref[piece // 2 :, cols] = bottom
    total = dot_nt(d_s[0], wq_ref[...]) + dot_nt(d_s[1], wk_ref[...]) + dot_nt(d_s[2], wv_ref[...])
    own_ref[...] = total[:half]
    send_ref[...] = total[half:].astype(jnp.bfloat16)


def token_grad(packed, rows, wq, wk, wv):
    depth, width = wq.shape
    piece = (packed.shape[1] - rows * 3 // 2) * 2 // 3
    grad = jax.ShapeDtypeStruct((piece, width), jnp.float32)
    return pl.pallas_call(
        token_grad_body,
        in_specs=[whole()] * 4,
        out_specs=[whole()] * 5,
        out_shape=[
            jax.ShapeDtypeStruct((rows // 2, depth), jnp.float32),
            jax.ShapeDtypeStruct((rows // 2, depth), jnp.bfloat16),
            grad,
            grad,
            grad,
        ],
        scratch_shapes=[pltpu.VMEM((3, rows, width), jnp.bfloat16)],
        compiler_params=params(),
        cost_estimate=cost(6 * rows * depth * width, 5 << 20),
        name="token_grad",
    )(packed, wq, wk, wv)


def ffn_grad_body(up_left, up_right, down_left, down_right, out_ref):
    width = up_right.shape[1]
    out_ref[:, :width] = contract_rows(up_left[...], up_right[...]).astype(jnp.bfloat16)
    out_ref[:, width:] = contract_rows(down_left[...], down_right[...]).astype(jnp.bfloat16)


def ffn_grad(chips, up_left, up_right, down_left, down_right):
    rows, depth = up_left.shape
    width = up_right.shape[1]
    tile = depth // chips
    column = lambda i: (0, jnp.where(i < chips // 2, 2 * i, 2 * chips - 1 - 2 * i))
    left = pl.BlockSpec((rows, tile), column)
    right = pl.BlockSpec((rows, width), lambda i: (0, 0))
    return pl.pallas_call(
        ffn_grad_body,
        grid=(chips,),
        in_specs=[left, right, left, right],
        out_specs=pl.BlockSpec((tile, 2 * width), lambda i: (i, 0)),
        out_shape=jax.ShapeDtypeStruct((depth, 2 * width), jnp.bfloat16),
        compiler_params=params("arbitrary"),
        cost_estimate=cost(4 * rows * depth * width, 12 << 20),
        name="ffn_grad",
    )(up_left, up_right, down_left, down_right)


def normalized(values):
    centred = values - jnp.mean(values, axis=-1, keepdims=True)
    inverse = lax.rsqrt(jnp.mean(centred * centred, axis=-1, keepdims=True) + 1e-05)
    return centred * inverse, inverse


def norm_back(grad, gain, unit, inverse):
    scaled = grad * gain
    along = jnp.mean(scaled * unit, axis=-1, keepdims=True)
    return (scaled - jnp.mean(scaled, axis=-1, keepdims=True) - unit * along) * inverse


def gelu_with_slope(values):
    cdf = 0.5 * (1.0 + lax.erf(values * 0.7071067811865476))
    density = jnp.exp(-0.5 * values * values) * 0.3989422804014327
    return values * cdf, cdf + values * density


def local_by_head(
    tokens,
    w_query,
    w_key,
    w_value,
    w_out,
    gain_attn,
    shift_attn,
    w_up,
    w_down,
    gain_ffn,
    shift_ffn,
    w_colbert,
    query_vecs,
    match_index,
    passage_of,
    cot_act,
    cot_scores,
):
    pass_count = lax.axis_size("pass")
    qry_count = lax.axis_size("qry")
    pass_index = lax.axis_index("pass")
    qry_index = lax.axis_index("qry")
    chips = pass_count // 2
    own_rows = tokens.shape[0]
    block_rows = own_rows * qry_count
    same_core = [[index for index in range(pass_count) if index % 2 == core] for core in (0, 1)]
    ring = [[2 * chip + core for chip in ring_chips(chips) for core in (0, 1)]]
    parity = pass_index % 2
    own_id = passage_of[pass_index]

    def swap(value):
        return swap_over(value, "qry", 1)

    def sibling(value):
        return swap_over(value, "pass", 1)

    def to_heads(value):
        return lax.all_to_all(
            value, "pass", 0, 0, axis_index_groups=same_core, tiled=True
        )

    gathered = jnp.concatenate([tokens, swap(tokens)], axis=0)
    tokens_all = lax.all_gather(gathered, "pass", axis=0, axis_index_groups=ring, tiled=True)

    seq_count = match_index.shape[1]
    query_rows = cot_scores.shape[0]
    pick_col = jnp.arange(seq_count, dtype=jnp.int32) == own_id
    span_count = jnp.sum((passage_of == own_id).astype(jnp.int32))
    first_index = jnp.sum((passage_of < own_id).astype(jnp.int32))
    raw_pick = jnp.sum(jnp.where(pick_col[None, :], match_index, 0), axis=1)
    local_row = raw_pick % (span_count * block_rows) - (pass_index - first_index) * block_rows
    inside = (local_row >= 0) & (local_row < block_rows)
    local_row = jnp.where(inside, (local_row + qry_index * own_rows) % block_rows, -1)
    one_hot = (local_row[:, None] == jnp.arange(block_rows, dtype=jnp.int32)[None, :]).astype(
        jnp.bfloat16
    )
    cot_pick = jnp.sum(jnp.where(pick_col[None, :], cot_scores, 0.0), axis=1)
    token_weight = jnp.repeat(cot_pick, query_vecs.shape[0] // query_rows)
    query_float = query_vecs.astype(jnp.float32)
    weighted_queries = (token_weight[:, None] * query_float).astype(jnp.bfloat16)
    unit_grad_part = contract_rows(one_hot, weighted_queries)
    turned_part = jnp.concatenate([unit_grad_part[own_rows:], unit_grad_part[:own_rows]], axis=0)
    unit_grad = unit_grad_part + swap(turned_part.astype(jnp.bfloat16)).astype(jnp.float32)

    block_ids = passage_of.astype(jnp.int32)
    same = block_ids[:, None] == block_ids[None, :]
    starts = jnp.sum((block_ids[None, :] < block_ids[:, None]).astype(jnp.int32), axis=1)
    counts = jnp.sum(same.astype(jnp.int32), axis=1)
    info = jnp.concatenate([starts, counts, parity[None].astype(jnp.int32)])

    own_pack = to_heads(project(gathered, w_query, w_key, w_value))
    sib_pack = sibling(own_pack)
    ctx_pack, ctx_turned, lse = attend(info, own_pack, sib_pack)
    context_low, attn_own, attn_send = out_project(to_heads(ctx_pack), w_out)
    attn_rows = attn_own + swap(attn_send).astype(jnp.float32)
    unit_attn, inverse_attn = normalized(tokens.astype(jnp.float32) + attn_rows)
    hidden = unit_attn * gain_attn + shift_attn
    hidden_low = hidden.astype(jnp.bfloat16)
    hidden_all = jnp.concatenate([hidden_low, swap(hidden_low)], axis=0)

    inner_pre = dot_nn(hidden_all, w_up)
    gated, slope = gelu_with_slope(inner_pre)
    gated_low = gated.astype(jnp.bfloat16)
    ffn_part = dot_nn(gated_low, w_down)
    ffn_rows = ffn_part[:own_rows] + swap(ffn_part[own_rows:].astype(jnp.bfloat16)).astype(
        jnp.float32
    )
    unit_ffn, inverse_ffn = normalized(hidden + ffn_rows)
    output = unit_ffn * gain_ffn + shift_ffn
    output_low = output.astype(jnp.bfloat16)
    output_other = swap(output_low)

    def colbert(rows, grad_rows):
        proj = dot_nn(rows, w_colbert)
        inverse = lax.rsqrt(jnp.sum(proj * proj, axis=1, keepdims=True) + 1e-06)
        unit = proj * inverse
        along = jnp.sum(unit * grad_rows, axis=1, keepdims=True)
        return unit.astype(jnp.bfloat16), ((grad_rows - unit * along) * inverse).astype(
            jnp.bfloat16
        )

    unit_own, proj_own = colbert(output_low, unit_grad[:own_rows])
    out_grad = cot_act.astype(jnp.float32) + dot_nt(proj_own, w_colbert)
    pre_grad = norm_back(out_grad, gain_ffn, unit_ffn, inverse_ffn)
    grad_gain_ffn = jnp.sum(out_grad * unit_ffn, axis=0)
    grad_shift_ffn = jnp.sum(out_grad, axis=0)
    pre_low = pre_grad.astype(jnp.bfloat16)
    ffn_all = jnp.concatenate([pre_low, swap(pre_low)], axis=0)

    unit_other, proj_other = colbert(output_other, unit_grad[own_rows:])
    output_all = jnp.concatenate([output_low, output_other], axis=0)
    proj_all = jnp.concatenate([proj_own, proj_other], axis=0)
    grad_colbert_part = contract_rows(output_all, proj_all).astype(jnp.bfloat16)
    colbert_piece = lax.psum_scatter(
        grad_colbert_part, "pass", scatter_dimension=0, axis_index_groups=ring, tiled=True
    )
    grad_colbert = lax.all_gather(
        colbert_piece, "pass", axis=0, axis_index_groups=ring, tiled=True
    ).astype(jnp.float32)
    picked = dot_nn(one_hot, jnp.concatenate([unit_own, unit_other], axis=0))
    per_query = jnp.sum((query_float * picked).reshape(query_rows, -1), axis=1)
    score_block = per_query[:, None] * pick_col.astype(jnp.float32)[None, :]
    score_part = lax.dynamic_update_slice(
        jnp.zeros((query_rows * qry_count, seq_count), jnp.float32),
        score_block,
        (qry_index * query_rows, jnp.zeros((), jnp.int32)),
    )

    inner_low = (dot_nt(ffn_all, w_down) * slope).astype(jnp.bfloat16)
    hidden_part = dot_nt(inner_low, w_up)
    hidden_grad = (
        pre_grad
        + hidden_part[:own_rows]
        + swap(hidden_part[own_rows:].astype(jnp.bfloat16)).astype(jnp.float32)
    )
    ffn_grads = ffn_grad(chips, hidden_all, inner_low, ffn_all, gated_low)
    ffn_sums = lax.psum_scatter(
        ffn_grads, "pass", scatter_dimension=0, axis_index_groups=ring, tiled=True
    )
    width = w_up.shape[1]
    grad_up = ffn_sums[:, :width].astype(jnp.float32)
    grad_down = ffn_sums[:, width:].astype(jnp.float32).T

    attn_pre = norm_back(hidden_grad, gain_attn, unit_attn, inverse_attn)
    grad_gain_attn = jnp.sum(hidden_grad * unit_attn, axis=0)
    grad_shift_attn = jnp.sum(hidden_grad, axis=0)
    attn_low = attn_pre.astype(jnp.bfloat16)
    attn_all = jnp.concatenate([attn_low, swap(attn_low)], axis=0)

    small = jnp.concatenate(
        [
            grad_gain_attn,
            grad_shift_attn,
            grad_gain_ffn,
            grad_shift_ffn,
            score_part.reshape(-1),
        ]
    ).reshape(-1, LANES)
    for mask in [1 << bit for bit in range(pass_count.bit_length() - 1)]:
        small = small + swap_over(small, "pass", mask)
    small = small + swap(small)
    model = tokens.shape[1]
    norms = small[: 4 * model // LANES].reshape(4, model)
    scores = small[4 * model // LANES :].reshape(score_part.shape)

    own_dctx = to_heads(ctx_grad_packed(attn_all, w_out))
    dkv, dq = attend_back(info, own_pack, sib_pack, own_dctx, ctx_turned, lse)
    back = head_grad(info, tokens_all, dkv, sibling(dkv), dq, sibling(dq))
    token_own, token_send, grad_query, grad_key, grad_value = token_grad(
        to_heads(back), block_rows, w_query, w_key, w_value
    )
    grad_tokens = attn_pre + token_own + swap(token_send).astype(jnp.float32)

    grad_out_part = contract_rows(attn_all, context_low).astype(jnp.bfloat16)
    tile = model // chips
    grad_out_part = jnp.concatenate(
        [grad_out_part[tile * chip : tile * (chip + 1)] for chip in ring_chips(chips)], axis=0
    )
    grad_out = (
        lax.psum_scatter(
            grad_out_part, "pass", scatter_dimension=0, axis_index_groups=ring, tiled=True
        )
        .astype(jnp.float32)
        .T
    )
    return (
        output_low,
        scores,
        grad_tokens,
        grad_query,
        grad_key,
        grad_value,
        grad_out,
        grad_up,
        grad_down,
        grad_colbert,
        norms[0],
        norms[1],
        norms[2],
        norms[3],
    )


def solution(mesh):
    by_head = mesh.shape["qry"] == 2
    return jax.shard_map(
        local_by_head if by_head else local_general,
        mesh=mesh,
        in_specs=(
            P(("pass", "qry"), None),
            P(None, "qry"),
            P(None, "qry"),
            P(None, "qry"),
            P("qry", None),
            P(),
            P(),
            P(None, "qry"),
            P("qry", None),
            P(),
            P(),
            P(),
            P("qry", None),
            P("qry", None),
            P(),
            P(("pass", "qry"), None),
            P("qry", None),
        ),
        out_specs=(
            P(("pass", "qry"), None),
            P(),
            P(("pass", "qry"), None),
            P("pass", "qry"),
            P("pass", "qry"),
            P("pass", "qry"),
            P("qry", "pass"),
            P("pass", "qry"),
            P("qry", "pass"),
            P(),
            P(),
            P(),
            P(),
            P(),
        ),
        check_vma=False,
    )
```

```python
import functools
import math

import jax
import jax.numpy as jnp
from jax import lax
from jax.experimental import pallas as pl
from jax.experimental.pallas import tpu as pltpu
from jax.sharding import PartitionSpec as P

HD = 64
SPAN = 8
LANES = 128
VMEM_LIMIT = 56 << 20
LOG2E = math.log2(math.e)


def passed_along(value, axis, steps):
    count = lax.axis_size(axis)
    first, last = (max(0, -steps), min(count, count - steps))
    return lax.ppermute(value, axis, [(source, source + steps) for source in range(first, last)])


def layer_norm(values, gain, shift):
    row_mean = jnp.mean(values, axis=-1, keepdims=True)
    centred = values - row_mean
    variance = jnp.mean(centred * centred, axis=-1, keepdims=True)
    return centred * lax.rsqrt(variance + 1e-05) * gain + shift


def gelu_exact(values):
    return 0.5 * values * (1.0 + jax.scipy.special.erf(values * 0.7071067811865476))


def normalize_rows(proj_rows):
    return proj_rows * lax.rsqrt(jnp.sum(proj_rows * proj_rows, axis=1, keepdims=True) + 1e-06)


def head_split(array):
    return array.reshape(array.shape[0], array.shape[1] // HD, HD)


def block_scores(queries, key_rows):
    return jnp.einsum("qhd,khd->hqk", queries, key_rows, preferred_element_type=jnp.float32) * 0.125


def grad_block(queries, ctx_grad, log_total, row_delta, key_rows, value_rows):
    scaled = block_scores(queries, key_rows)
    probs = jnp.exp(scaled - log_total[:, :, None])
    dprob = jnp.einsum("qhd,khd->hqk", ctx_grad, value_rows, preferred_element_type=jnp.float32)
    dscore = (0.125 * probs * (dprob - row_delta[:, :, None])).astype(jnp.bfloat16)
    dquery = jnp.einsum("hqk,khd->qhd", dscore, key_rows, preferred_element_type=jnp.float32)
    dkey = jnp.einsum("hqk,qhd->khd", dscore, queries, preferred_element_type=jnp.float32)
    dvalue = jnp.einsum(
        "hqk,qhd->khd", probs.astype(jnp.bfloat16), ctx_grad, preferred_element_type=jnp.float32
    )
    return (dquery, jnp.stack([dkey, dvalue]))


def contract_rows(left, right):
    return lax.dot_general(
        left, right, (((0,), (0,)), ((), ())), preferred_element_type=jnp.float32
    )


def contract_cols(left, right):
    return lax.dot_general(
        left, right, (((1,), (1,)), ((), ())), preferred_element_type=jnp.float32
    )


def local_general(
    tokens,
    w_query,
    w_key,
    w_value,
    w_out,
    gain_attn,
    shift_attn,
    w_up,
    w_down,
    gain_ffn,
    shift_ffn,
    w_colbert,
    query_vecs,
    match_index,
    passage_of,
    cot_act,
    cot_scores,
):
    pass_count = lax.axis_size("pass")
    qry_count = lax.axis_size("qry")
    pass_index = lax.axis_index("pass")
    qry_index = lax.axis_index("qry")
    own_id = passage_of[pass_index]

    def source_valid(offset):
        source = pass_index - offset
        inside = (source >= 0) & (source < pass_count)
        return inside & (passage_of[jnp.clip(source, 0, pass_count - 1)] == own_id)

    gathered = lax.all_gather(tokens, "qry", axis=0, tiled=True)
    block_rows = gathered.shape[0]
    local_width = w_query.shape[1]
    w_qkv = jnp.concatenate([w_query, w_key, w_value], axis=1)
    qkv_rows = jnp.dot(gathered, w_qkv, preferred_element_type=jnp.float32).astype(jnp.bfloat16)
    query_flat = qkv_rows[:, :local_width]
    key_flat = qkv_rows[:, local_width : 2 * local_width]
    value_flat = qkv_rows[:, 2 * local_width :]
    queries = head_split(query_flat)
    heads = queries.shape[1]
    own_pair = jnp.stack([key_flat, value_flat])
    offsets = [distance for distance in range(1, SPAN)] + [-distance for distance in range(1, SPAN)]

    def fetch_keys():
        received = []
        for offset in offsets:
            received.append(passed_along(own_pair, "pass", offset))
        return received

    remote = fetch_keys()

    def stat_of(kv_pair):
        return jax.nn.logsumexp(block_scores(queries, head_split(kv_pair[0])), axis=2)

    log_total = stat_of(own_pair)
    for offset, kv_pair in zip(offsets, remote):
        log_total = lax.cond(
            source_valid(offset),
            lambda current, kv_pair=kv_pair: jnp.logaddexp(current, stat_of(kv_pair)),
            lambda current: current,
            log_total,
        )

    def weighted(kv_pair):
        probs = jnp.exp(
            block_scores(queries, head_split(kv_pair[0])) - log_total[:, :, None]
        ).astype(jnp.bfloat16)
        return jnp.einsum(
            "hqk,khd->qhd", probs, head_split(kv_pair[1]), preferred_element_type=jnp.float32
        )

    context = weighted(own_pair)
    for offset, kv_pair in zip(offsets, remote):
        context = lax.cond(
            source_valid(offset),
            lambda running, kv_pair=kv_pair: running + weighted(kv_pair),
            lambda running: running,
            context,
        )
    context_low = context.reshape(block_rows, local_width).astype(jnp.bfloat16)
    piece_rows = context_low
    attn_rows = lax.psum_scatter(
        jnp.dot(piece_rows, w_out, preferred_element_type=jnp.float32).astype(jnp.bfloat16),
        "qry",
        scatter_dimension=0,
        tiled=True,
    ).astype(jnp.float32)
    hidden, norm_attn_back = jax.vjp(
        layer_norm, tokens.astype(jnp.float32) + attn_rows, gain_attn, shift_attn
    )
    hidden_all = lax.all_gather(hidden.astype(jnp.bfloat16), "qry", axis=0, tiled=True)
    inner_pre = jnp.dot(hidden_all, w_up, preferred_element_type=jnp.float32)
    gated_float, gelu_back = jax.vjp(gelu_exact, inner_pre)
    gated_low = gated_float.astype(jnp.bfloat16)
    piece_rows = gated_low
    ffn_rows = lax.psum_scatter(
        jnp.dot(piece_rows, w_down, preferred_element_type=jnp.float32).astype(jnp.bfloat16),
        "qry",
        scatter_dimension=0,
        tiled=True,
    ).astype(jnp.float32)
    output, norm_ffn_back = jax.vjp(layer_norm, hidden + ffn_rows, gain_ffn, shift_ffn)
    output_low = output.astype(jnp.bfloat16)
    proj_rows = jnp.dot(output_low, w_colbert, preferred_element_type=jnp.float32)
    unit_vecs, unit_back = jax.vjp(normalize_rows, proj_rows)
    unit_all = lax.all_gather(unit_vecs.astype(jnp.bfloat16), "qry", axis=0, tiled=True)
    seq_count = match_index.shape[1]
    query_rows = cot_scores.shape[0]
    numbers = jnp.arange(seq_count, dtype=jnp.int32)
    pick_col = numbers == own_id
    span_count = jnp.sum((passage_of == own_id).astype(jnp.int32))
    first_index = jnp.sum((passage_of < own_id).astype(jnp.int32))
    length = span_count * block_rows
    raw_pick = jnp.sum(jnp.where(pick_col[None, :], match_index, 0), axis=1)
    local_row = raw_pick % length - (pass_index - first_index) * block_rows
    one_hot = (local_row[:, None] == jnp.arange(block_rows, dtype=jnp.int32)[None, :]).astype(
        jnp.bfloat16
    )
    picked = jnp.dot(one_hot, unit_all, preferred_element_type=jnp.float32)
    query_float = query_vecs.astype(jnp.float32)
    match_vals = jnp.sum(query_float * picked, axis=1)
    per_query = jnp.sum(match_vals.reshape(query_rows, -1), axis=1)
    score_block = per_query[:, None] * pick_col.astype(jnp.float32)[None, :]
    score_part = lax.dynamic_update_slice(
        jnp.zeros((query_rows * qry_count, seq_count), jnp.float32),
        score_block,
        (qry_index * query_rows, jnp.zeros((), jnp.int32)),
    )
    cot_pick = jnp.sum(jnp.where(pick_col[None, :], cot_scores, 0.0), axis=1)
    token_weight = jnp.repeat(cot_pick, query_vecs.shape[0] // query_rows)
    weighted_queries = (token_weight[:, None] * query_float).astype(jnp.bfloat16)
    piece_rows = one_hot
    unit_grad = lax.psum_scatter(
        contract_rows(piece_rows, weighted_queries).astype(jnp.bfloat16),
        "qry",
        scatter_dimension=0,
        tiled=True,
    ).astype(jnp.float32)
    (proj_grad,) = unit_back(unit_grad)
    proj_low = proj_grad.astype(jnp.bfloat16)
    grad_colbert = contract_rows(output_low, proj_low)
    out_grad = cot_act.astype(jnp.float32) + contract_cols(proj_low, w_colbert)
    pre_grad, grad_gain_ffn, grad_shift_ffn = norm_ffn_back(out_grad)
    ffn_all = lax.all_gather(pre_grad.astype(jnp.bfloat16), "qry", axis=0, tiled=True)
    gated_grad = contract_cols(ffn_all, w_down)
    grad_down = contract_rows(gated_low, ffn_all)
    (inner_grad,) = gelu_back(gated_grad)
    inner_low = inner_grad.astype(jnp.bfloat16)
    grad_up = contract_rows(hidden_all, inner_low)
    piece_rows = inner_low
    hidden_grad = pre_grad + lax.psum_scatter(
        contract_cols(piece_rows, w_up).astype(jnp.bfloat16), "qry", scatter_dimension=0, tiled=True
    ).astype(jnp.float32)
    attn_pre_grad, grad_gain_attn, grad_shift_attn = norm_attn_back(hidden_grad)
    attn_all = lax.all_gather(attn_pre_grad.astype(jnp.bfloat16), "qry", axis=0, tiled=True)
    grad_out = contract_rows(context_low, attn_all)
    ctx_grad = head_split(contract_cols(attn_all, w_out).astype(jnp.bfloat16))
    row_delta = jnp.einsum("qhd,qhd->hq", ctx_grad.astype(jnp.float32), context)
    remote_back = fetch_keys()
    dquery, dkv_own = grad_block(
        queries, ctx_grad, log_total, row_delta, head_split(key_flat), head_split(value_flat)
    )
    key_value_grad = dkv_own
    zero_query = jnp.zeros_like(dquery)
    zero_pair = jnp.zeros((2, block_rows, heads, HD), jnp.float32)
    for offset, kv_pair in zip(offsets, remote_back):
        query_part, pair_part = lax.cond(
            source_valid(offset),
            lambda incoming: grad_block(
                queries,
                ctx_grad,
                log_total,
                row_delta,
                head_split(incoming[0]),
                head_split(incoming[1]),
            ),
            lambda incoming: (zero_query, zero_pair),
            kv_pair,
        )
        dquery = dquery + query_part
        returned = passed_along(
            pair_part.reshape(2, block_rows, local_width).astype(jnp.bfloat16), "pass", -offset
        ).astype(jnp.float32)
        key_value_grad = key_value_grad + returned.reshape(2, block_rows, heads, HD)
    dqkv_low = jnp.concatenate(
        [
            dquery.reshape(block_rows, local_width),
            key_value_grad[0].reshape(block_rows, local_width),
            key_value_grad[1].reshape(block_rows, local_width),
        ],
        axis=1,
    ).astype(jnp.bfloat16)
    grad_qkv = contract_rows(gathered, dqkv_low)
    piece_rows = dqkv_low
    grad_tokens = attn_pre_grad + lax.psum_scatter(
        contract_cols(piece_rows, w_qkv).astype(jnp.bfloat16),
        "qry",
        scatter_dimension=0,
        tiled=True,
    ).astype(jnp.float32)
    summed = (
        lax.psum_scatter(
            grad_qkv[:, :local_width].astype(jnp.bfloat16), "pass", scatter_dimension=0, tiled=True
        ).astype(jnp.float32),
        lax.psum_scatter(
            grad_qkv[:, local_width : 2 * local_width].astype(jnp.bfloat16),
            "pass",
            scatter_dimension=0,
            tiled=True,
        ).astype(jnp.float32),
        lax.psum_scatter(
            grad_qkv[:, 2 * local_width :].astype(jnp.bfloat16),
            "pass",
            scatter_dimension=0,
            tiled=True,
        ).astype(jnp.float32),
        lax.psum_scatter(
            grad_out.astype(jnp.bfloat16), "pass", scatter_dimension=1, tiled=True
        ).astype(jnp.float32),
        lax.psum_scatter(
            grad_up.astype(jnp.bfloat16), "pass", scatter_dimension=0, tiled=True
        ).astype(jnp.float32),
        lax.psum_scatter(
            grad_down.astype(jnp.bfloat16), "pass", scatter_dimension=1, tiled=True
        ).astype(jnp.float32),
    )
    shared = lax.psum(
        (grad_colbert, grad_gain_attn, grad_shift_attn, grad_gain_ffn, grad_shift_ffn, score_part),
        ("pass", "qry"),
    )
    return (
        output_low,
        shared[5],
        grad_tokens,
        summed[0],
        summed[1],
        summed[2],
        summed[3],
        summed[4],
        summed[5],
        shared[0],
        shared[1],
        shared[2],
        shared[3],
        shared[4],
    )


def swap_over(value, axis, mask):
    count = lax.axis_size(axis)
    return lax.ppermute(value, axis, [(index, index ^ mask) for index in range(count)])


def ring_chips(chips):
    layers = chips // 2
    return [2 * z for z in range(layers)] + [2 * z + 1 for z in reversed(range(layers))]


def low_lanes(rows):
    return lax.broadcasted_iota(jnp.int32, (rows, LANES), 1) < HD


def split_lanes(first, second):
    low = low_lanes(first.shape[0])
    return (
        jnp.where(low, first, pltpu.roll(second, HD, 1)),
        jnp.where(low, pltpu.roll(first, HD, 1), second),
    )


def dot_nn(left, right):
    return jnp.dot(left, right, preferred_element_type=jnp.float32)


def dot_nt(left, right):
    return contract_cols(left, right)


def params(*semantics):
    return pltpu.CompilerParams(
        dimension_semantics=semantics or None, vmem_limit_bytes=VMEM_LIMIT
    )


def cost(flops, moved, transcendentals=0):
    return pl.CostEstimate(
        flops=int(flops), bytes_accessed=int(moved), transcendentals=int(transcendentals)
    )


def project_body(x_ref, wq_ref, wk_ref, wv_ref, out_ref):
    x = x_ref[...]
    rows = x.shape[0]
    half = rows // 2
    query = dot_nn(x, wq_ref[...])
    key = dot_nn(x, wk_ref[...])
    value = dot_nn(x, wv_ref[...])
    for pair in range(query.shape[1] // LANES):
        cols = slice(pair * LANES, (pair + 1) * LANES)
        first, second = split_lanes(key[:, cols], value[:, cols])
        out_ref[2 * pair, 0:rows] = first.astype(jnp.bfloat16)
        out_ref[2 * pair + 1, 0:rows] = second.astype(jnp.bfloat16)
        first, second = split_lanes(query[:half, cols], query[half:, cols])
        out_ref[2 * pair, rows : rows + half] = first.astype(jnp.bfloat16)
        out_ref[2 * pair + 1, rows : rows + half] = second.astype(jnp.bfloat16)


def project(x, wq, wk, wv):
    rows, depth = x.shape
    width = wq.shape[1]
    heads = width // HD
    steps = 2
    weight = pl.BlockSpec((depth, width // steps), lambda i: (0, i))
    return pl.pallas_call(
        project_body,
        grid=(steps,),
        in_specs=[pl.BlockSpec((rows, depth), lambda i: (0, 0)), weight, weight, weight],
        out_specs=pl.BlockSpec((heads // steps, rows * 3 // 2, LANES), lambda i: (i, 0, 0)),
        out_shape=jax.ShapeDtypeStruct((heads, rows * 3 // 2, LANES), jnp.bfloat16),
        compiler_params=params("arbitrary"),
        cost_estimate=cost(2 * rows * depth * width * 3, 2 * (3 * depth * width + 4 * rows * depth)),
        name="project",
    )(x, wq, wk, wv)


def load_query(packed):
    wide = packed.astype(jnp.float32)
    low = low_lanes(wide.shape[0])
    top = jnp.where(low, wide, 0.0)
    bottom = jnp.where(low, pltpu.roll(wide, HD, 1), 0.0)
    return jnp.concatenate([top, bottom], axis=0).astype(jnp.bfloat16)


def pack_transposed(columns):
    half = columns.shape[1] // 2
    return jnp.concatenate([columns[:, :half], columns[:, half:]], axis=0).T


def square_sums(rows_low):
    group = lambda axis: lax.broadcasted_iota(jnp.int32, (LANES, LANES), axis) // HD
    ones = (group(0) == group(1)).astype(jnp.bfloat16)
    wide = rows_low.astype(jnp.float32)
    sums = dot_nn((wide * wide).astype(jnp.bfloat16), ones)
    return jnp.max(sums.reshape(sums.shape[0] // 8, 8, LANES), axis=0)


def over_blocks(first, count, step):
    def pair(index, carry):
        step(first + 2 * index, 2)
        return carry

    lax.fori_loop(0, count // 2, pair, 0)

    @pl.when(count % 2 == 1)
    def _():
        step(first + count - 1, 1)


def attend_body(
    info_ref, own_ref, sib_ref, ctx_ref, ctxt_ref, lse_ref, kt_ref, kv_s, vt_s, score_s, total_s
):
    chips = own_ref.shape[0]
    blocks = 2 * chips
    rows = kv_s.shape[1]
    parity = info_ref[2 * blocks]
    scale = 0.125 * LOG2E
    ones_rows = lax.broadcasted_iota(jnp.int32, (LANES, rows), 0) < HD

    def gather(chip, carry):
        key_top, query_top = carry
        for ref, which in ((own_ref, parity), (sib_ref, 1 - parity)):
            block = ref[chip, 0:rows]
            kv_s[2 * chip + which] = block
            turned = block.astype(jnp.float32).T
            vt_s[2 * chip + which] = jnp.where(ones_rows, 1.0, turned).astype(jnp.bfloat16)
            kt_ref[2 * chip + which] = turned[:HD].astype(jnp.bfloat16)
            key_top = jnp.maximum(key_top, square_sums(block))
        query_top = jnp.maximum(query_top, square_sums(own_ref[chip, rows : rows + rows // 2]))
        return key_top, query_top

    zero = jnp.zeros((8, LANES), jnp.float32)
    key_top, query_top = lax.fori_loop(0, chips, gather, (zero, zero))
    key_top = jnp.max(jnp.where(low_lanes(8), key_top, 0.0))
    bound = jnp.max(query_top) * key_top * (1.02 * scale * scale)

    def finish(item, total, shift):
        weight = total[0:1]
        context = total[HD:] / weight
        ctxt_ref[item] = context
        lse_ref[item] = jnp.broadcast_to(shift + jnp.log2(weight), (8, rows))
        ctx_ref[item] = pack_transposed(context).astype(jnp.bfloat16)

    def items(one_item):
        def body(item, carry):
            block = 2 * item + parity
            query = load_query(own_ref[item, rows : rows + rows // 2])
            one_item(item, info_ref[block], info_ref[blocks + block], query)
            return carry

        lax.fori_loop(0, chips, body, 0)

    @pl.when(bound < 3600.0)
    def _():
        def one_item(item, first, count, query):
            total_s[...] = jnp.zeros_like(total_s)

            def step(block, n):
                keys = kv_s[pl.ds(block, n)].reshape(n * rows, LANES)
                prob = jnp.exp2(dot_nt(keys, query) * scale).astype(jnp.bfloat16)
                total = total_s[...]
                for index in range(n):
                    part = prob[index * rows : (index + 1) * rows]
                    total = total + dot_nn(vt_s[block + index], part)
                total_s[...] = total

            over_blocks(first, count, step)
            finish(item, total_s[...], 0.0)

        items(one_item)

    @pl.when(jnp.logical_not(bound < 3600.0))
    def _():
        def one_item(item, first, count, query):
            def scores(step, top):
                score = dot_nt(kv_s[first + step], query) * scale
                score_s[step] = score
                return jnp.maximum(top, jnp.max(score.reshape(rows // 8, 8, rows), axis=0))

            top = lax.fori_loop(0, count, scores, jnp.full((8, rows), -jnp.inf, jnp.float32))
            top = jnp.max(top, axis=0, keepdims=True)

            def weigh(step, total):
                prob = jnp.exp2(score_s[step] - top).astype(jnp.bfloat16)
                return total + dot_nn(vt_s[first + step], prob)

            total = lax.fori_loop(0, count, weigh, jnp.zeros((LANES, rows), jnp.float32))
            finish(item, total, top)

        items(one_item)


def whole():
    return pl.BlockSpec(memory_space=pltpu.VMEM)


def attend(info, own, sib):
    chips, packed, _ = own.shape
    rows = packed * 2 // 3
    blocks = 2 * chips
    return pl.pallas_call(
        attend_body,
        in_specs=[pl.BlockSpec(memory_space=pltpu.SMEM), whole(), whole()],
        out_specs=[whole()] * 4,
        out_shape=[
            jax.ShapeDtypeStruct((chips, rows // 2, LANES), jnp.bfloat16),
            jax.ShapeDtypeStruct((chips, HD, rows), jnp.float32),
            jax.ShapeDtypeStruct((chips, 8, rows), jnp.float32),
            jax.ShapeDtypeStruct((blocks, HD, rows), jnp.bfloat16),
        ],
        scratch_shapes=[
            pltpu.VMEM((blocks, rows, LANES), jnp.bfloat16),
            pltpu.VMEM((blocks, LANES, rows), jnp.bfloat16),
            pltpu.VMEM((SPAN, rows, rows), jnp.float32),
            pltpu.VMEM((LANES, rows), jnp.float32),
        ],
        compiler_params=params(),
        cost_estimate=cost(2 * 2 * 40 * rows * rows * LANES, 4 << 20, 40 * rows * rows),
        name="attend",
    )(info, own, sib)


def attend_back_body(
    info_ref,
    own_ref,
    sib_ref,
    dctx_ref,
    ctxt_ref,
    lse_ref,
    kt_ref,
    dkv_ref,
    dq_ref,
    kv_s,
    acc_s,
    total_s,
):
    chips = own_ref.shape[0]
    blocks = 2 * chips
    rows = kv_s.shape[1]
    half = rows // 2
    parity = info_ref[2 * blocks]
    scale = 0.125 * LOG2E

    def gather(chip, carry):
        for ref, which in ((own_ref, parity), (sib_ref, 1 - parity)):
            kv_s[2 * chip + which] = ref[chip, 0:rows]
            acc_s[2 * chip + which] = jnp.zeros((rows, LANES), jnp.float32)
        return carry

    lax.fori_loop(0, chips, gather, 0)
    low = low_lanes(half)

    def one_block(item, carry):
        block = 2 * item + parity
        query = load_query(own_ref[item, rows : rows + half])
        packed = dctx_ref[item].astype(jnp.float32)
        top = jnp.where(low, 0.0, pltpu.roll(packed, HD, 1))
        bottom = jnp.where(low, 0.0, packed)
        dctx = jnp.concatenate([top, bottom], axis=0).astype(jnp.bfloat16)
        turned = packed.T
        dctx_t = jnp.concatenate([turned[:HD], turned[HD:]], axis=1)
        delta = jnp.sum(dctx_t * ctxt_ref[item], axis=0, keepdims=True)
        lse = lse_ref[item, 0:1]
        both = jnp.concatenate([query, dctx], axis=0)
        total_s[...] = jnp.zeros_like(total_s)

        def step(index, n):
            kv = kv_s[pl.ds(index, n)].reshape(n * rows, LANES)
            prob = jnp.exp2(dot_nt(kv, query) * scale - lse)
            dscore = (prob * (dot_nt(kv, dctx) - delta)).astype(jnp.bfloat16)
            pair = jnp.concatenate([dscore, prob.astype(jnp.bfloat16)], axis=1)
            acc_s[pl.ds(index, n)] += dot_nn(pair, both).reshape(n, rows, LANES)
            total = total_s[...]
            for part in range(n):
                total = total + dot_nn(kt_ref[index + part], dscore[part * rows : (part + 1) * rows])
            total_s[...] = total

        over_blocks(info_ref[block], info_ref[blocks + block], step)
        dq_ref[item] = pack_transposed(total_s[...] * 0.125).astype(jnp.bfloat16)
        return carry

    lax.fori_loop(0, chips, one_block, 0)
    key_scale = jnp.where(low_lanes(rows), 0.125, 1.0)

    def finish(index, carry):
        dkv_ref[index] = (acc_s[index] * key_scale).astype(jnp.bfloat16)
        return carry

    lax.fori_loop(0, blocks, finish, 0)


def attend_back(info, own, sib, dctx, ctxt, lse, kt):
    chips, packed, _ = own.shape
    rows = packed * 2 // 3
    blocks = 2 * chips
    return pl.pallas_call(
        attend_back_body,
        in_specs=[pl.BlockSpec(memory_space=pltpu.SMEM)] + [whole()] * 6,
        out_specs=[whole(), whole()],
        out_shape=[
            jax.ShapeDtypeStruct((blocks, rows, LANES), jnp.bfloat16),
            jax.ShapeDtypeStruct((chips, rows // 2, LANES), jnp.bfloat16),
        ],
        scratch_shapes=[
            pltpu.VMEM((blocks, rows, LANES), jnp.bfloat16),
            pltpu.VMEM((blocks, rows, LANES), jnp.float32),
            pltpu.VMEM((HD, rows), jnp.float32),
        ],
        compiler_params=params(),
        cost_estimate=cost(2 * 5 * 40 * rows * rows * LANES, 5 << 20, 40 * rows * rows),
        name="attend_back",
    )(info, own, sib, dctx, ctxt, lse, kt)


def combine_body(info_ref, dkv_ref, sib_ref, dq_ref, out_ref):
    chips, half, _ = dq_ref.shape
    rows = 2 * half
    parity = info_ref[4 * chips]

    def one(chip, carry):
        block = 2 * chip + parity
        total = dkv_ref[block].astype(jnp.float32) + sib_ref[block].astype(jnp.float32)
        out_ref[chip, 0:rows] = total.astype(jnp.bfloat16)
        out_ref[chip, rows : rows + half] = dq_ref[chip]
        return carry

    lax.fori_loop(0, chips, one, 0)


def combine(info, dkv, dkv_sib, dq):
    chips, half, _ = dq.shape
    return pl.pallas_call(
        combine_body,
        in_specs=[pl.BlockSpec(memory_space=pltpu.SMEM)] + [whole()] * 3,
        out_specs=whole(),
        out_shape=jax.ShapeDtypeStruct((chips, 3 * half, LANES), jnp.bfloat16),
        compiler_params=params(),
        cost_estimate=cost(1 << 20, 3 << 20),
        name="combine",
    )(info, dkv, dkv_sib, dq)


def out_project_body(in_ref, w_ref, ctx_ref, own_ref, send_ref):
    heads, half, _ = in_ref.shape
    for pair in range(heads // 2):
        cols = slice(pair * LANES, (pair + 1) * LANES)
        top, bottom = split_lanes(
            in_ref[2 * pair].astype(jnp.float32), in_ref[2 * pair + 1].astype(jnp.float32)
        )
        ctx_ref[0:half, cols] = top.astype(jnp.bfloat16)
        ctx_ref[half:, cols] = bottom.astype(jnp.bfloat16)
    rows = dot_nn(ctx_ref[...], w_ref[...])
    own_ref[...] = rows[:half]
    send_ref[...] = rows[half:].astype(jnp.bfloat16)


def out_project(packed, w_out):
    heads, half, _ = packed.shape
    width, depth = w_out.shape
    return pl.pallas_call(
        out_project_body,
        in_specs=[whole()] * 2,
        out_specs=[whole()] * 3,
        out_shape=[
            jax.ShapeDtypeStruct((2 * half, width), jnp.bfloat16),
            jax.ShapeDtypeStruct((half, depth), jnp.float32),
            jax.ShapeDtypeStruct((half, depth), jnp.bfloat16),
        ],
        compiler_params=params(),
        cost_estimate=cost(4 * half * width * depth, 3 << 20),
        name="out_project",
    )(packed, w_out)


def ctx_grad_body(own_ref, other_ref, w_ref, out_ref):
    half = out_ref.shape[1]
    grad = dot_nt(jnp.concatenate([own_ref[...], other_ref[...]], axis=0), w_ref[...])
    for pair in range(grad.shape[1] // LANES):
        cols = slice(pair * LANES, (pair + 1) * LANES)
        first, second = split_lanes(grad[:half, cols], grad[half:, cols])
        out_ref[2 * pair] = first.astype(jnp.bfloat16)
        out_ref[2 * pair + 1] = second.astype(jnp.bfloat16)


def ctx_grad_packed(grad_own, grad_other, w_out):
    rows, depth = 2 * grad_own.shape[0], grad_own.shape[1]
    width = w_out.shape[0]
    return pl.pallas_call(
        ctx_grad_body,
        in_specs=[whole()] * 3,
        out_specs=whole(),
        out_shape=jax.ShapeDtypeStruct((width // HD, rows // 2, LANES), jnp.bfloat16),
        compiler_params=params(),
        cost_estimate=cost(2 * rows * width * depth, 2 << 20),
        name="ctx_grad",
    )(grad_own, grad_other, w_out)


def head_grad_body(
    info_ref, tok_ref, dkv_ref, dkv_sib_ref, dq_ref, dq_sib_ref, out_ref, acc_s, grad_s
):
    step = pl.program_id(0)
    steps = pl.num_programs(0)
    chips, half, _ = dq_ref.shape
    blocks = 2 * chips
    rows = 2 * half
    parity = info_ref[2 * blocks]
    group = chips // steps
    columns = []
    for index in range(group):
        place = step * group + index
        chip = jnp.where(place < chips // 2, 2 * place, 2 * chips - 1 - 2 * place)
        for core in range(2):
            block = 2 * chip + core
            total = dkv_ref[block].astype(jnp.float32) + dkv_sib_ref[block].astype(jnp.float32)
            dq = jnp.where(
                parity == core,
                dq_ref[chip].astype(jnp.float32),
                dq_sib_ref[chip].astype(jnp.float32),
            ).T
            dq = jnp.concatenate([dq[:HD], dq[HD:]], axis=1)
            columns.append(jnp.concatenate([total.T, dq], axis=0).astype(jnp.bfloat16))
    part = dot_nn(jnp.concatenate(columns, axis=1), tok_ref[...])

    @pl.when(step == 0)
    def _():
        acc_s[...] = part

    @pl.when(step > 0)
    def _():
        acc_s[...] += part

    @pl.when(step == steps - 1)
    def _():
        grad = acc_s[...]
        depth = grad.shape[1] // blocks
        wide = jnp.concatenate([grad, grad[2 * HD :]], axis=0)
        grad_s[...] = wide.T.reshape(blocks, depth, 2 * LANES)

        def pack(index, carry):
            part = grad_s[2 * index + parity]
            out_ref[index, 0:depth] = part[:, :LANES].astype(jnp.bfloat16)
            query = part[:, LANES:]
            mixed = jnp.where(low_lanes(depth // 2), query[: depth // 2], query[depth // 2 :])
            out_ref[index, depth : depth + depth // 2] = mixed.astype(jnp.bfloat16)
            return carry

        lax.fori_loop(0, chips, pack, 0)


def head_grad(info, tokens_all, dkv, dkv_sib, dq, dq_sib):
    blocks, rows, _ = dkv.shape
    chips = blocks // 2
    depth = tokens_all.shape[1]
    piece = depth // blocks
    steps = 4
    full = lambda shape: pl.BlockSpec(shape, lambda i: (0,) * len(shape))
    return pl.pallas_call(
        head_grad_body,
        grid=(steps,),
        in_specs=[
            pl.BlockSpec(memory_space=pltpu.SMEM),
            pl.BlockSpec((blocks * rows // steps, depth), lambda i: (i, 0)),
            full(dkv.shape),
            full(dkv.shape),
            full(dq.shape),
            full(dq.shape),
        ],
        out_specs=full((chips, piece + piece // 2, LANES)),
        out_shape=jax.ShapeDtypeStruct((chips, piece + piece // 2, LANES), jnp.bfloat16),
        scratch_shapes=[
            pltpu.VMEM((3 * HD, depth), jnp.float32),
            pltpu.VMEM((blocks, piece, 2 * LANES), jnp.float32),
        ],
        compiler_params=params("arbitrary"),
        cost_estimate=cost(2 * blocks * rows * depth * 3 * HD, blocks * rows * depth * 2),
        name="head_grad",
    )(info, tokens_all, dkv, dkv_sib, dq, dq_sib)


def token_grad_body(in_ref, wq_ref, wk_ref, wv_ref, own_ref, send_ref, d_s):
    heads = in_ref.shape[0]
    rows = d_s.shape[1]
    half = rows // 2
    load = lambda head, lo, hi: in_ref[head, lo:hi].astype(jnp.float32)
    for pair in range(heads // 2):
        cols = slice(pair * LANES, (pair + 1) * LANES)
        a, b = 2 * pair, 2 * pair + 1
        key, value = split_lanes(load(a, 0, rows), load(b, 0, rows))
        d_s[1, :, cols] = key.astype(jnp.bfloat16)
        d_s[2, :, cols] = value.astype(jnp.bfloat16)
        top, bottom = split_lanes(load(a, rows, rows + half), load(b, rows, rows + half))
        d_s[0, :half, cols] = top.astype(jnp.bfloat16)
        d_s[0, half:, cols] = bottom.astype(jnp.bfloat16)
    total = dot_nt(d_s[0], wq_ref[...]) + dot_nt(d_s[1], wk_ref[...]) + dot_nt(d_s[2], wv_ref[...])
    own_ref[...] = total[:half]
    send_ref[...] = total[half:].astype(jnp.bfloat16)


def token_grad(packed, wq, wk, wv):
    depth, width = wq.shape
    rows = packed.shape[1] * 2 // 3
    return pl.pallas_call(
        token_grad_body,
        in_specs=[whole()] * 4,
        out_specs=[whole()] * 2,
        out_shape=[
            jax.ShapeDtypeStruct((rows // 2, depth), jnp.float32),
            jax.ShapeDtypeStruct((rows // 2, depth), jnp.bfloat16),
        ],
        scratch_shapes=[pltpu.VMEM((3, rows, width), jnp.bfloat16)],
        compiler_params=params(),
        cost_estimate=cost(6 * rows * depth * width, 5 << 20),
        name="token_grad",
    )(packed, wq, wk, wv)


def split_heads_body(in_ref, gq_ref, gk_ref, gv_ref):
    heads = in_ref.shape[0]
    piece = gq_ref.shape[0]
    last = piece + piece // 2
    load = lambda head, lo, hi: in_ref[head, lo:hi].astype(jnp.float32)
    for pair in range(heads // 2):
        cols = slice(pair * LANES, (pair + 1) * LANES)
        a, b = 2 * pair, 2 * pair + 1
        key, value = split_lanes(load(a, 0, piece), load(b, 0, piece))
        gk_ref[:, cols] = key
        gv_ref[:, cols] = value
        top, bottom = split_lanes(load(a, piece, last), load(b, piece, last))
        gq_ref[: piece // 2, cols] = top
        gq_ref[piece // 2 :, cols] = bottom


def split_heads(packed):
    heads, height, _ = packed.shape
    grad = jax.ShapeDtypeStruct((height * 2 // 3, heads * HD), jnp.float32)
    return pl.pallas_call(
        split_heads_body,
        in_specs=[whole()],
        out_specs=[whole()] * 3,
        out_shape=[grad] * 3,
        compiler_params=params(),
        cost_estimate=cost(1 << 18, 1 << 20),
        name="split_heads",
    )(packed)


def late_grad_body(orders, tiles, parts, *refs):
    *arrays, out_ref, turned_s = refs
    step = pl.program_id(0)
    width = out_ref.shape[1]
    terms = []
    for count in parts:
        terms.append((arrays[:count], arrays[count : 2 * count]))
        arrays = arrays[2 * count :]

    @pl.when(step == 0)
    def _():
        for index, (lefts, _) in enumerate(terms):
            size = lefts[0].shape[1] // len(orders[index])
            for which, left in enumerate(lefts):
                half = left.shape[0]
                for place, chip in enumerate(orders[index]):
                    piece = left[:, chip * size : (chip + 1) * size].T
                    rows = slice(place * size, (place + 1) * size)
                    turned_s[index, rows, which * half : (which + 1) * half] = piece

    start = 0
    for index, (_, rights) in enumerate(terms):

        @pl.when((step >= start) & (step < start + tiles[index]))
        def _(index=index, start=start, rights=rights):
            cols = pl.ds(pl.multiple_of((step - start) * width, width), width)
            right = jnp.concatenate([ref[:, cols] for ref in rights], axis=0)
            left = turned_s[index, :, : right.shape[0]]
            out_ref[...] = dot_nn(left, right).astype(jnp.bfloat16)

        start += tiles[index]


def late_grad(chips, terms):
    half, depth = terms[0][0][0].shape
    tile = 512
    orders = [ring_chips(chips) if term[2] else list(range(chips)) for term in terms]
    arrays = [array for term in terms for group in term[:2] for array in group]
    tiles = [term[1][0].shape[1] // tile for term in terms]
    parts = [len(term[0]) for term in terms]
    width = sum(tiles) * tile
    fixed = lambda array: pl.BlockSpec(array.shape, lambda i: (0, 0))
    return pl.pallas_call(
        functools.partial(late_grad_body, orders, tiles, parts),
        grid=(sum(tiles),),
        in_specs=[fixed(array) for array in arrays],
        out_specs=pl.BlockSpec((depth, tile), lambda i: (0, i)),
        out_shape=jax.ShapeDtypeStruct((depth, width), jnp.bfloat16),
        scratch_shapes=[pltpu.VMEM((len(terms), depth, 2 * half), jnp.bfloat16)],
        compiler_params=params("arbitrary"),
        cost_estimate=cost(4 * half * depth * width, 2 * depth * width + (3 << 20)),
        name="late_grad",
    )(*arrays)


def out_grad_body(left_ref, other_ref, ctx_ref, small_ref, out_ref):
    cores, chips, height, _ = out_ref.shape
    piece = height - small_ref.shape[0]
    left = jnp.concatenate([left_ref[...], other_ref[...]], axis=0)
    grad = contract_rows(left, ctx_ref[...]).astype(jnp.bfloat16)
    for index in range(cores * chips):
        place = (index % cores, index // cores)
        out_ref[place[0], place[1], :piece] = grad[index * piece : (index + 1) * piece]
        out_ref[place[0], place[1], piece:] = small_ref[...]


def out_grad_pack(count, grad_own, grad_other, context_low, small):
    depth = grad_own.shape[1]
    rows, width = context_low.shape
    height = depth // count + small.shape[0]
    return pl.pallas_call(
        out_grad_body,
        in_specs=[whole()] * 4,
        out_specs=whole(),
        out_shape=jax.ShapeDtypeStruct((2, count // 2, height, width), jnp.bfloat16),
        compiler_params=params(),
        cost_estimate=cost(2 * rows * depth * width, 2 << 20),
        name="out_grad",
    )(grad_own, grad_other, context_low, small)


def normalized(values):
    centred = values - jnp.mean(values, axis=-1, keepdims=True)
    inverse = lax.rsqrt(jnp.mean(centred * centred, axis=-1, keepdims=True) + 1e-05)
    return centred * inverse, inverse


def norm_back(grad, gain, unit, inverse):
    scaled = grad * gain
    along = jnp.mean(scaled * unit, axis=-1, keepdims=True)
    return (scaled - jnp.mean(scaled, axis=-1, keepdims=True) - unit * along) * inverse


def gelu_with_slope(values):
    cdf = 0.5 * (1.0 + lax.erf(values * 0.7071067811865476))
    density = jnp.exp(-0.5 * values * values) * 0.3989422804014327
    return values * cdf, cdf + values * density


def local_by_head(
    tokens,
    w_query,
    w_key,
    w_value,
    w_out,
    gain_attn,
    shift_attn,
    w_up,
    w_down,
    gain_ffn,
    shift_ffn,
    w_colbert,
    query_vecs,
    match_index,
    passage_of,
    cot_act,
    cot_scores,
):
    pass_count = lax.axis_size("pass")
    qry_count = lax.axis_size("qry")
    pass_index = lax.axis_index("pass")
    qry_index = lax.axis_index("qry")
    chips = pass_count // 2
    own_rows = tokens.shape[0]
    block_rows = own_rows * qry_count
    same_core = [[index for index in range(pass_count) if index % 2 == core] for core in (0, 1)]
    ring = [[2 * chip + core for chip in ring_chips(chips) for core in (0, 1)]]
    parity = pass_index % 2
    own_id = passage_of[pass_index]

    def swap(value):
        return swap_over(value, "qry", 1)

    def sibling(value):
        return swap_over(value, "pass", 1)

    def to_heads(value):
        return lax.all_to_all(
            value, "pass", 0, 0, axis_index_groups=same_core, tiled=True
        )

    def after(value, *others):
        return lax.optimization_barrier((value,) + others)[0]

    def together(*values):
        return lax.optimization_barrier(values)

    gathered = jnp.concatenate([tokens, swap(tokens)], axis=0)
    block_ids = passage_of.astype(jnp.int32)
    same = block_ids[:, None] == block_ids[None, :]
    starts = jnp.sum((block_ids[None, :] < block_ids[:, None]).astype(jnp.int32), axis=1)
    counts = jnp.sum(same.astype(jnp.int32), axis=1)
    info = jnp.concatenate([starts, counts, parity[None].astype(jnp.int32)])

    seq_count = match_index.shape[1]
    query_rows = cot_scores.shape[0]
    pick_col = jnp.arange(seq_count, dtype=jnp.int32) == own_id
    span_count = jnp.sum((passage_of == own_id).astype(jnp.int32))
    first_index = jnp.sum((passage_of < own_id).astype(jnp.int32))
    raw_pick = jnp.sum(jnp.where(pick_col[None, :], match_index, 0), axis=1)
    local_row = raw_pick % (span_count * block_rows) - (pass_index - first_index) * block_rows
    inside = (local_row >= 0) & (local_row < block_rows)
    local_row = jnp.where(inside, (local_row + qry_index * own_rows) % block_rows, -1)
    one_hot = (local_row[:, None] == jnp.arange(block_rows, dtype=jnp.int32)[None, :]).astype(
        jnp.bfloat16
    )
    cot_pick = jnp.sum(jnp.where(pick_col[None, :], cot_scores, 0.0), axis=1)
    token_weight = jnp.repeat(cot_pick, query_vecs.shape[0] // query_rows)
    query_float = query_vecs.astype(jnp.float32)
    weighted_queries = (token_weight[:, None] * query_float).astype(jnp.bfloat16)
    unit_grad_part = contract_rows(one_hot, weighted_queries)
    turned_part = jnp.concatenate([unit_grad_part[own_rows:], unit_grad_part[:own_rows]], axis=0)
    unit_grad_send = turned_part.astype(jnp.bfloat16)

    own_pack = to_heads(project(gathered, w_query, w_key, w_value))
    own_pack, unit_grad_send = together(own_pack, unit_grad_send)
    sib_pack = sibling(own_pack)
    unit_grad_recv = swap(unit_grad_send)
    ctx_pack, ctx_turned, lse, key_turned = attend(info, own_pack, sib_pack)
    unit_grad = unit_grad_part + unit_grad_recv.astype(jnp.float32)
    ctx_recv = to_heads(after(ctx_pack, unit_grad_recv))
    tokens_all = lax.all_gather(
        after(gathered, ctx_recv), "pass", axis=0, axis_index_groups=ring, tiled=True
    )
    context_low, attn_own, attn_send = out_project(ctx_recv, w_out)
    attn_rows = attn_own + swap(attn_send).astype(jnp.float32)
    unit_attn, inverse_attn = normalized(tokens.astype(jnp.float32) + attn_rows)
    hidden = unit_attn * gain_attn + shift_attn
    hidden_low = hidden.astype(jnp.bfloat16)
    hidden_other = swap(hidden_low)
    hidden_all = jnp.concatenate([hidden_low, hidden_other], axis=0)

    inner_pre = dot_nn(hidden_all, w_up)
    gated, slope = gelu_with_slope(inner_pre)
    gated_low, slope = lax.optimization_barrier((gated.astype(jnp.bfloat16), slope))
    ffn_part = dot_nn(gated_low, w_down)
    ffn_rows = ffn_part[:own_rows] + swap(ffn_part[own_rows:].astype(jnp.bfloat16)).astype(
        jnp.float32
    )
    unit_ffn, inverse_ffn = normalized(hidden + ffn_rows)
    output = unit_ffn * gain_ffn + shift_ffn
    output_low = output.astype(jnp.bfloat16)

    def colbert(rows, grad_rows):
        proj = dot_nn(rows, w_colbert)
        inverse = lax.rsqrt(jnp.sum(proj * proj, axis=1, keepdims=True) + 1e-06)
        unit = proj * inverse
        along = jnp.sum(unit * grad_rows, axis=1, keepdims=True)
        return unit.astype(jnp.bfloat16), ((grad_rows - unit * along) * inverse).astype(
            jnp.bfloat16
        )

    unit_own, proj_own = colbert(output_low, unit_grad[:own_rows])
    out_grad = cot_act.astype(jnp.float32) + dot_nt(proj_own, w_colbert)
    pre_grad = norm_back(out_grad, gain_ffn, unit_ffn, inverse_ffn)
    pre_low = pre_grad.astype(jnp.bfloat16)
    pre_other = swap(pre_low)
    ffn_all = jnp.concatenate([pre_low, pre_other], axis=0)

    inner_low = (dot_nt(ffn_all, w_down) * slope).astype(jnp.bfloat16)
    hidden_part = dot_nt(inner_low, w_up)
    hidden_send = hidden_part[own_rows:].astype(jnp.bfloat16)
    hidden_recv = swap(hidden_send)
    inner_late = after(inner_low, hidden_send)
    width = w_up.shape[1]
    late = late_grad(
        chips,
        (
            ((hidden_low, hidden_other), (inner_late[:own_rows], inner_late[own_rows:]), True),
            ((pre_low, pre_other), (gated_low[:own_rows], gated_low[own_rows:]), True),
            ((output_low,), (proj_own,), False),
        ),
    )
    hidden_recv, late, tokens_all = together(hidden_recv, late, tokens_all)
    late_sums = lax.psum_scatter(
        late, "pass", scatter_dimension=0, axis_index_groups=ring, tiled=True
    )

    hidden_grad = (
        pre_grad + hidden_part[:own_rows] + hidden_recv.astype(jnp.float32)
    )
    attn_pre = norm_back(hidden_grad, gain_attn, unit_attn, inverse_attn)
    attn_low = attn_pre.astype(jnp.bfloat16)
    attn_other = swap(attn_low)

    unit_other = swap(after(unit_own, attn_other))
    picked = dot_nn(one_hot, jnp.concatenate([unit_own, unit_other], axis=0))
    per_query = jnp.sum((query_float * picked).reshape(query_rows, -1), axis=1)
    score_block = per_query[:, None] * pick_col.astype(jnp.float32)[None, :]
    score_part = lax.dynamic_update_slice(
        jnp.zeros((query_rows * qry_count, seq_count), jnp.float32),
        score_block,
        (qry_index * query_rows, jnp.zeros((), jnp.int32)),
    )
    model = tokens.shape[1]
    local_width = w_query.shape[1]
    small = jnp.concatenate(
        [
            jnp.sum(hidden_grad * unit_attn, axis=0),
            jnp.sum(hidden_grad, axis=0),
            jnp.sum(out_grad * unit_ffn, axis=0),
            jnp.sum(out_grad, axis=0),
            score_part.reshape(-1),
        ]
    )
    small_rows = -(-small.shape[0] // (16 * local_width)) * 16
    small_low = (
        jnp.pad(small, (0, small_rows * local_width - small.shape[0]))
        .astype(jnp.bfloat16)
        .reshape(small_rows, local_width)
    )

    dctx_send = ctx_grad_packed(attn_low, attn_other, w_out)
    own_dctx = to_heads(dctx_send)
    out_pack = out_grad_pack(
        pass_count, after(attn_low, dctx_send), attn_other, context_low, small_low
    )
    own_dctx, out_pack = together(own_dctx, out_pack)
    dkv, dq = attend_back(info, own_pack, sib_pack, own_dctx, ctx_turned, lse, key_turned)
    dkv_sib, dq_sib = together(sibling(dkv), sibling(dq))
    back_send = combine(info, dkv, dkv_sib, dq)
    back = to_heads(back_send)
    dkv, out_pack = after(dkv, back_send), after(out_pack, back_send)
    out_mine = lax.dynamic_index_in_dim(out_pack, parity, 0, keepdims=False)
    out_send = lax.dynamic_index_in_dim(out_pack, 1 - parity, 0, keepdims=False)
    out_both = out_mine.astype(jnp.float32) + sibling(out_send).astype(jnp.float32)
    head_grads = head_grad(info, tokens_all, dkv, dkv_sib, dq, dq_sib)
    back, head_grads, out_both = together(back, head_grads, out_both.astype(jnp.bfloat16))
    head_recv = to_heads(head_grads)
    out_recv = to_heads(out_both)
    token_own, token_send = token_grad(back, w_query, w_key, w_value)
    head_recv, token_send = together(head_recv, token_send)
    token_recv = swap(token_send)
    grad_tokens = attn_pre + token_own + token_recv.astype(jnp.float32)
    out_recv = after(out_recv, token_recv)
    grad_query, grad_key, grad_value = split_heads(head_recv)

    grad_up = late_sums[:, :width].astype(jnp.float32)
    grad_down = late_sums[:, width : 2 * width].astype(jnp.float32).T
    colbert_piece = after(late_sums, back)[:, 2 * width :]
    colbert_sum = colbert_piece.astype(jnp.float32) + swap(colbert_piece).astype(jnp.float32)
    grad_colbert = lax.all_gather(
        colbert_sum.astype(jnp.bfloat16), "pass", axis=0, axis_index_groups=ring, tiled=True
    ).astype(jnp.float32)

    out_sums = jnp.sum(out_recv.astype(jnp.float32), axis=0)
    grad_out = out_sums[: model // pass_count].T
    small_sums = out_sums[model // pass_count :]
    small_sums = (small_sums + swap(small_sums)).reshape(-1)
    norms = small_sums[: 4 * model].reshape(4, model)
    scores = small_sums[4 * model : small.shape[0]].reshape(score_part.shape)
    return (
        output_low,
        scores,
        grad_tokens,
        grad_query,
        grad_key,
        grad_value,
        grad_out,
        grad_up,
        grad_down,
        grad_colbert,
        norms[0],
        norms[1],
        norms[2],
        norms[3],
    )


def solution(mesh):
    by_head = mesh.shape["qry"] == 2
    return jax.shard_map(
        local_by_head if by_head else local_general,
        mesh=mesh,
        in_specs=(
            P(("pass", "qry"), None),
            P(None, "qry"),
            P(None, "qry"),
            P(None, "qry"),
            P("qry", None),
            P(),
            P(),
            P(None, "qry"),
            P("qry", None),
            P(),
            P(),
            P(),
            P("qry", None),
            P("qry", None),
            P(),
            P(("pass", "qry"), None),
            P("qry", None),
        ),
        out_specs=(
            P(("pass", "qry"), None),
            P(),
            P(("pass", "qry"), None),
            P("pass", "qry"),
            P("pass", "qry"),
            P("pass", "qry"),
            P("qry", "pass"),
            P("pass", "qry"),
            P("qry", "pass"),
            P(),
            P(),
            P(),
            P(),
            P(),
        ),
        check_vma=False,
    )
```

```python
import functools
import math

import jax
import jax.numpy as jnp
from jax import lax
from jax.experimental import pallas as pl
from jax.experimental.pallas import tpu as pltpu
from jax.sharding import PartitionSpec as P

HD = 64
SPAN = 8
LANES = 128
VMEM_LIMIT = 24 << 20
WIDE_LIMIT = 55 << 20
LOG2E = math.log2(math.e)


def passed_along(value, axis, steps):
    count = lax.axis_size(axis)
    first, last = (max(0, -steps), min(count, count - steps))
    return lax.ppermute(value, axis, [(source, source + steps) for source in range(first, last)])


def layer_norm(values, gain, shift):
    row_mean = jnp.mean(values, axis=-1, keepdims=True)
    centred = values - row_mean
    variance = jnp.mean(centred * centred, axis=-1, keepdims=True)
    return centred * lax.rsqrt(variance + 1e-05) * gain + shift


def gelu_exact(values):
    return 0.5 * values * (1.0 + jax.scipy.special.erf(values * 0.7071067811865476))


def normalize_rows(proj_rows):
    return proj_rows * lax.rsqrt(jnp.sum(proj_rows * proj_rows, axis=1, keepdims=True) + 1e-06)


def head_split(array):
    return array.reshape(array.shape[0], array.shape[1] // HD, HD)


def block_scores(queries, key_rows):
    return jnp.einsum("qhd,khd->hqk", queries, key_rows, preferred_element_type=jnp.float32) * 0.125


def grad_block(queries, ctx_grad, log_total, row_delta, key_rows, value_rows):
    scaled = block_scores(queries, key_rows)
    probs = jnp.exp(scaled - log_total[:, :, None])
    dprob = jnp.einsum("qhd,khd->hqk", ctx_grad, value_rows, preferred_element_type=jnp.float32)
    dscore = (0.125 * probs * (dprob - row_delta[:, :, None])).astype(jnp.bfloat16)
    dquery = jnp.einsum("hqk,khd->qhd", dscore, key_rows, preferred_element_type=jnp.float32)
    dkey = jnp.einsum("hqk,qhd->khd", dscore, queries, preferred_element_type=jnp.float32)
    dvalue = jnp.einsum(
        "hqk,qhd->khd", probs.astype(jnp.bfloat16), ctx_grad, preferred_element_type=jnp.float32
    )
    return (dquery, jnp.stack([dkey, dvalue]))


def contract_rows(left, right):
    return lax.dot_general(
        left, right, (((0,), (0,)), ((), ())), preferred_element_type=jnp.float32
    )


def contract_cols(left, right):
    return lax.dot_general(
        left, right, (((1,), (1,)), ((), ())), preferred_element_type=jnp.float32
    )


def local_general(
    tokens,
    w_query,
    w_key,
    w_value,
    w_out,
    gain_attn,
    shift_attn,
    w_up,
    w_down,
    gain_ffn,
    shift_ffn,
    w_colbert,
    query_vecs,
    match_index,
    passage_of,
    cot_act,
    cot_scores,
):
    pass_count = lax.axis_size("pass")
    qry_count = lax.axis_size("qry")
    pass_index = lax.axis_index("pass")
    qry_index = lax.axis_index("qry")
    own_id = passage_of[pass_index]

    def source_valid(offset):
        source = pass_index - offset
        inside = (source >= 0) & (source < pass_count)
        return inside & (passage_of[jnp.clip(source, 0, pass_count - 1)] == own_id)

    gathered = lax.all_gather(tokens, "qry", axis=0, tiled=True)
    block_rows = gathered.shape[0]
    local_width = w_query.shape[1]
    w_qkv = jnp.concatenate([w_query, w_key, w_value], axis=1)
    qkv_rows = jnp.dot(gathered, w_qkv, preferred_element_type=jnp.float32).astype(jnp.bfloat16)
    query_flat = qkv_rows[:, :local_width]
    key_flat = qkv_rows[:, local_width : 2 * local_width]
    value_flat = qkv_rows[:, 2 * local_width :]
    queries = head_split(query_flat)
    heads = queries.shape[1]
    own_pair = jnp.stack([key_flat, value_flat])
    offsets = [distance for distance in range(1, SPAN)] + [-distance for distance in range(1, SPAN)]

    def fetch_keys():
        received = []
        for offset in offsets:
            received.append(passed_along(own_pair, "pass", offset))
        return received

    remote = fetch_keys()

    def stat_of(kv_pair):
        return jax.nn.logsumexp(block_scores(queries, head_split(kv_pair[0])), axis=2)

    log_total = stat_of(own_pair)
    for offset, kv_pair in zip(offsets, remote):
        log_total = lax.cond(
            source_valid(offset),
            lambda current, kv_pair=kv_pair: jnp.logaddexp(current, stat_of(kv_pair)),
            lambda current: current,
            log_total,
        )

    def weighted(kv_pair):
        probs = jnp.exp(
            block_scores(queries, head_split(kv_pair[0])) - log_total[:, :, None]
        ).astype(jnp.bfloat16)
        return jnp.einsum(
            "hqk,khd->qhd", probs, head_split(kv_pair[1]), preferred_element_type=jnp.float32
        )

    context = weighted(own_pair)
    for offset, kv_pair in zip(offsets, remote):
        context = lax.cond(
            source_valid(offset),
            lambda running, kv_pair=kv_pair: running + weighted(kv_pair),
            lambda running: running,
            context,
        )
    context_low = context.reshape(block_rows, local_width).astype(jnp.bfloat16)
    piece_rows = context_low
    attn_rows = lax.psum_scatter(
        jnp.dot(piece_rows, w_out, preferred_element_type=jnp.float32).astype(jnp.bfloat16),
        "qry",
        scatter_dimension=0,
        tiled=True,
    ).astype(jnp.float32)
    hidden, norm_attn_back = jax.vjp(
        layer_norm, tokens.astype(jnp.float32) + attn_rows, gain_attn, shift_attn
    )
    hidden_all = lax.all_gather(hidden.astype(jnp.bfloat16), "qry", axis=0, tiled=True)
    inner_pre = jnp.dot(hidden_all, w_up, preferred_element_type=jnp.float32)
    gated_float, gelu_back = jax.vjp(gelu_exact, inner_pre)
    gated_low = gated_float.astype(jnp.bfloat16)
    piece_rows = gated_low
    ffn_rows = lax.psum_scatter(
        jnp.dot(piece_rows, w_down, preferred_element_type=jnp.float32).astype(jnp.bfloat16),
        "qry",
        scatter_dimension=0,
        tiled=True,
    ).astype(jnp.float32)
    output, norm_ffn_back = jax.vjp(layer_norm, hidden + ffn_rows, gain_ffn, shift_ffn)
    output_low = output.astype(jnp.bfloat16)
    proj_rows = jnp.dot(output_low, w_colbert, preferred_element_type=jnp.float32)
    unit_vecs, unit_back = jax.vjp(normalize_rows, proj_rows)
    unit_all = lax.all_gather(unit_vecs.astype(jnp.bfloat16), "qry", axis=0, tiled=True)
    seq_count = match_index.shape[1]
    query_rows = cot_scores.shape[0]
    numbers = jnp.arange(seq_count, dtype=jnp.int32)
    pick_col = numbers == own_id
    span_count = jnp.sum((passage_of == own_id).astype(jnp.int32))
    first_index = jnp.sum((passage_of < own_id).astype(jnp.int32))
    length = span_count * block_rows
    raw_pick = jnp.sum(jnp.where(pick_col[None, :], match_index, 0), axis=1)
    local_row = raw_pick % length - (pass_index - first_index) * block_rows
    one_hot = (local_row[:, None] == jnp.arange(block_rows, dtype=jnp.int32)[None, :]).astype(
        jnp.bfloat16
    )
    picked = jnp.dot(one_hot, unit_all, preferred_element_type=jnp.float32)
    query_float = query_vecs.astype(jnp.float32)
    match_vals = jnp.sum(query_float * picked, axis=1)
    per_query = jnp.sum(match_vals.reshape(query_rows, -1), axis=1)
    score_block = per_query[:, None] * pick_col.astype(jnp.float32)[None, :]
    score_part = lax.dynamic_update_slice(
        jnp.zeros((query_rows * qry_count, seq_count), jnp.float32),
        score_block,
        (qry_index * query_rows, jnp.zeros((), jnp.int32)),
    )
    cot_pick = jnp.sum(jnp.where(pick_col[None, :], cot_scores, 0.0), axis=1)
    token_weight = jnp.repeat(cot_pick, query_vecs.shape[0] // query_rows)
    weighted_queries = (token_weight[:, None] * query_float).astype(jnp.bfloat16)
    piece_rows = one_hot
    unit_grad = lax.psum_scatter(
        contract_rows(piece_rows, weighted_queries).astype(jnp.bfloat16),
        "qry",
        scatter_dimension=0,
        tiled=True,
    ).astype(jnp.float32)
    (proj_grad,) = unit_back(unit_grad)
    proj_low = proj_grad.astype(jnp.bfloat16)
    grad_colbert = contract_rows(output_low, proj_low)
    out_grad = cot_act.astype(jnp.float32) + contract_cols(proj_low, w_colbert)
    pre_grad, grad_gain_ffn, grad_shift_ffn = norm_ffn_back(out_grad)
    ffn_all = lax.all_gather(pre_grad.astype(jnp.bfloat16), "qry", axis=0, tiled=True)
    gated_grad = contract_cols(ffn_all, w_down)
    grad_down = contract_rows(gated_low, ffn_all)
    (inner_grad,) = gelu_back(gated_grad)
    inner_low = inner_grad.astype(jnp.bfloat16)
    grad_up = contract_rows(hidden_all, inner_low)
    piece_rows = inner_low
    hidden_grad = pre_grad + lax.psum_scatter(
        contract_cols(piece_rows, w_up).astype(jnp.bfloat16), "qry", scatter_dimension=0, tiled=True
    ).astype(jnp.float32)
    attn_pre_grad, grad_gain_attn, grad_shift_attn = norm_attn_back(hidden_grad)
    attn_all = lax.all_gather(attn_pre_grad.astype(jnp.bfloat16), "qry", axis=0, tiled=True)
    grad_out = contract_rows(context_low, attn_all)
    ctx_grad = head_split(contract_cols(attn_all, w_out).astype(jnp.bfloat16))
    row_delta = jnp.einsum("qhd,qhd->hq", ctx_grad.astype(jnp.float32), context)
    remote_back = fetch_keys()
    dquery, dkv_own = grad_block(
        queries, ctx_grad, log_total, row_delta, head_split(key_flat), head_split(value_flat)
    )
    key_value_grad = dkv_own
    zero_query = jnp.zeros_like(dquery)
    zero_pair = jnp.zeros((2, block_rows, heads, HD), jnp.float32)
    for offset, kv_pair in zip(offsets, remote_back):
        query_part, pair_part = lax.cond(
            source_valid(offset),
            lambda incoming: grad_block(
                queries,
                ctx_grad,
                log_total,
                row_delta,
                head_split(incoming[0]),
                head_split(incoming[1]),
            ),
            lambda incoming: (zero_query, zero_pair),
            kv_pair,
        )
        dquery = dquery + query_part
        returned = passed_along(
            pair_part.reshape(2, block_rows, local_width).astype(jnp.bfloat16), "pass", -offset
        ).astype(jnp.float32)
        key_value_grad = key_value_grad + returned.reshape(2, block_rows, heads, HD)
    dqkv_low = jnp.concatenate(
        [
            dquery.reshape(block_rows, local_width),
            key_value_grad[0].reshape(block_rows, local_width),
            key_value_grad[1].reshape(block_rows, local_width),
        ],
        axis=1,
    ).astype(jnp.bfloat16)
    grad_qkv = contract_rows(gathered, dqkv_low)
    piece_rows = dqkv_low
    grad_tokens = attn_pre_grad + lax.psum_scatter(
        contract_cols(piece_rows, w_qkv).astype(jnp.bfloat16),
        "qry",
        scatter_dimension=0,
        tiled=True,
    ).astype(jnp.float32)
    summed = (
        lax.psum_scatter(
            grad_qkv[:, :local_width].astype(jnp.bfloat16), "pass", scatter_dimension=0, tiled=True
        ).astype(jnp.float32),
        lax.psum_scatter(
            grad_qkv[:, local_width : 2 * local_width].astype(jnp.bfloat16),
            "pass",
            scatter_dimension=0,
            tiled=True,
        ).astype(jnp.float32),
        lax.psum_scatter(
            grad_qkv[:, 2 * local_width :].astype(jnp.bfloat16),
            "pass",
            scatter_dimension=0,
            tiled=True,
        ).astype(jnp.float32),
        lax.psum_scatter(
            grad_out.astype(jnp.bfloat16), "pass", scatter_dimension=1, tiled=True
        ).astype(jnp.float32),
        lax.psum_scatter(
            grad_up.astype(jnp.bfloat16), "pass", scatter_dimension=0, tiled=True
        ).astype(jnp.float32),
        lax.psum_scatter(
            grad_down.astype(jnp.bfloat16), "pass", scatter_dimension=1, tiled=True
        ).astype(jnp.float32),
    )
    shared = lax.psum(
        (grad_colbert, grad_gain_attn, grad_shift_attn, grad_gain_ffn, grad_shift_ffn, score_part),
        ("pass", "qry"),
    )
    return (
        output_low,
        shared[5],
        grad_tokens,
        summed[0],
        summed[1],
        summed[2],
        summed[3],
        summed[4],
        summed[5],
        shared[0],
        shared[1],
        shared[2],
        shared[3],
        shared[4],
    )


def swap_over(value, axis, mask):
    count = lax.axis_size(axis)
    return lax.ppermute(value, axis, [(index, index ^ mask) for index in range(count)])


def ring_chips(chips):
    layers = chips // 2
    return [2 * z for z in range(layers)] + [2 * z + 1 for z in reversed(range(layers))]


def low_lanes(rows):
    return lax.broadcasted_iota(jnp.int32, (rows, LANES), 1) < HD


def split_lanes(first, second):
    low = low_lanes(first.shape[0])
    return (
        jnp.where(low, first, pltpu.roll(second, HD, 1)),
        jnp.where(low, pltpu.roll(first, HD, 1), second),
    )


def dot_nn(left, right):
    return jnp.dot(left, right, preferred_element_type=jnp.float32)


def dot_nt(left, right):
    return contract_cols(left, right)


def params(*semantics, limit=VMEM_LIMIT):
    return pltpu.CompilerParams(
        dimension_semantics=semantics or None, vmem_limit_bytes=limit
    )


def cost(flops, moved, transcendentals=0):
    return pl.CostEstimate(
        flops=int(flops), bytes_accessed=int(moved), transcendentals=int(transcendentals)
    )


def project_body(x_ref, wq_ref, wk_ref, wv_ref, out_ref):
    x = x_ref[...]
    rows = x.shape[0]
    half = rows // 2
    query = dot_nn(x, wq_ref[...])
    key = dot_nn(x, wk_ref[...])
    value = dot_nn(x, wv_ref[...])
    for pair in range(query.shape[1] // LANES):
        cols = slice(pair * LANES, (pair + 1) * LANES)
        first, second = split_lanes(key[:, cols], value[:, cols])
        out_ref[2 * pair, 0:rows] = first.astype(jnp.bfloat16)
        out_ref[2 * pair + 1, 0:rows] = second.astype(jnp.bfloat16)
        first, second = split_lanes(query[:half, cols], query[half:, cols])
        out_ref[2 * pair, rows : rows + half] = first.astype(jnp.bfloat16)
        out_ref[2 * pair + 1, rows : rows + half] = second.astype(jnp.bfloat16)


def project(x, wq, wk, wv):
    rows, depth = x.shape
    width = wq.shape[1]
    heads = width // HD
    steps = 2
    weight = pl.BlockSpec((depth, width // steps), lambda i: (0, i))
    return pl.pallas_call(
        project_body,
        grid=(steps,),
        in_specs=[pl.BlockSpec((rows, depth), lambda i: (0, 0)), weight, weight, weight],
        out_specs=pl.BlockSpec((heads // steps, rows * 3 // 2, LANES), lambda i: (i, 0, 0)),
        out_shape=jax.ShapeDtypeStruct((heads, rows * 3 // 2, LANES), jnp.bfloat16),
        compiler_params=params("arbitrary", limit=WIDE_LIMIT),
        cost_estimate=cost(2 * rows * depth * width * 3, 2 * (3 * depth * width + 4 * rows * depth)),
        name="project",
    )(x, wq, wk, wv)


def load_query(packed):
    wide = packed.astype(jnp.float32)
    low = low_lanes(wide.shape[0])
    top = jnp.where(low, wide, 0.0)
    bottom = jnp.where(low, pltpu.roll(wide, HD, 1), 0.0)
    return jnp.concatenate([top, bottom], axis=0).astype(jnp.bfloat16)


def pack_transposed(columns):
    half = columns.shape[1] // 2
    return jnp.concatenate([columns[:, :half], columns[:, half:]], axis=0).T


def square_sums(rows_low):
    group = lambda axis: lax.broadcasted_iota(jnp.int32, (LANES, LANES), axis) // HD
    ones = (group(0) == group(1)).astype(jnp.bfloat16)
    wide = rows_low.astype(jnp.float32)
    sums = dot_nn((wide * wide).astype(jnp.bfloat16), ones)
    return jnp.max(sums.reshape(sums.shape[0] // 8, 8, LANES), axis=0)


def over_blocks(first, count, step):
    for size in (8, 4, 2, 1):

        @pl.when(count & size != 0)
        def _(size=size):
            step(first + (count & ~(2 * size - 1)), size)


def attend_body(
    info_ref, own_ref, sib_ref, ctx_ref, ctxt_ref, lse_ref, kv_s, v1_s, q_s, total_s, score_s, top_s
):
    chips = own_ref.shape[0]
    blocks = 2 * chips
    rows = kv_s.shape[1]
    half = rows // 2
    parity = info_ref[2 * blocks]
    scale = 0.125 * LOG2E
    low = low_lanes(rows)
    key_top = query_top = jnp.zeros((8, LANES), jnp.float32)
    for chip in range(chips):
        for ref, which in ((own_ref, parity), (sib_ref, 1 - parity)):
            block = ref[chip, 0:rows]
            kv_s[2 * chip + which] = block
            v1_s[2 * chip + which] = jnp.where(low, 1.0, block.astype(jnp.float32)).astype(
                jnp.bfloat16
            )
            key_top = jnp.maximum(key_top, square_sums(block))
        packed = own_ref[chip, rows : rows + half]
        q_s[chip] = load_query(packed)
        query_top = jnp.maximum(query_top, square_sums(packed))
    key_top = jnp.max(jnp.where(low_lanes(8), key_top, 0.0))
    bound = jnp.max(query_top) * key_top * (1.02 * scale * scale)
    safe = bound < 3600.0

    @pl.when(safe)
    def _():
        def one_item(item, carry):
            query = q_s[item]
            total_s[item] = jnp.zeros((rows, LANES), jnp.float32)

            def step(block, n):
                keys = kv_s[pl.ds(block, n)].reshape(n * rows, LANES)
                values = v1_s[pl.ds(block, n)].reshape(n * rows, LANES)
                prob = jnp.exp2(dot_nt(query, keys) * scale).astype(jnp.bfloat16)
                total_s[item] += dot_nn(prob, values)

            place = 2 * item + parity
            over_blocks(info_ref[place], info_ref[blocks + place], step)
            top_s[item] = jnp.zeros((8, rows), jnp.float32)
            return carry

        lax.fori_loop(0, chips, one_item, 0)

    @pl.when(jnp.logical_not(safe))
    def _():
        def one_item(item, carry):
            query = q_s[item]
            place = 2 * item + parity
            first, count = info_ref[place], info_ref[blocks + place]

            def scores(step, top):
                score = dot_nt(query, kv_s[first + step]) * scale
                score_s[step] = score
                return jnp.maximum(top, score)

            top = lax.fori_loop(0, count, scores, jnp.full((rows, rows), -jnp.inf, jnp.float32))
            top = jnp.max(top, axis=1, keepdims=True)
            total_s[item] = jnp.zeros((rows, LANES), jnp.float32)

            def weigh(step, carry):
                prob = jnp.exp2(score_s[step] - top).astype(jnp.bfloat16)
                total_s[item] += dot_nn(prob, v1_s[first + step])
                return carry

            lax.fori_loop(0, count, weigh, 0)
            top_s[item] = jnp.broadcast_to(top, (rows, LANES)).T[0:8]
            return carry

        lax.fori_loop(0, chips, one_item, 0)

    narrow = low_lanes(half)
    for item in range(chips):
        total = total_s[item]
        turned = total.T
        weight = turned[0:8]
        lse_ref[item] = top_s[item] + jnp.log2(weight)
        ctxt_ref[item] = turned[HD:] / weight[0:1]
        inverse = 1.0 / jnp.where(low, total, 1.0)
        context = total * pltpu.roll(inverse, HD, 1)
        ctx_ref[item] = jnp.where(
            narrow, pltpu.roll(context[:half], HD, 1), context[half:]
        ).astype(jnp.bfloat16)


def whole():
    return pl.BlockSpec(memory_space=pltpu.VMEM)


def attend(info, own, sib):
    chips, packed, _ = own.shape
    rows = packed * 2 // 3
    blocks = 2 * chips
    return pl.pallas_call(
        attend_body,
        in_specs=[pl.BlockSpec(memory_space=pltpu.SMEM), whole(), whole()],
        out_specs=[whole()] * 3,
        out_shape=[
            jax.ShapeDtypeStruct((chips, rows // 2, LANES), jnp.bfloat16),
            jax.ShapeDtypeStruct((chips, HD, rows), jnp.float32),
            jax.ShapeDtypeStruct((chips, 8, rows), jnp.float32),
        ],
        scratch_shapes=[
            pltpu.VMEM((blocks, rows, LANES), jnp.bfloat16),
            pltpu.VMEM((blocks, rows, LANES), jnp.bfloat16),
            pltpu.VMEM((chips, rows, LANES), jnp.bfloat16),
            pltpu.VMEM((chips, rows, LANES), jnp.float32),
            pltpu.VMEM((SPAN, rows, rows), jnp.float32),
            pltpu.VMEM((chips, 8, rows), jnp.float32),
        ],
        compiler_params=params(limit=2 * VMEM_LIMIT),
        cost_estimate=cost(2 * 2 * 40 * rows * rows * LANES, 4 << 20, 40 * rows * rows),
        name="attend",
    )(info, own, sib)


def prepare_body(info_ref, own_ref, sib_ref, kv_ref, kt_ref, q_ref):
    chips = own_ref.shape[0]
    rows = kv_ref.shape[1]
    parity = info_ref[4 * chips]
    for chip in range(chips):
        for ref, which in ((own_ref, parity), (sib_ref, 1 - parity)):
            block = ref[chip, 0:rows]
            kv_ref[2 * chip + which] = block
            kt_ref[2 * chip + which] = block.astype(jnp.float32).T[:HD].astype(jnp.bfloat16)
        q_ref[chip] = load_query(own_ref[chip, rows : rows + rows // 2])


def prepare(info, own, sib):
    chips, packed, _ = own.shape
    rows = packed * 2 // 3
    return pl.pallas_call(
        prepare_body,
        in_specs=[pl.BlockSpec(memory_space=pltpu.SMEM), whole(), whole()],
        out_specs=[whole()] * 3,
        out_shape=[
            jax.ShapeDtypeStruct((2 * chips, rows, LANES), jnp.bfloat16),
            jax.ShapeDtypeStruct((2 * chips, HD, rows), jnp.bfloat16),
            jax.ShapeDtypeStruct((chips, rows, LANES), jnp.bfloat16),
        ],
        compiler_params=params(),
        cost_estimate=cost(1 << 20, 4 << 20),
        name="prepare",
    )(info, own, sib)


def attend_back_body(
    info_ref,
    kv_ref,
    kt_ref,
    q_ref,
    dctx_ref,
    ctxt_ref,
    lse_ref,
    mine_ref,
    other_ref,
    dq_ref,
    acc_s,
    both_s,
    delta_s,
    total_s,
):
    chips = q_ref.shape[0]
    blocks = 2 * chips
    rows = kv_ref.shape[1]
    half = rows // 2
    parity = info_ref[2 * blocks]
    scale = 0.125 * LOG2E
    low = low_lanes(half)
    for item in range(chips):
        packed = dctx_ref[item].astype(jnp.float32)
        both_s[item, :rows] = q_ref[item]
        both_s[item, rows : rows + half] = jnp.where(
            low, 0.0, pltpu.roll(packed, HD, 1)
        ).astype(jnp.bfloat16)
        both_s[item, rows + half :] = jnp.where(low, 0.0, packed).astype(jnp.bfloat16)
        turned = packed.T
        turned = jnp.concatenate([turned[:HD], turned[HD:]], axis=1)
        delta = jnp.sum(turned * ctxt_ref[item], axis=0, keepdims=True)
        delta_s[item] = jnp.broadcast_to(delta, (8, rows))
        acc_s[2 * item] = jnp.zeros((rows, LANES), jnp.float32)
        acc_s[2 * item + 1] = jnp.zeros((rows, LANES), jnp.float32)
        total_s[item] = jnp.zeros((HD, rows), jnp.float32)

    def one_item(item, carry):
        query = both_s[item, :rows]
        dctx = both_s[item, rows:]
        delta = delta_s[item, 0:1]
        lse = lse_ref[item, 0:1]

        def step(block, n):
            kv = kv_ref[pl.ds(block, n)].reshape(n * rows, LANES)
            prob = jnp.exp2(dot_nt(kv, query) * scale - lse)
            dscore = (prob * (dot_nt(kv, dctx) - delta)).astype(jnp.bfloat16)
            pair = jnp.concatenate([dscore, prob.astype(jnp.bfloat16)], axis=1)
            acc_s[pl.ds(block, n)] += dot_nn(pair, both_s[item]).reshape(n, rows, LANES)
            total = total_s[item]
            for part in range(n):
                total = total + dot_nn(kt_ref[block + part], dscore[part * rows : (part + 1) * rows])
            total_s[item] = total

        place = 2 * item + parity
        over_blocks(info_ref[place], info_ref[blocks + place], step)
        return carry

    lax.fori_loop(0, chips, one_item, 0)
    key_scale = jnp.where(low_lanes(rows), 0.125, 1.0)
    for item in range(chips):
        dq_ref[item] = pack_transposed(total_s[item] * 0.125).astype(jnp.bfloat16)
        mine_ref[item] = (acc_s[2 * item + parity] * key_scale).astype(jnp.bfloat16)
        other_ref[item] = (acc_s[2 * item + 1 - parity] * key_scale).astype(jnp.bfloat16)


def attend_back(info, kv, kt, query, dctx, ctxt, lse):
    chips, rows, _ = query.shape
    blocks = 2 * chips
    share = jax.ShapeDtypeStruct((chips, rows, LANES), jnp.bfloat16)
    return pl.pallas_call(
        attend_back_body,
        in_specs=[pl.BlockSpec(memory_space=pltpu.SMEM)] + [whole()] * 6,
        out_specs=[whole()] * 3,
        out_shape=[share, share, jax.ShapeDtypeStruct((chips, rows // 2, LANES), jnp.bfloat16)],
        scratch_shapes=[
            pltpu.VMEM((blocks, rows, LANES), jnp.float32),
            pltpu.VMEM((chips, 2 * rows, LANES), jnp.bfloat16),
            pltpu.VMEM((chips, 8, rows), jnp.float32),
            pltpu.VMEM((chips, HD, rows), jnp.float32),
        ],
        compiler_params=params(limit=WIDE_LIMIT),
        cost_estimate=cost(2 * 5 * 40 * rows * rows * LANES, 5 << 20, 40 * rows * rows),
        name="attend_back",
    )(info, kv, kt, query, dctx, ctxt, lse)


def combine_body(mine_ref, sib_ref, dq_ref, out_ref):
    chips, rows, _ = mine_ref.shape
    for chip in range(chips):
        total = mine_ref[chip].astype(jnp.float32) + sib_ref[chip].astype(jnp.float32)
        out_ref[chip, 0:rows] = total.astype(jnp.bfloat16)
        out_ref[chip, rows:] = dq_ref[chip]


def combine(mine, sib, dq):
    chips, rows, _ = mine.shape
    return pl.pallas_call(
        combine_body,
        in_specs=[whole()] * 3,
        out_specs=whole(),
        out_shape=jax.ShapeDtypeStruct((chips, rows * 3 // 2, LANES), jnp.bfloat16),
        compiler_params=params(),
        cost_estimate=cost(1 << 20, 2 << 20),
        name="combine",
    )(mine, sib, dq)


def out_norm_body(
    info_ref,
    in_ref,
    other_ref,
    w_ref,
    w_mine_ref,
    w_sib_ref,
    tok_ref,
    gain_ref,
    shift_ref,
    ctx_ref,
    *outs,
):
    *outs, far_s = outs
    heads, half, _ = in_ref.shape
    parity = info_ref[2 * 2 * in_ref.shape[0]]
    for pair in range(heads // 2):
        cols = slice(pair * LANES, (pair + 1) * LANES)
        top, bottom = split_lanes(
            in_ref[2 * pair].astype(jnp.float32), in_ref[2 * pair + 1].astype(jnp.float32)
        )
        ctx_ref[0:half, cols] = top.astype(jnp.bfloat16)
        ctx_ref[half:, cols] = bottom.astype(jnp.bfloat16)
        top, bottom = split_lanes(
            other_ref[2 * pair].astype(jnp.float32), other_ref[2 * pair + 1].astype(jnp.float32)
        )
        far_s[0:half, cols] = bottom.astype(jnp.bfloat16)
        far_s[half:, cols] = top.astype(jnp.bfloat16)
    first = parity == 0
    mine, sib = w_mine_ref[...], w_sib_ref[...]
    w_far = jnp.concatenate([jnp.where(first, mine, sib), jnp.where(first, sib, mine)], axis=0)
    rows = dot_nn(ctx_ref[...], w_ref[...]) + dot_nn(far_s[...], w_far)
    unit, inverse = norm_rows(tok_ref[...].astype(jnp.float32) + rows)
    hidden = unit * gain_ref[...] + shift_ref[...]
    inverse = jnp.broadcast_to(inverse, (2 * half, LANES))
    for index, value in enumerate((hidden, hidden.astype(jnp.bfloat16), unit, inverse)):
        outs[2 * index][...] = value[:half]
        outs[2 * index + 1][...] = value[half:]


def out_norm(info, packed, packed_other, w_out, w_mine, w_sib, tokens, gain, shift):
    heads, half, _ = packed.shape
    width, depth = w_out.shape
    wide = jax.ShapeDtypeStruct((half, depth), jnp.float32)
    low = jax.ShapeDtypeStruct((half, depth), jnp.bfloat16)
    narrow = jax.ShapeDtypeStruct((half, LANES), jnp.float32)
    return pl.pallas_call(
        out_norm_body,
        in_specs=[pl.BlockSpec(memory_space=pltpu.SMEM)] + [whole()] * 8,
        out_specs=[whole()] * 9,
        out_shape=[jax.ShapeDtypeStruct((2 * half, width), jnp.bfloat16)]
        + [wide, wide, low, low, wide, wide, narrow, narrow],
        scratch_shapes=[pltpu.VMEM((2 * half, width), jnp.bfloat16)],
        compiler_params=params(),
        cost_estimate=cost(8 * half * width * depth, 5 << 20),
        name="out_norm",
    )(info, packed, packed_other, w_out, w_mine, w_sib, tokens, gain[None], shift[None])


def ctx_grad_body(own_ref, other_ref, w_ref, out_ref):
    half = out_ref.shape[1]
    grad = dot_nt(jnp.concatenate([own_ref[...], other_ref[...]], axis=0), w_ref[...])
    for pair in range(grad.shape[1] // LANES):
        cols = slice(pair * LANES, (pair + 1) * LANES)
        first, second = split_lanes(grad[:half, cols], grad[half:, cols])
        out_ref[2 * pair] = first.astype(jnp.bfloat16)
        out_ref[2 * pair + 1] = second.astype(jnp.bfloat16)


def ctx_grad_packed(grad_own, grad_other, w_out):
    rows, depth = 2 * grad_own.shape[0], grad_own.shape[1]
    width = w_out.shape[0]
    return pl.pallas_call(
        ctx_grad_body,
        in_specs=[whole()] * 3,
        out_specs=whole(),
        out_shape=jax.ShapeDtypeStruct((width // HD, rows // 2, LANES), jnp.bfloat16),
        compiler_params=params(),
        cost_estimate=cost(2 * rows * width * depth, 2 << 20),
        name="ctx_grad",
    )(grad_own, grad_other, w_out)


def head_grad_body(info_ref, tok_ref, own_ref, sib_ref, out_ref, acc_s, grad_s):
    step = pl.program_id(0)
    steps = pl.num_programs(0)
    chips, packed, _ = own_ref.shape
    blocks = 2 * chips
    rows = packed * 2 // 3
    parity = info_ref[2 * blocks]
    group = chips // steps
    columns = []
    for index in range(group):
        place = step * group + index
        chip = jnp.where(place < chips // 2, 2 * place, 2 * chips - 1 - 2 * place)
        own, sib = own_ref[chip].astype(jnp.float32), sib_ref[chip].astype(jnp.float32)
        for core in range(2):
            block = jnp.where(parity == core, own, sib)
            dq = block[rows:].T
            dq = jnp.concatenate([dq[:HD], dq[HD:]], axis=1)
            columns.append(jnp.concatenate([block[:rows].T, dq], axis=0).astype(jnp.bfloat16))
    part = dot_nn(jnp.concatenate(columns, axis=1), tok_ref[...])

    @pl.when(step == 0)
    def _():
        acc_s[...] = part

    @pl.when(step > 0)
    def _():
        acc_s[...] += part

    @pl.when(step == steps - 1)
    def _():
        grad = acc_s[...]
        depth = grad.shape[1] // blocks
        wide = jnp.concatenate([grad, grad[2 * HD :]], axis=0)
        grad_s[...] = wide.T.reshape(blocks, depth, 2 * LANES)

        def pack(index, carry):
            part = grad_s[2 * index + parity]
            out_ref[index, 0:depth] = part[:, :LANES].astype(jnp.bfloat16)
            query = part[:, LANES:]
            mixed = jnp.where(low_lanes(depth // 2), query[: depth // 2], query[depth // 2 :])
            out_ref[index, depth : depth + depth // 2] = mixed.astype(jnp.bfloat16)
            return carry

        lax.fori_loop(0, chips, pack, 0)


def head_grad(info, tokens_all, own, sib):
    chips, packed, _ = own.shape
    blocks = 2 * chips
    rows = packed * 2 // 3
    depth = tokens_all.shape[1]
    piece = depth // blocks
    steps = 4
    full = lambda shape: pl.BlockSpec(shape, lambda i: (0,) * len(shape))
    return pl.pallas_call(
        head_grad_body,
        grid=(steps,),
        in_specs=[
            pl.BlockSpec(memory_space=pltpu.SMEM),
            pl.BlockSpec((blocks * rows // steps, depth), lambda i: (i, 0)),
            full(own.shape),
            full(sib.shape),
        ],
        out_specs=full((chips, piece + piece // 2, LANES)),
        out_shape=jax.ShapeDtypeStruct((chips, piece + piece // 2, LANES), jnp.bfloat16),
        scratch_shapes=[
            pltpu.VMEM((3 * HD, depth), jnp.float32),
            pltpu.VMEM((blocks, piece, 2 * LANES), jnp.float32),
        ],
        compiler_params=params("arbitrary", limit=2 * VMEM_LIMIT),
        cost_estimate=cost(2 * blocks * rows * depth * 3 * HD, blocks * rows * depth * 2),
        name="head_grad",
    )(info, tokens_all, own, sib)


def token_grad_body(in_ref, wq_ref, wk_ref, wv_ref, own_ref, send_ref, d_s):
    heads = in_ref.shape[0]
    rows = d_s.shape[1]
    half = rows // 2
    load = lambda head, lo, hi: in_ref[head, lo:hi].astype(jnp.float32)
    for pair in range(heads // 2):
        cols = slice(pair * LANES, (pair + 1) * LANES)
        a, b = 2 * pair, 2 * pair + 1
        key, value = split_lanes(load(a, 0, rows), load(b, 0, rows))
        d_s[1, :, cols] = key.astype(jnp.bfloat16)
        d_s[2, :, cols] = value.astype(jnp.bfloat16)
        top, bottom = split_lanes(load(a, rows, rows + half), load(b, rows, rows + half))
        d_s[0, :half, cols] = top.astype(jnp.bfloat16)
        d_s[0, half:, cols] = bottom.astype(jnp.bfloat16)
    total = dot_nt(d_s[0], wq_ref[...]) + dot_nt(d_s[1], wk_ref[...]) + dot_nt(d_s[2], wv_ref[...])
    own_ref[...] = total[:half]
    send_ref[...] = total[half:].astype(jnp.bfloat16)


def token_grad(packed, wq, wk, wv):
    depth, width = wq.shape
    rows = packed.shape[1] * 2 // 3
    return pl.pallas_call(
        token_grad_body,
        in_specs=[whole()] * 4,
        out_specs=[whole()] * 2,
        out_shape=[
            jax.ShapeDtypeStruct((rows // 2, depth), jnp.float32),
            jax.ShapeDtypeStruct((rows // 2, depth), jnp.bfloat16),
        ],
        scratch_shapes=[pltpu.VMEM((3, rows, width), jnp.bfloat16)],
        compiler_params=params(),
        cost_estimate=cost(6 * rows * depth * width, 5 << 20),
        name="token_grad",
    )(packed, wq, wk, wv)


def split_heads_body(in_ref, gq_ref, gk_ref, gv_ref):
    heads = in_ref.shape[0]
    piece = gq_ref.shape[0]
    last = piece + piece // 2
    load = lambda head, lo, hi: in_ref[head, lo:hi].astype(jnp.float32)
    for pair in range(heads // 2):
        cols = slice(pair * LANES, (pair + 1) * LANES)
        a, b = 2 * pair, 2 * pair + 1
        key, value = split_lanes(load(a, 0, piece), load(b, 0, piece))
        gk_ref[:, cols] = key
        gv_ref[:, cols] = value
        top, bottom = split_lanes(load(a, piece, last), load(b, piece, last))
        gq_ref[: piece // 2, cols] = top
        gq_ref[piece // 2 :, cols] = bottom


def split_heads(packed):
    heads, height, _ = packed.shape
    grad = jax.ShapeDtypeStruct((height * 2 // 3, heads * HD), jnp.float32)
    return pl.pallas_call(
        split_heads_body,
        in_specs=[whole()],
        out_specs=[whole()] * 3,
        out_shape=[grad] * 3,
        compiler_params=params(),
        cost_estimate=cost(1 << 18, 1 << 20),
        name="split_heads",
    )(packed)


def out_sum_body(keep_ref, came_ref, out_ref):
    piece = out_ref.shape[1]
    for tile in range(out_ref.shape[0] // LANES):
        rows = slice(tile * piece, (tile + 1) * piece)
        total = keep_ref[0, rows].astype(jnp.float32) + came_ref[0, rows].astype(jnp.float32)
        out_ref[tile * LANES : (tile + 1) * LANES] = total.T


def out_sum(keep, came, width):
    piece = keep.shape[1] * LANES // width
    return pl.pallas_call(
        out_sum_body,
        in_specs=[whole()] * 2,
        out_specs=whole(),
        out_shape=jax.ShapeDtypeStruct((width, piece), jnp.float32),
        compiler_params=params(),
        cost_estimate=cost(1 << 17, 1 << 19),
        name="out_sum",
    )(keep, came)


def late_grad_body(orders, tiles, first_ref, *refs):
    *arrays, out_ref, turned_s, tile_s, sems = refs
    tile = tile_s.shape[2]
    terms = [arrays[index : index + 4] for index in range(0, len(arrays), 4)]
    first = first_ref[0] == 0

    def ordered(own, other):
        return (jnp.where(first, own, other), jnp.where(first, other, own))

    def columns(place):
        return pl.ds(pl.multiple_of(place * tile, tile), tile)

    def copy(place):
        slot = place % 2
        return pltpu.make_async_copy(tile_s.at[slot], out_ref.at[:, columns(place)], sems.at[slot])

    start = 0
    for index, (own, other, own_right, other_right) in enumerate(terms):
        half, depth = own.shape
        size = depth // len(orders[index])
        for place, chip in enumerate(orders[index]):
            cols = slice(chip * size, (chip + 1) * size)
            rows = slice(place * size, (place + 1) * size)
            for which, piece in enumerate(ordered(own[:, cols], other[:, cols])):
                turned_s[rows, which * half : (which + 1) * half] = piece.T

        def step(number, carry, start=start, own_right=own_right, other_right=other_right):
            place = start + number
            cols = columns(number)
            right = jnp.concatenate(ordered(own_right[:, cols], other_right[:, cols]), axis=0)

            @pl.when(place >= 2)
            def _():
                copy(place - 2).wait()

            tile_s[place % 2] = dot_nn(turned_s[...], right).astype(jnp.bfloat16)
            copy(place).start()
            return carry

        lax.fori_loop(0, tiles[index], step, 0)
        start += tiles[index]
    for place in range(start - 2, start):
        copy(place).wait()


def late_grad(first, chips, terms):
    half, depth = terms[0][0].shape
    tile = 1024
    orders = [ring_chips(chips) if term[4] else list(range(chips)) for term in terms]
    arrays = [array for term in terms for array in term[:4]]
    tiles = [term[2].shape[1] // tile for term in terms]
    width = sum(tiles) * tile
    return pl.pallas_call(
        functools.partial(late_grad_body, orders, tiles),
        in_specs=[pl.BlockSpec(memory_space=pltpu.SMEM)] + [whole()] * len(arrays),
        out_specs=pl.BlockSpec(memory_space=pl.ANY),
        out_shape=jax.ShapeDtypeStruct((depth, width), jnp.bfloat16),
        scratch_shapes=[
            pltpu.VMEM((depth, 2 * half), jnp.bfloat16),
            pltpu.VMEM((2, depth, tile), jnp.bfloat16),
            pltpu.SemaphoreType.DMA((2,)),
        ],
        compiler_params=params(limit=WIDE_LIMIT),
        cost_estimate=cost(4 * half * depth * width, 2 * depth * width + (3 << 20)),
        name="late_grad",
    )(first, *arrays)


def halve_body(place, info_ref, mine_ref, came_ref, keep_ref, send_ref):
    bit = info_ref[place]
    for index in range(keep_ref.shape[0]):
        for ref, block in ((keep_ref, 2 * index + bit), (send_ref, 2 * index + 1 - bit)):
            total = mine_ref[block].astype(jnp.float32) + came_ref[block].astype(jnp.float32)
            ref[index] = total.astype(jnp.bfloat16)


def halve(info, place, mine, came):
    count, height, width = mine.shape
    share = jax.ShapeDtypeStruct((count // 2, height, width), jnp.bfloat16)
    return pl.pallas_call(
        functools.partial(halve_body, place),
        in_specs=[pl.BlockSpec(memory_space=pltpu.SMEM)] + [whole()] * 2,
        out_specs=[whole()] * 2,
        out_shape=[share] * 2,
        compiler_params=params(),
        cost_estimate=cost(1 << 18, 2 << 20),
        name="halve",
    )(info, mine, came)


def widen_body(in_ref, out_ref):
    out_ref[...] = in_ref[...].astype(jnp.float32)


def widen(values):
    rows, width = values.shape
    steps = 4
    block = pl.BlockSpec((rows // steps, width), lambda i: (i, 0))
    return pl.pallas_call(
        widen_body,
        grid=(steps,),
        in_specs=[block],
        out_specs=block,
        out_shape=jax.ShapeDtypeStruct((rows, width), jnp.float32),
        compiler_params=params("arbitrary", limit=WIDE_LIMIT),
        cost_estimate=cost(1 << 20, 6 << 20),
        name="widen",
    )(values)


def out_grad_body(info_ref, left_ref, other_ref, ctx_ref, mine_ref, send_ref, grad_s):
    blocks, piece, width = grad_s.shape
    chips = blocks // 2
    parity = info_ref[2 * blocks]
    left = jnp.concatenate([left_ref[...], other_ref[...]], axis=0)
    grad_s[...] = contract_rows(left, ctx_ref[...]).reshape(blocks, piece, width)
    for chip in range(chips):
        for ref, block in ((mine_ref, 2 * chip + parity), (send_ref, 2 * chip + 1 - parity)):
            part = grad_s[block].astype(jnp.bfloat16)
            for tile in range(width // LANES):
                cols = slice(tile * LANES, (tile + 1) * LANES)
                ref[chip, tile * piece : (tile + 1) * piece] = part[:, cols]


def out_grad_pack(info, chips, grad_own, grad_other, context_low):
    depth = grad_own.shape[1]
    rows, width = context_low.shape
    piece = depth // (2 * chips)
    height = piece * width // LANES
    share = jax.ShapeDtypeStruct((chips, height, LANES), jnp.bfloat16)
    return pl.pallas_call(
        out_grad_body,
        in_specs=[pl.BlockSpec(memory_space=pltpu.SMEM)] + [whole()] * 3,
        out_specs=[whole()] * 2,
        out_shape=[share] * 2,
        scratch_shapes=[pltpu.VMEM((2 * chips, piece, width), jnp.float32)],
        compiler_params=params(),
        cost_estimate=cost(2 * rows * depth * width, 2 << 20),
        name="out_grad",
    )(info, grad_own, grad_other, context_low)


def norm_rows(values):
    centred = values - jnp.mean(values, axis=-1, keepdims=True)
    inverse = lax.rsqrt(jnp.mean(centred * centred, axis=-1, keepdims=True) + 1e-05)
    return centred * inverse, inverse


def back_rows(grad, gain, unit, inverse):
    scaled = grad * gain
    along = jnp.mean(scaled * unit, axis=-1, keepdims=True)
    return (scaled - jnp.mean(scaled, axis=-1, keepdims=True) - unit * along) * inverse


def store_sums(ref, grad, unit):
    width = ref.shape[1]
    for index, total in enumerate((jnp.sum(grad * unit, axis=0), jnp.sum(grad, axis=0))):
        for part in range(2):
            row = 2 * index + part
            ref[row : row + 1] = total[None, part * width : (part + 1) * width]


def attn_norm_back_body(
    pre_ref, own_ref, recv_ref, gain_ref, unit_ref, inv_ref, grad_ref, low_ref, sums_ref
):
    grad = pre_ref[...] + (own_ref[...].astype(jnp.float32) + recv_ref[...].astype(jnp.float32))
    unit = unit_ref[...]
    back = back_rows(grad, gain_ref[...], unit, inv_ref[:, 0:1])
    grad_ref[...] = back
    low_ref[...] = back.astype(jnp.bfloat16)
    store_sums(sums_ref, grad, unit)


def attn_norm_back(pre, own, recv, gain, unit, inverse, width):
    rows, depth = pre.shape
    return pl.pallas_call(
        attn_norm_back_body,
        in_specs=[whole()] * 6,
        out_specs=[whole()] * 3,
        out_shape=[
            jax.ShapeDtypeStruct((rows, depth), jnp.float32),
            jax.ShapeDtypeStruct((rows, depth), jnp.bfloat16),
            jax.ShapeDtypeStruct((4, width), jnp.float32),
        ],
        compiler_params=params(),
        cost_estimate=cost(1 << 20, 2 << 20),
        name="attn_norm_back",
    )(pre, own, recv, gain[None], unit, inverse)


def turn_body(
    hid_ref,
    own_ref,
    recv_ref,
    gain_ref,
    shift_ref,
    w_ref,
    pick_ref,
    cot_ref,
    out_ref,
    unit_ref,
    proj_ref,
    pre_ref,
    low_ref,
    sums_ref,
):
    values = hid_ref[...] + (own_ref[...].astype(jnp.float32) + recv_ref[...].astype(jnp.float32))
    unit, inverse = norm_rows(values)
    gain = gain_ref[...]
    output = (unit * gain + shift_ref[...]).astype(jnp.bfloat16)
    out_ref[...] = output
    proj = dot_nn(output, w_ref[...])
    scale = lax.rsqrt(jnp.sum(proj * proj, axis=1, keepdims=True) + 1e-06)
    vec = proj * scale
    unit_ref[...] = vec.astype(jnp.bfloat16)
    pick = pick_ref[...]
    along = jnp.sum(vec * pick, axis=1, keepdims=True)
    proj_low = ((pick - vec * along) * scale).astype(jnp.bfloat16)
    proj_ref[...] = proj_low
    grad = cot_ref[...].astype(jnp.float32) + dot_nt(proj_low, w_ref[...])
    pre = back_rows(grad, gain, unit, inverse)
    pre_ref[...] = pre
    low_ref[...] = pre.astype(jnp.bfloat16)
    store_sums(sums_ref, grad, unit)


def turn(hidden, own, recv, gain, shift, w_colbert, pick, cot, width):
    rows, depth = hidden.shape
    low = jax.ShapeDtypeStruct((rows, depth), jnp.bfloat16)
    return pl.pallas_call(
        turn_body,
        in_specs=[whole()] * 8,
        out_specs=[whole()] * 6,
        out_shape=[
            low,
            low,
            low,
            jax.ShapeDtypeStruct((rows, depth), jnp.float32),
            low,
            jax.ShapeDtypeStruct((4, width), jnp.float32),
        ],
        compiler_params=params(),
        cost_estimate=cost(4 * rows * depth * depth, 5 << 20),
        name="turn",
    )(hidden, own, recv, gain[None], shift[None], w_colbert, pick, cot)


def gelu_with_slope(values):
    cdf = 0.5 * (1.0 + lax.erf(values * 0.7071067811865476))
    density = jnp.exp(-0.5 * values * values) * 0.3989422804014327
    return values * cdf, cdf + values * density


def local_by_head(
    tokens,
    w_query,
    w_key,
    w_value,
    w_out,
    gain_attn,
    shift_attn,
    w_up,
    w_down,
    gain_ffn,
    shift_ffn,
    w_colbert,
    query_vecs,
    match_index,
    passage_of,
    cot_act,
    cot_scores,
):
    pass_count = lax.axis_size("pass")
    qry_count = lax.axis_size("qry")
    pass_index = lax.axis_index("pass")
    qry_index = lax.axis_index("qry")
    chips = pass_count // 2
    own_rows = tokens.shape[0]
    block_rows = own_rows * qry_count
    same_core = [[index for index in range(pass_count) if index % 2 == core] for core in (0, 1)]
    ring = [[2 * chip + core for chip in ring_chips(chips) for core in (0, 1)]]
    parity = pass_index % 2
    own_id = passage_of[pass_index]

    def swap(value):
        return swap_over(value, "qry", 1)

    def sibling(value):
        return swap_over(value, "pass", 1)

    def to_heads(value):
        return lax.all_to_all(
            value, "pass", 0, 0, axis_index_groups=same_core, tiled=True
        )

    def after(value, *others):
        return lax.optimization_barrier((value,) + others)[0]

    def together(*values):
        return lax.optimization_barrier(values)

    tokens_other = swap(tokens)
    gathered = jnp.concatenate([tokens, tokens_other], axis=0)
    block_ids = passage_of.astype(jnp.int32)
    same = block_ids[:, None] == block_ids[None, :]
    starts = jnp.sum((block_ids[None, :] < block_ids[:, None]).astype(jnp.int32), axis=1)
    counts = jnp.sum(same.astype(jnp.int32), axis=1)
    chip = (pass_index // 2).astype(jnp.int32)
    bits = chips.bit_length() - 1
    info = jnp.concatenate(
        [starts, counts, parity[None].astype(jnp.int32)]
        + [((chip >> bit) & 1)[None] for bit in range(bits)]
    )
    first_bit = 2 * pass_count + 1

    seq_count = match_index.shape[1]
    query_rows = cot_scores.shape[0]
    pick_col = jnp.arange(seq_count, dtype=jnp.int32) == own_id
    span_count = jnp.sum((passage_of == own_id).astype(jnp.int32))
    first_index = jnp.sum((passage_of < own_id).astype(jnp.int32))
    raw_pick = jnp.sum(jnp.where(pick_col[None, :], match_index, 0), axis=1)
    local_row = raw_pick % (span_count * block_rows) - (pass_index - first_index) * block_rows
    inside = (local_row >= 0) & (local_row < block_rows)
    local_row = jnp.where(inside, (local_row + qry_index * own_rows) % block_rows, -1)
    one_hot = (local_row[:, None] == jnp.arange(block_rows, dtype=jnp.int32)[None, :]).astype(
        jnp.bfloat16
    )
    cot_pick = jnp.sum(jnp.where(pick_col[None, :], cot_scores, 0.0), axis=1)
    token_weight = jnp.repeat(cot_pick, query_vecs.shape[0] // query_rows)
    query_float = query_vecs.astype(jnp.float32)
    weighted_queries = (token_weight[:, None] * query_float).astype(jnp.bfloat16)
    unit_grad_part = contract_rows(one_hot, weighted_queries)
    turned_part = jnp.concatenate([unit_grad_part[own_rows:], unit_grad_part[:own_rows]], axis=0)
    unit_grad_send = turned_part.astype(jnp.bfloat16)

    own_send = project(gathered, w_query, w_key, w_value)
    own_pack = to_heads(own_send)
    piece = w_out.shape[0] // 2
    w_out_send = lax.dynamic_slice_in_dim(w_out, parity * piece, piece, axis=0)
    w_out_mine = swap(after(w_out_send, own_send))
    w_out_sib = sibling(w_out_mine)
    own_pack, unit_grad_send, w_out_sib = together(own_pack, unit_grad_send, w_out_sib)
    sib_pack = sibling(own_pack)
    unit_grad_recv = swap(unit_grad_send)
    cot_other = swap(after(cot_act, unit_grad_send))
    ctx_pack, ctx_turned, lse = attend(info, own_pack, sib_pack)
    unit_grad = unit_grad_part.astype(jnp.bfloat16).astype(jnp.float32) + unit_grad_recv.astype(
        jnp.float32
    )
    unit_grad_own, unit_grad_other = unit_grad[:own_rows], unit_grad[own_rows:]
    ctx_recv = to_heads(ctx_pack)
    ready = prepare(info, after(own_pack, ctx_pack), sib_pack)
    ctx_recv, unit_grad_own, unit_grad_other, cot_other, kv, key_turned, query = together(
        ctx_recv, unit_grad_own, unit_grad_other, cot_other, *ready
    )
    tokens_all = lax.all_gather(
        after(gathered, ctx_recv), "pass", axis=0, axis_index_groups=ring, tiled=True
    )
    (
        context_low,
        hidden,
        hidden_far,
        hidden_low,
        hidden_other,
        unit_attn,
        unit_attn_far,
        inverse_attn,
        inverse_attn_far,
    ) = out_norm(
        info,
        ctx_recv,
        swap(ctx_recv),
        w_out,
        w_out_mine,
        w_out_sib,
        gathered,
        gain_attn,
        shift_attn,
    )

    def activate(rows):
        gated, slope = gelu_with_slope(dot_nn(rows, w_up))
        return lax.optimization_barrier((gated.astype(jnp.bfloat16), slope))

    gated_other, slope_other = activate(hidden_other)
    gated_own, slope_own = activate(hidden_low)

    def both_halves(rows_own, rows_other, product):
        part_other = product(rows_other).astype(jnp.bfloat16)
        part_own = product(after(rows_own, part_other)).astype(jnp.bfloat16)
        recv_own = swap(part_other)
        recv_other = swap(part_own)
        return part_own, part_other, recv_own, recv_other

    part_own, part_other, recv_own, recv_other = both_halves(
        gated_own, gated_other, lambda rows: dot_nn(rows, w_down)
    )
    local_width = w_query.shape[1]
    width = w_up.shape[1]
    model = tokens.shape[1]

    def turned(rows, part, recv, pick, cot):
        return turn(
            rows, part, recv, gain_ffn, shift_ffn, w_colbert, pick, cot, local_width
        )

    output_low, unit_own, proj_own, pre_grad, pre_low, sums_ffn = turned(
        hidden, part_own, recv_own, unit_grad_own, cot_act
    )
    inner_own = (dot_nt(pre_low, w_down) * slope_own).astype(jnp.bfloat16)
    recv_other, inner_own = together(recv_other, inner_own)
    output_other, unit_other, proj_other, pre_far, pre_other, _ = turned(
        hidden_far, part_other, recv_other, unit_grad_other, cot_other
    )
    inner_other = (dot_nt(pre_other, w_down) * slope_other).astype(jnp.bfloat16)
    part_own, part_other, recv_own, recv_other = both_halves(
        inner_own, inner_other, lambda rows: dot_nt(rows, w_up)
    )
    late = late_grad(
        qry_index[None].astype(jnp.int32),
        chips,
        (
            (hidden_low, hidden_other, after(inner_own, part_own), inner_other, True),
            (pre_low, pre_other, gated_own, gated_other, True),
            (output_low, output_other, proj_own, proj_other, False),
        ),
    )
    recv_own, recv_other, late = together(recv_own, recv_other, late)
    late_sums = lax.psum_scatter(
        late, "pass", scatter_dimension=0, axis_index_groups=ring, tiled=True
    )

    def back_to_attn(pre, part, recv, unit, inverse):
        return attn_norm_back(pre, part, recv, gain_attn, unit, inverse, local_width)

    attn_pre, attn_low, sums_attn = back_to_attn(
        pre_grad, part_own, recv_own, unit_attn, inverse_attn
    )
    _, attn_other, _ = back_to_attn(
        pre_far, part_other, recv_other, unit_attn_far, inverse_attn_far
    )

    dctx_send = ctx_grad_packed(attn_low, attn_other, w_out)
    own_dctx = to_heads(dctx_send)
    out_mine, out_send = out_grad_pack(
        info, chips, after(attn_low, dctx_send), attn_other, context_low
    )
    own_dctx, out_mine, out_send = together(own_dctx, out_mine, out_send)
    mine, other, dq = attend_back(info, kv, key_turned, query, own_dctx, ctx_turned, lse)
    back_send = combine(mine, sibling(other), dq)
    back = to_heads(back_send)
    back_own, out_send, unit_other = together(back_send, out_send, unit_other)

    out_keep, out_send = halve(info, first_bit, out_mine, sibling(out_send))
    out_came = swap_over(out_send, "pass", 2)
    unit_other = after(unit_other, out_send)
    picked = dot_nn(one_hot, jnp.concatenate([unit_own, unit_other], axis=0))
    per_query = jnp.sum((query_float * picked).reshape(query_rows, -1), axis=1)
    score_block = per_query[:, None] * pick_col.astype(jnp.float32)[None, :]
    score_part = lax.dynamic_update_slice(
        jnp.zeros((query_rows * qry_count, seq_count), jnp.float32),
        score_block,
        (qry_index * query_rows, jnp.zeros((), jnp.int32)),
    )
    score_rows = jnp.pad(score_part.reshape(1, -1), ((0, 7), (0, local_width - score_part.size)))
    small = jnp.concatenate([sums_attn, sums_ffn, score_rows], axis=0)
    small = small + swap(small)
    small = small + sibling(small)
    head_grads = head_grad(info, tokens_all, back_own, sibling(back_own))
    back, head_grads, small = together(back, head_grads, small)
    head_recv = to_heads(head_grads)
    token_own, token_send = token_grad(back, w_query, w_key, w_value)
    token_recv = swap(token_send)
    late_sums = after(late_sums, token_recv)
    colbert_all = lax.all_gather(
        late_sums[:, 2 * width :], "pass", axis=0, axis_index_groups=ring, tiled=True
    )
    out_keep = after(out_keep, token_recv)
    for step in range(1, bits):
        out_keep, out_send = halve(info, first_bit + step, out_keep, out_came)
        out_came = swap_over(out_send, "pass", 2 << step)
    for step in range(bits):
        small = small + swap_over(small, "pass", 2 << step)
    grad_out = out_sum(out_keep, out_came, local_width)
    grad_tokens = attn_pre + token_own + token_recv.astype(jnp.float32)
    grad_query, grad_key, grad_value = split_heads(after(head_recv, token_recv))
    grad_up = late_sums[:, :width].astype(jnp.float32)
    grad_down = late_sums[:, width : 2 * width].astype(jnp.float32).T
    grad_colbert = widen(after(colbert_all, grad_up, grad_down, grad_out))
    norms = small[:8].reshape(4, model)
    scores = small[8].reshape(-1)[: score_part.size].reshape(score_part.shape)
    return (
        output_low,
        scores,
        grad_tokens,
        grad_query,
        grad_key,
        grad_value,
        grad_out,
        grad_up,
        grad_down,
        grad_colbert,
        norms[0],
        norms[1],
        norms[2],
        norms[3],
    )


def solution(mesh):
    by_head = mesh.shape["qry"] == 2
    return jax.shard_map(
        local_by_head if by_head else local_general,
        mesh=mesh,
        in_specs=(
            P(("pass", "qry"), None),
            P(None, "qry"),
            P(None, "qry"),
            P(None, "qry"),
            P("qry", None),
            P(),
            P(),
            P(None, "qry"),
            P("qry", None),
            P(),
            P(),
            P(),
            P("qry", None),
            P("qry", None),
            P(),
            P(("pass", "qry"), None),
            P("qry", None),
        ),
        out_specs=(
            P(("pass", "qry"), None),
            P(),
            P(("pass", "qry"), None),
            P("pass", "qry"),
            P("pass", "qry"),
            P("pass", "qry"),
            P("qry", "pass"),
            P("pass", "qry"),
            P("qry", "pass"),
            P(),
            P(),
            P(),
            P(),
            P(),
        ),
        check_vma=False,
    )
```

```python
import functools
import math

import jax
import jax.numpy as jnp
from jax import lax
from jax.experimental import pallas as pl
from jax.experimental.pallas import tpu as pltpu
from jax.sharding import PartitionSpec as P

HD = 64
SPAN = 8
LANES = 128
VMEM_LIMIT = 24 << 20
WIDE_LIMIT = 55 << 20
LOG2E = math.log2(math.e)


def passed_along(value, axis, steps):
    count = lax.axis_size(axis)
    first, last = (max(0, -steps), min(count, count - steps))
    return lax.ppermute(value, axis, [(source, source + steps) for source in range(first, last)])


def layer_norm(values, gain, shift):
    row_mean = jnp.mean(values, axis=-1, keepdims=True)
    centred = values - row_mean
    variance = jnp.mean(centred * centred, axis=-1, keepdims=True)
    return centred * lax.rsqrt(variance + 1e-05) * gain + shift


def gelu_exact(values):
    return 0.5 * values * (1.0 + jax.scipy.special.erf(values * 0.7071067811865476))


def normalize_rows(proj_rows):
    return proj_rows * lax.rsqrt(jnp.sum(proj_rows * proj_rows, axis=1, keepdims=True) + 1e-06)


def head_split(array):
    return array.reshape(array.shape[0], array.shape[1] // HD, HD)


def block_scores(queries, key_rows):
    return jnp.einsum("qhd,khd->hqk", queries, key_rows, preferred_element_type=jnp.float32) * 0.125


def grad_block(queries, ctx_grad, log_total, row_delta, key_rows, value_rows):
    scaled = block_scores(queries, key_rows)
    probs = jnp.exp(scaled - log_total[:, :, None])
    dprob = jnp.einsum("qhd,khd->hqk", ctx_grad, value_rows, preferred_element_type=jnp.float32)
    dscore = (0.125 * probs * (dprob - row_delta[:, :, None])).astype(jnp.bfloat16)
    dquery = jnp.einsum("hqk,khd->qhd", dscore, key_rows, preferred_element_type=jnp.float32)
    dkey = jnp.einsum("hqk,qhd->khd", dscore, queries, preferred_element_type=jnp.float32)
    dvalue = jnp.einsum(
        "hqk,qhd->khd", probs.astype(jnp.bfloat16), ctx_grad, preferred_element_type=jnp.float32
    )
    return (dquery, jnp.stack([dkey, dvalue]))


def contract_rows(left, right):
    return lax.dot_general(
        left, right, (((0,), (0,)), ((), ())), preferred_element_type=jnp.float32
    )


def contract_cols(left, right):
    return lax.dot_general(
        left, right, (((1,), (1,)), ((), ())), preferred_element_type=jnp.float32
    )


def local_general(
    tokens,
    w_query,
    w_key,
    w_value,
    w_out,
    gain_attn,
    shift_attn,
    w_up,
    w_down,
    gain_ffn,
    shift_ffn,
    w_colbert,
    query_vecs,
    match_index,
    passage_of,
    cot_act,
    cot_scores,
):
    pass_count = lax.axis_size("pass")
    qry_count = lax.axis_size("qry")
    pass_index = lax.axis_index("pass")
    qry_index = lax.axis_index("qry")
    own_id = passage_of[pass_index]

    def source_valid(offset):
        source = pass_index - offset
        inside = (source >= 0) & (source < pass_count)
        return inside & (passage_of[jnp.clip(source, 0, pass_count - 1)] == own_id)

    gathered = lax.all_gather(tokens, "qry", axis=0, tiled=True)
    block_rows = gathered.shape[0]
    local_width = w_query.shape[1]
    w_qkv = jnp.concatenate([w_query, w_key, w_value], axis=1)
    qkv_rows = jnp.dot(gathered, w_qkv, preferred_element_type=jnp.float32).astype(jnp.bfloat16)
    query_flat = qkv_rows[:, :local_width]
    key_flat = qkv_rows[:, local_width : 2 * local_width]
    value_flat = qkv_rows[:, 2 * local_width :]
    queries = head_split(query_flat)
    heads = queries.shape[1]
    own_pair = jnp.stack([key_flat, value_flat])
    offsets = [distance for distance in range(1, SPAN)] + [-distance for distance in range(1, SPAN)]

    def fetch_keys():
        received = []
        for offset in offsets:
            received.append(passed_along(own_pair, "pass", offset))
        return received

    remote = fetch_keys()

    def stat_of(kv_pair):
        return jax.nn.logsumexp(block_scores(queries, head_split(kv_pair[0])), axis=2)

    log_total = stat_of(own_pair)
    for offset, kv_pair in zip(offsets, remote):
        log_total = lax.cond(
            source_valid(offset),
            lambda current, kv_pair=kv_pair: jnp.logaddexp(current, stat_of(kv_pair)),
            lambda current: current,
            log_total,
        )

    def weighted(kv_pair):
        probs = jnp.exp(
            block_scores(queries, head_split(kv_pair[0])) - log_total[:, :, None]
        ).astype(jnp.bfloat16)
        return jnp.einsum(
            "hqk,khd->qhd", probs, head_split(kv_pair[1]), preferred_element_type=jnp.float32
        )

    context = weighted(own_pair)
    for offset, kv_pair in zip(offsets, remote):
        context = lax.cond(
            source_valid(offset),
            lambda running, kv_pair=kv_pair: running + weighted(kv_pair),
            lambda running: running,
            context,
        )
    context_low = context.reshape(block_rows, local_width).astype(jnp.bfloat16)
    piece_rows = context_low
    attn_rows = lax.psum_scatter(
        jnp.dot(piece_rows, w_out, preferred_element_type=jnp.float32).astype(jnp.bfloat16),
        "qry",
        scatter_dimension=0,
        tiled=True,
    ).astype(jnp.float32)
    hidden, norm_attn_back = jax.vjp(
        layer_norm, tokens.astype(jnp.float32) + attn_rows, gain_attn, shift_attn
    )
    hidden_all = lax.all_gather(hidden.astype(jnp.bfloat16), "qry", axis=0, tiled=True)
    inner_pre = jnp.dot(hidden_all, w_up, preferred_element_type=jnp.float32)
    gated_float, gelu_back = jax.vjp(gelu_exact, inner_pre)
    gated_low = gated_float.astype(jnp.bfloat16)
    piece_rows = gated_low
    ffn_rows = lax.psum_scatter(
        jnp.dot(piece_rows, w_down, preferred_element_type=jnp.float32).astype(jnp.bfloat16),
        "qry",
        scatter_dimension=0,
        tiled=True,
    ).astype(jnp.float32)
    output, norm_ffn_back = jax.vjp(layer_norm, hidden + ffn_rows, gain_ffn, shift_ffn)
    output_low = output.astype(jnp.bfloat16)
    proj_rows = jnp.dot(output_low, w_colbert, preferred_element_type=jnp.float32)
    unit_vecs, unit_back = jax.vjp(normalize_rows, proj_rows)
    unit_all = lax.all_gather(unit_vecs.astype(jnp.bfloat16), "qry", axis=0, tiled=True)
    seq_count = match_index.shape[1]
    query_rows = cot_scores.shape[0]
    numbers = jnp.arange(seq_count, dtype=jnp.int32)
    pick_col = numbers == own_id
    span_count = jnp.sum((passage_of == own_id).astype(jnp.int32))
    first_index = jnp.sum((passage_of < own_id).astype(jnp.int32))
    length = span_count * block_rows
    raw_pick = jnp.sum(jnp.where(pick_col[None, :], match_index, 0), axis=1)
    local_row = raw_pick % length - (pass_index - first_index) * block_rows
    one_hot = (local_row[:, None] == jnp.arange(block_rows, dtype=jnp.int32)[None, :]).astype(
        jnp.bfloat16
    )
    picked = jnp.dot(one_hot, unit_all, preferred_element_type=jnp.float32)
    query_float = query_vecs.astype(jnp.float32)
    match_vals = jnp.sum(query_float * picked, axis=1)
    per_query = jnp.sum(match_vals.reshape(query_rows, -1), axis=1)
    score_block = per_query[:, None] * pick_col.astype(jnp.float32)[None, :]
    score_part = lax.dynamic_update_slice(
        jnp.zeros((query_rows * qry_count, seq_count), jnp.float32),
        score_block,
        (qry_index * query_rows, jnp.zeros((), jnp.int32)),
    )
    cot_pick = jnp.sum(jnp.where(pick_col[None, :], cot_scores, 0.0), axis=1)
    token_weight = jnp.repeat(cot_pick, query_vecs.shape[0] // query_rows)
    weighted_queries = (token_weight[:, None] * query_float).astype(jnp.bfloat16)
    piece_rows = one_hot
    unit_grad = lax.psum_scatter(
        contract_rows(piece_rows, weighted_queries).astype(jnp.bfloat16),
        "qry",
        scatter_dimension=0,
        tiled=True,
    ).astype(jnp.float32)
    (proj_grad,) = unit_back(unit_grad)
    proj_low = proj_grad.astype(jnp.bfloat16)
    grad_colbert = contract_rows(output_low, proj_low)
    out_grad = cot_act.astype(jnp.float32) + contract_cols(proj_low, w_colbert)
    pre_grad, grad_gain_ffn, grad_shift_ffn = norm_ffn_back(out_grad)
    ffn_all = lax.all_gather(pre_grad.astype(jnp.bfloat16), "qry", axis=0, tiled=True)
    gated_grad = contract_cols(ffn_all, w_down)
    grad_down = contract_rows(gated_low, ffn_all)
    (inner_grad,) = gelu_back(gated_grad)
    inner_low = inner_grad.astype(jnp.bfloat16)
    grad_up = contract_rows(hidden_all, inner_low)
    piece_rows = inner_low
    hidden_grad = pre_grad + lax.psum_scatter(
        contract_cols(piece_rows, w_up).astype(jnp.bfloat16), "qry", scatter_dimension=0, tiled=True
    ).astype(jnp.float32)
    attn_pre_grad, grad_gain_attn, grad_shift_attn = norm_attn_back(hidden_grad)
    attn_all = lax.all_gather(attn_pre_grad.astype(jnp.bfloat16), "qry", axis=0, tiled=True)
    grad_out = contract_rows(context_low, attn_all)
    ctx_grad = head_split(contract_cols(attn_all, w_out).astype(jnp.bfloat16))
    row_delta = jnp.einsum("qhd,qhd->hq", ctx_grad.astype(jnp.float32), context)
    remote_back = fetch_keys()
    dquery, dkv_own = grad_block(
        queries, ctx_grad, log_total, row_delta, head_split(key_flat), head_split(value_flat)
    )
    key_value_grad = dkv_own
    zero_query = jnp.zeros_like(dquery)
    zero_pair = jnp.zeros((2, block_rows, heads, HD), jnp.float32)
    for offset, kv_pair in zip(offsets, remote_back):
        query_part, pair_part = lax.cond(
            source_valid(offset),
            lambda incoming: grad_block(
                queries,
                ctx_grad,
                log_total,
                row_delta,
                head_split(incoming[0]),
                head_split(incoming[1]),
            ),
            lambda incoming: (zero_query, zero_pair),
            kv_pair,
        )
        dquery = dquery + query_part
        returned = passed_along(
            pair_part.reshape(2, block_rows, local_width).astype(jnp.bfloat16), "pass", -offset
        ).astype(jnp.float32)
        key_value_grad = key_value_grad + returned.reshape(2, block_rows, heads, HD)
    dqkv_low = jnp.concatenate(
        [
            dquery.reshape(block_rows, local_width),
            key_value_grad[0].reshape(block_rows, local_width),
            key_value_grad[1].reshape(block_rows, local_width),
        ],
        axis=1,
    ).astype(jnp.bfloat16)
    grad_qkv = contract_rows(gathered, dqkv_low)
    piece_rows = dqkv_low
    grad_tokens = attn_pre_grad + lax.psum_scatter(
        contract_cols(piece_rows, w_qkv).astype(jnp.bfloat16),
        "qry",
        scatter_dimension=0,
        tiled=True,
    ).astype(jnp.float32)
    summed = (
        lax.psum_scatter(
            grad_qkv[:, :local_width].astype(jnp.bfloat16), "pass", scatter_dimension=0, tiled=True
        ).astype(jnp.float32),
        lax.psum_scatter(
            grad_qkv[:, local_width : 2 * local_width].astype(jnp.bfloat16),
            "pass",
            scatter_dimension=0,
            tiled=True,
        ).astype(jnp.float32),
        lax.psum_scatter(
            grad_qkv[:, 2 * local_width :].astype(jnp.bfloat16),
            "pass",
            scatter_dimension=0,
            tiled=True,
        ).astype(jnp.float32),
        lax.psum_scatter(
            grad_out.astype(jnp.bfloat16), "pass", scatter_dimension=1, tiled=True
        ).astype(jnp.float32),
        lax.psum_scatter(
            grad_up.astype(jnp.bfloat16), "pass", scatter_dimension=0, tiled=True
        ).astype(jnp.float32),
        lax.psum_scatter(
            grad_down.astype(jnp.bfloat16), "pass", scatter_dimension=1, tiled=True
        ).astype(jnp.float32),
    )
    shared = lax.psum(
        (grad_colbert, grad_gain_attn, grad_shift_attn, grad_gain_ffn, grad_shift_ffn, score_part),
        ("pass", "qry"),
    )
    return (
        output_low,
        shared[5],
        grad_tokens,
        summed[0],
        summed[1],
        summed[2],
        summed[3],
        summed[4],
        summed[5],
        shared[0],
        shared[1],
        shared[2],
        shared[3],
        shared[4],
    )


def swap_over(value, axis, mask):
    count = lax.axis_size(axis)
    return lax.ppermute(value, axis, [(index, index ^ mask) for index in range(count)])


def ring_chips(chips):
    layers = chips // 2
    return [2 * z for z in range(layers)] + [2 * z + 1 for z in reversed(range(layers))]


def low_lanes(rows):
    return lax.broadcasted_iota(jnp.int32, (rows, LANES), 1) < HD


def split_lanes(first, second):
    low = low_lanes(first.shape[0])
    return (
        jnp.where(low, first, pltpu.roll(second, HD, 1)),
        jnp.where(low, pltpu.roll(first, HD, 1), second),
    )


def dot_nn(left, right):
    return jnp.dot(left, right, preferred_element_type=jnp.float32)


def dot_nt(left, right):
    return contract_cols(left, right)


def params(*semantics, limit=VMEM_LIMIT):
    return pltpu.CompilerParams(
        dimension_semantics=semantics or None, vmem_limit_bytes=limit
    )


def cost(flops, moved, transcendentals=0):
    return pl.CostEstimate(
        flops=int(flops), bytes_accessed=int(moved), transcendentals=int(transcendentals)
    )


def project_body(x_ref, wq_ref, wk_ref, wv_ref, out_ref):
    x = x_ref[...]
    rows = x.shape[0]
    half = rows // 2
    query = dot_nn(x, wq_ref[...])
    key = dot_nn(x, wk_ref[...])
    value = dot_nn(x, wv_ref[...])
    for pair in range(query.shape[1] // LANES):
        cols = slice(pair * LANES, (pair + 1) * LANES)
        first, second = split_lanes(key[:, cols], value[:, cols])
        out_ref[2 * pair, 0:rows] = first.astype(jnp.bfloat16)
        out_ref[2 * pair + 1, 0:rows] = second.astype(jnp.bfloat16)
        first, second = split_lanes(query[:half, cols], query[half:, cols])
        out_ref[2 * pair, rows : rows + half] = first.astype(jnp.bfloat16)
        out_ref[2 * pair + 1, rows : rows + half] = second.astype(jnp.bfloat16)


def project(x, wq, wk, wv):
    rows, depth = x.shape
    width = wq.shape[1]
    heads = width // HD
    steps = 2
    weight = pl.BlockSpec((depth, width // steps), lambda i: (0, i))
    return pl.pallas_call(
        project_body,
        grid=(steps,),
        in_specs=[pl.BlockSpec((rows, depth), lambda i: (0, 0)), weight, weight, weight],
        out_specs=pl.BlockSpec((heads // steps, rows * 3 // 2, LANES), lambda i: (i, 0, 0)),
        out_shape=jax.ShapeDtypeStruct((heads, rows * 3 // 2, LANES), jnp.bfloat16),
        compiler_params=params("arbitrary", limit=WIDE_LIMIT),
        cost_estimate=cost(2 * rows * depth * width * 3, 2 * (3 * depth * width + 4 * rows * depth)),
        name="project",
    )(x, wq, wk, wv)


def load_query(packed):
    wide = packed.astype(jnp.float32)
    low = low_lanes(wide.shape[0])
    top = jnp.where(low, wide, 0.0)
    bottom = jnp.where(low, pltpu.roll(wide, HD, 1), 0.0)
    return jnp.concatenate([top, bottom], axis=0).astype(jnp.bfloat16)


def pack_transposed(columns):
    half = columns.shape[1] // 2
    return jnp.concatenate([columns[:, :half], columns[:, half:]], axis=0).T


def square_sums(rows_low):
    group = lambda axis: lax.broadcasted_iota(jnp.int32, (LANES, LANES), axis) // HD
    ones = (group(0) == group(1)).astype(jnp.bfloat16)
    wide = rows_low.astype(jnp.float32)
    sums = dot_nn((wide * wide).astype(jnp.bfloat16), ones)
    return jnp.max(sums.reshape(sums.shape[0] // 8, 8, LANES), axis=0)


def over_blocks(first, count, step):
    for size in (8, 4, 2, 1):

        @pl.when(count & size != 0)
        def _(size=size):
            step(first + (count & ~(2 * size - 1)), size)


def load_block(near_ref, far_ref, chip, block_ref):
    half = block_ref.shape[0] // 2
    block_ref[:half] = near_ref[chip, 0:half]
    block_ref[half:] = far_ref[chip, 0:half]


def load_queries(near_ref, far_ref, chip, block_ref):
    half = block_ref.shape[0] // 2
    block_ref[:half] = load_query(near_ref[chip, half:])
    block_ref[half:] = load_query(far_ref[chip, half:])


def attend_body(
    info_ref, near_ref, far_ref, near_sib_ref, far_sib_ref, ctx_ref, ctxt_ref, lse_ref, kv_s, v1_s, q_s, total_s, score_s, top_s
):
    chips = near_ref.shape[0]
    blocks = 2 * chips
    rows = kv_s.shape[1]
    half = rows // 2
    parity = info_ref[2 * blocks]
    scale = 0.125 * LOG2E
    low = low_lanes(rows)
    key_top = query_top = jnp.zeros((8, LANES), jnp.float32)
    for chip in range(chips):
        for refs, which in (
            ((near_ref, far_ref), parity),
            ((near_sib_ref, far_sib_ref), 1 - parity),
        ):
            place = 2 * chip + which
            load_block(*refs, chip, kv_s.at[place])
            block = kv_s[place]
            v1_s[place] = jnp.where(low, 1.0, block.astype(jnp.float32)).astype(jnp.bfloat16)
            key_top = jnp.maximum(key_top, square_sums(block))
        load_queries(near_ref, far_ref, chip, q_s.at[chip])
        query_top = jnp.maximum(query_top, square_sums(q_s[chip]))
    key_top = jnp.max(jnp.where(low_lanes(8), key_top, 0.0))
    bound = jnp.max(query_top) * key_top * (1.02 * scale * scale)
    safe = bound < 3600.0

    @pl.when(safe)
    def _():
        def one_item(item, carry):
            query = q_s[item]
            total_s[item] = jnp.zeros((rows, LANES), jnp.float32)

            def step(block, n):
                keys = kv_s[pl.ds(block, n)].reshape(n * rows, LANES)
                values = v1_s[pl.ds(block, n)].reshape(n * rows, LANES)
                prob = jnp.exp2(dot_nt(query, keys) * scale).astype(jnp.bfloat16)
                total_s[item] += dot_nn(prob, values)

            place = 2 * item + parity
            over_blocks(info_ref[place], info_ref[blocks + place], step)
            top_s[item] = jnp.zeros((8, rows), jnp.float32)
            return carry

        lax.fori_loop(0, chips, one_item, 0)

    @pl.when(jnp.logical_not(safe))
    def _():
        def one_item(item, carry):
            query = q_s[item]
            place = 2 * item + parity
            first, count = info_ref[place], info_ref[blocks + place]

            def scores(step, top):
                score = dot_nt(query, kv_s[first + step]) * scale
                score_s[step] = score
                return jnp.maximum(top, score)

            top = lax.fori_loop(0, count, scores, jnp.full((rows, rows), -jnp.inf, jnp.float32))
            top = jnp.max(top, axis=1, keepdims=True)
            total_s[item] = jnp.zeros((rows, LANES), jnp.float32)

            def weigh(step, carry):
                prob = jnp.exp2(score_s[step] - top).astype(jnp.bfloat16)
                total_s[item] += dot_nn(prob, v1_s[first + step])
                return carry

            lax.fori_loop(0, count, weigh, 0)
            top_s[item] = jnp.broadcast_to(top, (rows, LANES)).T[0:8]
            return carry

        lax.fori_loop(0, chips, one_item, 0)

    narrow = low_lanes(half)
    for item in range(chips):
        total = total_s[item]
        turned = total.T
        weight = turned[0:8]
        lse_ref[item] = top_s[item] + jnp.log2(weight)
        ctxt_ref[item] = turned[HD:] / weight[0:1]
        inverse = 1.0 / jnp.where(low, total, 1.0)
        context = total * pltpu.roll(inverse, HD, 1)
        ctx_ref[item] = jnp.where(
            narrow, pltpu.roll(context[:half], HD, 1), context[half:]
        ).astype(jnp.bfloat16)


def whole():
    return pl.BlockSpec(memory_space=pltpu.VMEM)


def attend(info, *packs):
    chips, packed, _ = packs[0].shape
    rows = packed * 4 // 3
    blocks = 2 * chips
    return pl.pallas_call(
        attend_body,
        in_specs=[pl.BlockSpec(memory_space=pltpu.SMEM)] + [whole()] * 4,
        out_specs=[whole()] * 3,
        out_shape=[
            jax.ShapeDtypeStruct((chips, rows // 2, LANES), jnp.bfloat16),
            jax.ShapeDtypeStruct((chips, HD, rows), jnp.float32),
            jax.ShapeDtypeStruct((chips, 8, rows), jnp.float32),
        ],
        scratch_shapes=[
            pltpu.VMEM((blocks, rows, LANES), jnp.bfloat16),
            pltpu.VMEM((blocks, rows, LANES), jnp.bfloat16),
            pltpu.VMEM((chips, rows, LANES), jnp.bfloat16),
            pltpu.VMEM((chips, rows, LANES), jnp.float32),
            pltpu.VMEM((SPAN, rows, rows), jnp.float32),
            pltpu.VMEM((chips, 8, rows), jnp.float32),
        ],
        compiler_params=params(limit=WIDE_LIMIT),
        cost_estimate=cost(2 * 2 * 40 * rows * rows * LANES, 4 << 20, 40 * rows * rows),
        name="attend",
    )(info, *packs)


def prepare_body(info_ref, near_ref, far_ref, near_sib_ref, far_sib_ref, kv_ref, kt_ref, q_ref):
    chips = near_ref.shape[0]
    parity = info_ref[4 * chips]
    for chip in range(chips):
        for refs, which in (
            ((near_ref, far_ref), parity),
            ((near_sib_ref, far_sib_ref), 1 - parity),
        ):
            place = 2 * chip + which
            load_block(*refs, chip, kv_ref.at[place])
            kt_ref[place] = kv_ref[place].astype(jnp.float32).T[:HD].astype(jnp.bfloat16)
        load_queries(near_ref, far_ref, chip, q_ref.at[chip])


def prepare(info, *packs):
    chips, packed, _ = packs[0].shape
    rows = packed * 4 // 3
    return pl.pallas_call(
        prepare_body,
        in_specs=[pl.BlockSpec(memory_space=pltpu.SMEM)] + [whole()] * 4,
        out_specs=[whole()] * 3,
        out_shape=[
            jax.ShapeDtypeStruct((2 * chips, rows, LANES), jnp.bfloat16),
            jax.ShapeDtypeStruct((2 * chips, HD, rows), jnp.bfloat16),
            jax.ShapeDtypeStruct((chips, rows, LANES), jnp.bfloat16),
        ],
        compiler_params=params(),
        cost_estimate=cost(1 << 20, 4 << 20),
        name="prepare",
    )(info, *packs)


def attend_back_body(
    info_ref,
    kv_ref,
    kt_ref,
    q_ref,
    dctx_ref,
    ctxt_ref,
    lse_ref,
    mine_ref,
    other_ref,
    dq_ref,
    acc_s,
    both_s,
    delta_s,
    total_s,
):
    chips = q_ref.shape[0]
    blocks = 2 * chips
    rows = kv_ref.shape[1]
    half = rows // 2
    parity = info_ref[2 * blocks]
    scale = 0.125 * LOG2E
    low = low_lanes(half)
    for item in range(chips):
        packed = dctx_ref[item].astype(jnp.float32)
        both_s[item, :rows] = q_ref[item]
        both_s[item, rows : rows + half] = jnp.where(
            low, 0.0, pltpu.roll(packed, HD, 1)
        ).astype(jnp.bfloat16)
        both_s[item, rows + half :] = jnp.where(low, 0.0, packed).astype(jnp.bfloat16)
        turned = packed.T
        turned = jnp.concatenate([turned[:HD], turned[HD:]], axis=1)
        delta = jnp.sum(turned * ctxt_ref[item], axis=0, keepdims=True)
        delta_s[item] = jnp.broadcast_to(delta, (8, rows))
        acc_s[2 * item] = jnp.zeros((rows, LANES), jnp.float32)
        acc_s[2 * item + 1] = jnp.zeros((rows, LANES), jnp.float32)
        total_s[item] = jnp.zeros((HD, rows), jnp.float32)

    def one_item(item, carry):
        query = both_s[item, :rows]
        dctx = both_s[item, rows:]
        delta = delta_s[item, 0:1]
        lse = lse_ref[item, 0:1]

        def step(block, n):
            kv = kv_ref[pl.ds(block, n)].reshape(n * rows, LANES)
            prob = jnp.exp2(dot_nt(kv, query) * scale - lse)
            dscore = (prob * (dot_nt(kv, dctx) - delta)).astype(jnp.bfloat16)
            pair = jnp.concatenate([dscore, prob.astype(jnp.bfloat16)], axis=1)
            acc_s[pl.ds(block, n)] += dot_nn(pair, both_s[item]).reshape(n, rows, LANES)
            total = total_s[item]
            for part in range(n):
                total = total + dot_nn(kt_ref[block + part], dscore[part * rows : (part + 1) * rows])
            total_s[item] = total

        place = 2 * item + parity
        over_blocks(info_ref[place], info_ref[blocks + place], step)
        return carry

    lax.fori_loop(0, chips, one_item, 0)
    key_scale = jnp.where(low_lanes(rows), 0.125, 1.0)
    for item in range(chips):
        dq_ref[item] = pack_transposed(total_s[item] * 0.125).astype(jnp.bfloat16)
        mine_ref[item] = (acc_s[2 * item + parity] * key_scale).astype(jnp.bfloat16)
        other_ref[item] = (acc_s[2 * item + 1 - parity] * key_scale).astype(jnp.bfloat16)


def attend_back(info, kv, kt, query, dctx, ctxt, lse):
    chips, rows, _ = query.shape
    blocks = 2 * chips
    share = jax.ShapeDtypeStruct((chips, rows, LANES), jnp.bfloat16)
    return pl.pallas_call(
        attend_back_body,
        in_specs=[pl.BlockSpec(memory_space=pltpu.SMEM)] + [whole()] * 6,
        out_specs=[whole()] * 3,
        out_shape=[share, share, jax.ShapeDtypeStruct((chips, rows // 2, LANES), jnp.bfloat16)],
        scratch_shapes=[
            pltpu.VMEM((blocks, rows, LANES), jnp.float32),
            pltpu.VMEM((chips, 2 * rows, LANES), jnp.bfloat16),
            pltpu.VMEM((chips, 8, rows), jnp.float32),
            pltpu.VMEM((chips, HD, rows), jnp.float32),
        ],
        compiler_params=params(limit=WIDE_LIMIT),
        cost_estimate=cost(2 * 5 * 40 * rows * rows * LANES, 5 << 20, 40 * rows * rows),
        name="attend_back",
    )(info, kv, kt, query, dctx, ctxt, lse)


def combine_body(mine_ref, sib_ref, dq_ref, out_ref):
    chips, rows, _ = mine_ref.shape
    for chip in range(chips):
        total = mine_ref[chip].astype(jnp.float32) + sib_ref[chip].astype(jnp.float32)
        out_ref[chip, 0:rows] = total.astype(jnp.bfloat16)
        out_ref[chip, rows:] = dq_ref[chip]


def combine(mine, sib, dq):
    chips, rows, _ = mine.shape
    return pl.pallas_call(
        combine_body,
        in_specs=[whole()] * 3,
        out_specs=whole(),
        out_shape=jax.ShapeDtypeStruct((chips, rows * 3 // 2, LANES), jnp.bfloat16),
        compiler_params=params(),
        cost_estimate=cost(1 << 20, 2 << 20),
        name="combine",
    )(mine, sib, dq)


def out_norm_body(
    info_ref,
    in_ref,
    other_ref,
    w_ref,
    w_mine_ref,
    w_sib_ref,
    tok_ref,
    gain_ref,
    shift_ref,
    ctx_ref,
    *outs,
):
    *outs, far_s = outs
    heads, half, _ = in_ref.shape
    parity = info_ref[2 * 2 * in_ref.shape[0]]
    for pair in range(heads // 2):
        cols = slice(pair * LANES, (pair + 1) * LANES)
        top, bottom = split_lanes(
            in_ref[2 * pair].astype(jnp.float32), in_ref[2 * pair + 1].astype(jnp.float32)
        )
        ctx_ref[0:half, cols] = top.astype(jnp.bfloat16)
        ctx_ref[half:, cols] = bottom.astype(jnp.bfloat16)
        top, bottom = split_lanes(
            other_ref[2 * pair].astype(jnp.float32), other_ref[2 * pair + 1].astype(jnp.float32)
        )
        far_s[0:half, cols] = bottom.astype(jnp.bfloat16)
        far_s[half:, cols] = top.astype(jnp.bfloat16)
    first = parity == 0
    mine, sib = w_mine_ref[...], w_sib_ref[...]
    w_far = jnp.concatenate([jnp.where(first, mine, sib), jnp.where(first, sib, mine)], axis=0)
    rows = dot_nn(ctx_ref[...], w_ref[...]) + dot_nn(far_s[...], w_far)
    unit, inverse = norm_rows(tok_ref[...].astype(jnp.float32) + rows)
    hidden = unit * gain_ref[...] + shift_ref[...]
    inverse = jnp.broadcast_to(inverse, (2 * half, LANES))
    for index, value in enumerate((hidden, hidden.astype(jnp.bfloat16), unit, inverse)):
        outs[2 * index][...] = value[:half]
        outs[2 * index + 1][...] = value[half:]


def out_norm(info, packed, packed_other, w_out, w_mine, w_sib, tokens, gain, shift):
    heads, half, _ = packed.shape
    width, depth = w_out.shape
    wide = jax.ShapeDtypeStruct((half, depth), jnp.float32)
    low = jax.ShapeDtypeStruct((half, depth), jnp.bfloat16)
    narrow = jax.ShapeDtypeStruct((half, LANES), jnp.float32)
    return pl.pallas_call(
        out_norm_body,
        in_specs=[pl.BlockSpec(memory_space=pltpu.SMEM)] + [whole()] * 8,
        out_specs=[whole()] * 9,
        out_shape=[jax.ShapeDtypeStruct((2 * half, width), jnp.bfloat16)]
        + [wide, wide, low, low, wide, wide, narrow, narrow],
        scratch_shapes=[pltpu.VMEM((2 * half, width), jnp.bfloat16)],
        compiler_params=params(),
        cost_estimate=cost(8 * half * width * depth, 5 << 20),
        name="out_norm",
    )(info, packed, packed_other, w_out, w_mine, w_sib, tokens, gain[None], shift[None])


def ctx_grad_body(own_ref, other_ref, w_ref, out_ref):
    half = out_ref.shape[1]
    grad = dot_nt(jnp.concatenate([own_ref[...], other_ref[...]], axis=0), w_ref[...])
    for pair in range(grad.shape[1] // LANES):
        cols = slice(pair * LANES, (pair + 1) * LANES)
        first, second = split_lanes(grad[:half, cols], grad[half:, cols])
        out_ref[2 * pair] = first.astype(jnp.bfloat16)
        out_ref[2 * pair + 1] = second.astype(jnp.bfloat16)


def ctx_grad_packed(grad_own, grad_other, w_out):
    rows, depth = 2 * grad_own.shape[0], grad_own.shape[1]
    width = w_out.shape[0]
    return pl.pallas_call(
        ctx_grad_body,
        in_specs=[whole()] * 3,
        out_specs=whole(),
        out_shape=jax.ShapeDtypeStruct((width // HD, rows // 2, LANES), jnp.bfloat16),
        compiler_params=params(),
        cost_estimate=cost(2 * rows * width * depth, 2 << 20),
        name="ctx_grad",
    )(grad_own, grad_other, w_out)


def head_grad_body(info_ref, tok_ref, own_ref, sib_ref, out_ref, acc_s, grad_s):
    step = pl.program_id(0)
    steps = pl.num_programs(0)
    chips, packed, _ = own_ref.shape
    blocks = 2 * chips
    rows = packed * 2 // 3
    parity = info_ref[2 * blocks]
    group = chips // steps
    columns = []
    for index in range(group):
        place = step * group + index
        chip = jnp.where(place < chips // 2, 2 * place, 2 * chips - 1 - 2 * place)
        own, sib = own_ref[chip].astype(jnp.float32), sib_ref[chip].astype(jnp.float32)
        for core in range(2):
            block = jnp.where(parity == core, own, sib)
            dq = block[rows:].T
            dq = jnp.concatenate([dq[:HD], dq[HD:]], axis=1)
            columns.append(jnp.concatenate([block[:rows].T, dq], axis=0).astype(jnp.bfloat16))
    part = dot_nn(jnp.concatenate(columns, axis=1), tok_ref[...])

    @pl.when(step == 0)
    def _():
        acc_s[...] = part

    @pl.when(step > 0)
    def _():
        acc_s[...] += part

    @pl.when(step == steps - 1)
    def _():
        grad = acc_s[...]
        depth = grad.shape[1] // blocks
        wide = jnp.concatenate([grad, grad[2 * HD :]], axis=0)
        grad_s[...] = wide.T.reshape(blocks, depth, 2 * LANES)

        def pack(index, carry):
            part = grad_s[2 * index + parity]
            out_ref[index, 0:depth] = part[:, :LANES].astype(jnp.bfloat16)
            query = part[:, LANES:]
            mixed = jnp.where(low_lanes(depth // 2), query[: depth // 2], query[depth // 2 :])
            out_ref[index, depth : depth + depth // 2] = mixed.astype(jnp.bfloat16)
            return carry

        lax.fori_loop(0, chips, pack, 0)


def head_grad(info, tokens_all, own, sib):
    chips, packed, _ = own.shape
    blocks = 2 * chips
    rows = packed * 2 // 3
    depth = tokens_all.shape[1]
    piece = depth // blocks
    steps = 4
    full = lambda shape: pl.BlockSpec(shape, lambda i: (0,) * len(shape))
    return pl.pallas_call(
        head_grad_body,
        grid=(steps,),
        in_specs=[
            pl.BlockSpec(memory_space=pltpu.SMEM),
            pl.BlockSpec((blocks * rows // steps, depth), lambda i: (i, 0)),
            full(own.shape),
            full(sib.shape),
        ],
        out_specs=full((chips, piece + piece // 2, LANES)),
        out_shape=jax.ShapeDtypeStruct((chips, piece + piece // 2, LANES), jnp.bfloat16),
        scratch_shapes=[
            pltpu.VMEM((3 * HD, depth), jnp.float32),
            pltpu.VMEM((blocks, piece, 2 * LANES), jnp.float32),
        ],
        compiler_params=params("arbitrary", limit=2 * VMEM_LIMIT),
        cost_estimate=cost(2 * blocks * rows * depth * 3 * HD, blocks * rows * depth * 2),
        name="head_grad",
    )(info, tokens_all, own, sib)


def token_grad_body(in_ref, wq_ref, wk_ref, wv_ref, own_ref, send_ref, d_s):
    heads = in_ref.shape[0]
    rows = d_s.shape[1]
    half = rows // 2
    load = lambda head, lo, hi: in_ref[head, lo:hi].astype(jnp.float32)
    for pair in range(heads // 2):
        cols = slice(pair * LANES, (pair + 1) * LANES)
        a, b = 2 * pair, 2 * pair + 1
        key, value = split_lanes(load(a, 0, rows), load(b, 0, rows))
        d_s[1, :, cols] = key.astype(jnp.bfloat16)
        d_s[2, :, cols] = value.astype(jnp.bfloat16)
        top, bottom = split_lanes(load(a, rows, rows + half), load(b, rows, rows + half))
        d_s[0, :half, cols] = top.astype(jnp.bfloat16)
        d_s[0, half:, cols] = bottom.astype(jnp.bfloat16)
    total = dot_nt(d_s[0], wq_ref[...]) + dot_nt(d_s[1], wk_ref[...]) + dot_nt(d_s[2], wv_ref[...])
    own_ref[...] = total[:half]
    send_ref[...] = total[half:].astype(jnp.bfloat16)


def token_grad(packed, wq, wk, wv):
    depth, width = wq.shape
    rows = packed.shape[1] * 2 // 3
    return pl.pallas_call(
        token_grad_body,
        in_specs=[whole()] * 4,
        out_specs=[whole()] * 2,
        out_shape=[
            jax.ShapeDtypeStruct((rows // 2, depth), jnp.float32),
            jax.ShapeDtypeStruct((rows // 2, depth), jnp.bfloat16),
        ],
        scratch_shapes=[pltpu.VMEM((3, rows, width), jnp.bfloat16)],
        compiler_params=params(),
        cost_estimate=cost(6 * rows * depth * width, 5 << 20),
        name="token_grad",
    )(packed, wq, wk, wv)


def split_heads_body(in_ref, gq_ref, gk_ref, gv_ref):
    heads = in_ref.shape[0]
    piece = gq_ref.shape[0]
    last = piece + piece // 2
    load = lambda head, lo, hi: in_ref[head, lo:hi].astype(jnp.float32)
    for pair in range(heads // 2):
        cols = slice(pair * LANES, (pair + 1) * LANES)
        a, b = 2 * pair, 2 * pair + 1
        key, value = split_lanes(load(a, 0, piece), load(b, 0, piece))
        gk_ref[:, cols] = key
        gv_ref[:, cols] = value
        top, bottom = split_lanes(load(a, piece, last), load(b, piece, last))
        gq_ref[: piece // 2, cols] = top
        gq_ref[piece // 2 :, cols] = bottom


def split_heads(packed):
    heads, height, _ = packed.shape
    grad = jax.ShapeDtypeStruct((height * 2 // 3, heads * HD), jnp.float32)
    return pl.pallas_call(
        split_heads_body,
        in_specs=[whole()],
        out_specs=[whole()] * 3,
        out_shape=[grad] * 3,
        compiler_params=params(),
        cost_estimate=cost(1 << 18, 1 << 20),
        name="split_heads",
    )(packed)


def out_sum_body(keep_ref, came_ref, out_ref):
    piece = out_ref.shape[1]
    for tile in range(out_ref.shape[0] // LANES):
        rows = slice(tile * piece, (tile + 1) * piece)
        total = keep_ref[0, rows].astype(jnp.float32) + came_ref[0, rows].astype(jnp.float32)
        out_ref[tile * LANES : (tile + 1) * LANES] = total.T


def out_sum(keep, came, width):
    piece = keep.shape[1] * LANES // width
    return pl.pallas_call(
        out_sum_body,
        in_specs=[whole()] * 2,
        out_specs=whole(),
        out_shape=jax.ShapeDtypeStruct((width, piece), jnp.float32),
        compiler_params=params(),
        cost_estimate=cost(1 << 17, 1 << 19),
        name="out_sum",
    )(keep, came)


def late_grad_body(orders, tiles, first_ref, *refs):
    *arrays, out_ref, turned_s, tile_s, sems = refs
    tile = tile_s.shape[2]
    terms = [arrays[index : index + 4] for index in range(0, len(arrays), 4)]
    first = first_ref[0] == 0

    def ordered(own, other):
        return (jnp.where(first, own, other), jnp.where(first, other, own))

    def columns(place):
        return pl.ds(pl.multiple_of(place * tile, tile), tile)

    def copy(place):
        slot = place % 2
        return pltpu.make_async_copy(tile_s.at[slot], out_ref.at[:, columns(place)], sems.at[slot])

    start = 0
    for index, (own, other, own_right, other_right) in enumerate(terms):
        half, depth = own.shape
        size = depth // len(orders[index])
        for place, chip in enumerate(orders[index]):
            cols = slice(chip * size, (chip + 1) * size)
            rows = slice(place * size, (place + 1) * size)
            for which, piece in enumerate(ordered(own[:, cols], other[:, cols])):
                turned_s[rows, which * half : (which + 1) * half] = piece.T

        def step(number, carry, start=start, own_right=own_right, other_right=other_right):
            place = start + number
            cols = columns(number)
            right = jnp.concatenate(ordered(own_right[:, cols], other_right[:, cols]), axis=0)

            @pl.when(place >= 2)
            def _():
                copy(place - 2).wait()

            tile_s[place % 2] = dot_nn(turned_s[...], right).astype(jnp.bfloat16)
            copy(place).start()
            return carry

        lax.fori_loop(0, tiles[index], step, 0)
        start += tiles[index]
    for place in range(start - 2, start):
        copy(place).wait()


def late_grad(first, chips, terms):
    half, depth = terms[0][0].shape
    tile = 1024
    orders = [ring_chips(chips) if term[4] else list(range(chips)) for term in terms]
    arrays = [array for term in terms for array in term[:4]]
    tiles = [term[2].shape[1] // tile for term in terms]
    width = sum(tiles) * tile
    return pl.pallas_call(
        functools.partial(late_grad_body, orders, tiles),
        in_specs=[pl.BlockSpec(memory_space=pltpu.SMEM)] + [whole()] * len(arrays),
        out_specs=pl.BlockSpec(memory_space=pl.ANY),
        out_shape=jax.ShapeDtypeStruct((depth, width), jnp.bfloat16),
        scratch_shapes=[
            pltpu.VMEM((depth, 2 * half), jnp.bfloat16),
            pltpu.VMEM((2, depth, tile), jnp.bfloat16),
            pltpu.SemaphoreType.DMA((2,)),
        ],
        compiler_params=params(limit=WIDE_LIMIT),
        cost_estimate=cost(4 * half * depth * width, 2 * depth * width + (3 << 20)),
        name="late_grad",
    )(first, *arrays)


def halve_body(place, info_ref, mine_ref, came_ref, keep_ref, send_ref):
    bit = info_ref[place]
    for index in range(keep_ref.shape[0]):
        for ref, block in ((keep_ref, 2 * index + bit), (send_ref, 2 * index + 1 - bit)):
            total = mine_ref[block].astype(jnp.float32) + came_ref[block].astype(jnp.float32)
            ref[index] = total.astype(jnp.bfloat16)


def halve(info, place, mine, came):
    count, height, width = mine.shape
    share = jax.ShapeDtypeStruct((count // 2, height, width), jnp.bfloat16)
    return pl.pallas_call(
        functools.partial(halve_body, place),
        in_specs=[pl.BlockSpec(memory_space=pltpu.SMEM)] + [whole()] * 2,
        out_specs=[whole()] * 2,
        out_shape=[share] * 2,
        compiler_params=params(),
        cost_estimate=cost(1 << 18, 2 << 20),
        name="halve",
    )(info, mine, came)


def widen_body(in_ref, out_ref):
    out_ref[...] = in_ref[...].astype(jnp.float32)


def widen(values):
    rows, width = values.shape
    steps = 4
    block = pl.BlockSpec((rows // steps, width), lambda i: (i, 0))
    return pl.pallas_call(
        widen_body,
        grid=(steps,),
        in_specs=[block],
        out_specs=block,
        out_shape=jax.ShapeDtypeStruct((rows, width), jnp.float32),
        compiler_params=params("arbitrary", limit=WIDE_LIMIT),
        cost_estimate=cost(1 << 20, 6 << 20),
        name="widen",
    )(values)


def out_grad_body(info_ref, left_ref, other_ref, ctx_ref, mine_ref, send_ref, grad_s):
    blocks, piece, width = grad_s.shape
    chips = blocks // 2
    parity = info_ref[2 * blocks]
    left = jnp.concatenate([left_ref[...], other_ref[...]], axis=0)
    grad_s[...] = contract_rows(left, ctx_ref[...]).reshape(blocks, piece, width)
    for chip in range(chips):
        for ref, block in ((mine_ref, 2 * chip + parity), (send_ref, 2 * chip + 1 - parity)):
            part = grad_s[block].astype(jnp.bfloat16)
            for tile in range(width // LANES):
                cols = slice(tile * LANES, (tile + 1) * LANES)
                ref[chip, tile * piece : (tile + 1) * piece] = part[:, cols]


def out_grad_pack(info, chips, grad_own, grad_other, context_low):
    depth = grad_own.shape[1]
    rows, width = context_low.shape
    piece = depth // (2 * chips)
    height = piece * width // LANES
    share = jax.ShapeDtypeStruct((chips, height, LANES), jnp.bfloat16)
    return pl.pallas_call(
        out_grad_body,
        in_specs=[pl.BlockSpec(memory_space=pltpu.SMEM)] + [whole()] * 3,
        out_specs=[whole()] * 2,
        out_shape=[share] * 2,
        scratch_shapes=[pltpu.VMEM((2 * chips, piece, width), jnp.float32)],
        compiler_params=params(),
        cost_estimate=cost(2 * rows * depth * width, 2 << 20),
        name="out_grad",
    )(info, grad_own, grad_other, context_low)


def norm_rows(values):
    centred = values - jnp.mean(values, axis=-1, keepdims=True)
    inverse = lax.rsqrt(jnp.mean(centred * centred, axis=-1, keepdims=True) + 1e-05)
    return centred * inverse, inverse


def back_rows(grad, gain, unit, inverse):
    scaled = grad * gain
    along = jnp.mean(scaled * unit, axis=-1, keepdims=True)
    return (scaled - jnp.mean(scaled, axis=-1, keepdims=True) - unit * along) * inverse


def store_sums(ref, grad, unit):
    width = ref.shape[1]
    for index, total in enumerate((jnp.sum(grad * unit, axis=0), jnp.sum(grad, axis=0))):
        for part in range(2):
            row = 2 * index + part
            ref[row : row + 1] = total[None, part * width : (part + 1) * width]


def attn_norm_back_body(
    pre_ref, own_ref, recv_ref, gain_ref, unit_ref, inv_ref, grad_ref, low_ref, sums_ref
):
    grad = pre_ref[...] + (own_ref[...].astype(jnp.float32) + recv_ref[...].astype(jnp.float32))
    unit = unit_ref[...]
    back = back_rows(grad, gain_ref[...], unit, inv_ref[:, 0:1])
    grad_ref[...] = back
    low_ref[...] = back.astype(jnp.bfloat16)
    store_sums(sums_ref, grad, unit)


def attn_norm_back(pre, own, recv, gain, unit, inverse, width):
    rows, depth = pre.shape
    return pl.pallas_call(
        attn_norm_back_body,
        in_specs=[whole()] * 6,
        out_specs=[whole()] * 3,
        out_shape=[
            jax.ShapeDtypeStruct((rows, depth), jnp.float32),
            jax.ShapeDtypeStruct((rows, depth), jnp.bfloat16),
            jax.ShapeDtypeStruct((4, width), jnp.float32),
        ],
        compiler_params=params(),
        cost_estimate=cost(1 << 20, 2 << 20),
        name="attn_norm_back",
    )(pre, own, recv, gain[None], unit, inverse)


def turn_body(
    hid_ref,
    own_ref,
    recv_ref,
    gain_ref,
    shift_ref,
    w_ref,
    pick_ref,
    cot_ref,
    out_ref,
    unit_ref,
    proj_ref,
    pre_ref,
    low_ref,
    sums_ref,
):
    values = hid_ref[...] + (own_ref[...].astype(jnp.float32) + recv_ref[...].astype(jnp.float32))
    unit, inverse = norm_rows(values)
    gain = gain_ref[...]
    output = (unit * gain + shift_ref[...]).astype(jnp.bfloat16)
    out_ref[...] = output
    proj = dot_nn(output, w_ref[...])
    scale = lax.rsqrt(jnp.sum(proj * proj, axis=1, keepdims=True) + 1e-06)
    vec = proj * scale
    unit_ref[...] = vec.astype(jnp.bfloat16)
    pick = pick_ref[...]
    along = jnp.sum(vec * pick, axis=1, keepdims=True)
    proj_low = ((pick - vec * along) * scale).astype(jnp.bfloat16)
    proj_ref[...] = proj_low
    grad = cot_ref[...] + dot_nt(proj_low, w_ref[...])
    pre = back_rows(grad, gain, unit, inverse)
    pre_ref[...] = pre
    low_ref[...] = pre.astype(jnp.bfloat16)
    store_sums(sums_ref, grad, unit)


def turn(hidden, own, recv, gain, shift, w_colbert, pick, cot, width):
    rows, depth = hidden.shape
    low = jax.ShapeDtypeStruct((rows, depth), jnp.bfloat16)
    return pl.pallas_call(
        turn_body,
        in_specs=[whole()] * 8,
        out_specs=[whole()] * 6,
        out_shape=[
            low,
            low,
            low,
            jax.ShapeDtypeStruct((rows, depth), jnp.float32),
            low,
            jax.ShapeDtypeStruct((4, width), jnp.float32),
        ],
        compiler_params=params(),
        cost_estimate=cost(4 * rows * depth * depth, 5 << 20),
        name="turn",
    )(hidden, own, recv, gain[None], shift[None], w_colbert, pick, cot)


def gelu_with_slope(values):
    cdf = 0.5 * (1.0 + lax.erf(values * 0.7071067811865476))
    density = jnp.exp(-0.5 * values * values) * 0.3989422804014327
    return values * cdf, cdf + values * density


def local_by_head(
    tokens,
    w_query,
    w_key,
    w_value,
    w_out,
    gain_attn,
    shift_attn,
    w_up,
    w_down,
    gain_ffn,
    shift_ffn,
    w_colbert,
    query_vecs,
    match_index,
    passage_of,
    cot_act,
    cot_scores,
):
    pass_count = lax.axis_size("pass")
    qry_count = lax.axis_size("qry")
    pass_index = lax.axis_index("pass")
    qry_index = lax.axis_index("qry")
    chips = pass_count // 2
    own_rows = tokens.shape[0]
    block_rows = own_rows * qry_count
    same_core = [[index for index in range(pass_count) if index % 2 == core] for core in (0, 1)]
    ring = [[2 * chip + core for chip in ring_chips(chips) for core in (0, 1)]]
    parity = pass_index % 2
    own_id = passage_of[pass_index]

    def swap(value):
        return swap_over(value, "qry", 1)

    def sibling(value):
        return swap_over(value, "pass", 1)

    def to_heads(value):
        return lax.all_to_all(
            value, "pass", 0, 0, axis_index_groups=same_core, tiled=True
        )

    def after(value, *others):
        return lax.optimization_barrier((value,) + others)[0]

    def together(*values):
        return lax.optimization_barrier(values)

    near_send = project(tokens, w_query, w_key, w_value)
    near_pack = to_heads(near_send)
    tokens_other = swap(tokens)
    gathered = jnp.concatenate([tokens, tokens_other], axis=0)
    block_ids = passage_of.astype(jnp.int32)
    same = block_ids[:, None] == block_ids[None, :]
    starts = jnp.sum((block_ids[None, :] < block_ids[:, None]).astype(jnp.int32), axis=1)
    counts = jnp.sum(same.astype(jnp.int32), axis=1)
    chip = (pass_index // 2).astype(jnp.int32)
    bits = chips.bit_length() - 1
    info = jnp.concatenate(
        [starts, counts, parity[None].astype(jnp.int32)]
        + [((chip >> bit) & 1)[None] for bit in range(bits)]
    )
    first_bit = 2 * pass_count + 1

    seq_count = match_index.shape[1]
    query_rows = cot_scores.shape[0]
    pick_col = jnp.arange(seq_count, dtype=jnp.int32) == own_id
    span_count = jnp.sum((passage_of == own_id).astype(jnp.int32))
    first_index = jnp.sum((passage_of < own_id).astype(jnp.int32))
    raw_pick = jnp.sum(jnp.where(pick_col[None, :], match_index, 0), axis=1)
    local_row = raw_pick % (span_count * block_rows) - (pass_index - first_index) * block_rows
    inside = (local_row >= 0) & (local_row < block_rows)
    local_row = jnp.where(inside, (local_row + qry_index * own_rows) % block_rows, -1)
    one_hot = (local_row[:, None] == jnp.arange(block_rows, dtype=jnp.int32)[None, :]).astype(
        jnp.bfloat16
    )
    cot_pick = jnp.sum(jnp.where(pick_col[None, :], cot_scores, 0.0), axis=1)
    token_weight = jnp.repeat(cot_pick, query_vecs.shape[0] // query_rows)
    query_float = query_vecs.astype(jnp.float32)
    weighted_queries = (token_weight[:, None] * query_float).astype(jnp.bfloat16)
    unit_grad_part = contract_rows(one_hot, weighted_queries)
    turned_part = jnp.concatenate([unit_grad_part[own_rows:], unit_grad_part[:own_rows]], axis=0)
    unit_grad_send = turned_part.astype(jnp.bfloat16)

    far_send = project(after(tokens_other, near_send), w_query, w_key, w_value)
    near_pack, far_send = together(near_pack, far_send)
    far_pack = to_heads(far_send)
    near_sib = sibling(near_pack)
    piece = w_out.shape[0] // 2
    w_out_send = lax.dynamic_slice_in_dim(w_out, parity * piece, piece, axis=0)
    w_out_mine = swap(after(w_out_send, tokens_other))
    w_out_sib = sibling(w_out_mine)
    far_pack, near_sib, unit_grad_send, w_out_sib, gathered = together(
        far_pack, near_sib, unit_grad_send, w_out_sib, gathered
    )
    packs = (near_pack, far_pack, near_sib, sibling(far_pack))
    unit_grad_recv = swap(unit_grad_send)
    cot_other = swap(after(cot_act, unit_grad_send))
    ctx_pack, ctx_turned, lse = attend(info, *packs)
    unit_grad = unit_grad_part.astype(jnp.bfloat16).astype(jnp.float32) + unit_grad_recv.astype(
        jnp.float32
    )
    unit_grad_own, unit_grad_other = unit_grad[:own_rows], unit_grad[own_rows:]
    ctx_recv = to_heads(ctx_pack)
    ready = prepare(info, after(near_pack, ctx_pack), *packs[1:])
    cot_near = after(cot_act, ctx_pack).astype(jnp.float32)
    cot_far = after(cot_other, ctx_pack).astype(jnp.float32)
    ctx_recv, unit_grad_own, unit_grad_other, cot_near, cot_far, kv, key_turned, query = together(
        ctx_recv, unit_grad_own, unit_grad_other, cot_near, cot_far, *ready
    )
    tokens_all = lax.all_gather(
        after(gathered, far_pack), "pass", axis=0, axis_index_groups=ring, tiled=True
    )
    (
        context_low,
        hidden,
        hidden_far,
        hidden_low,
        hidden_other,
        unit_attn,
        unit_attn_far,
        inverse_attn,
        inverse_attn_far,
    ) = out_norm(
        info,
        ctx_recv,
        swap(ctx_recv),
        w_out,
        w_out_mine,
        w_out_sib,
        gathered,
        gain_attn,
        shift_attn,
    )

    def activate(rows):
        gated, slope = gelu_with_slope(dot_nn(rows, w_up))
        return lax.optimization_barrier((gated.astype(jnp.bfloat16), slope))

    gated_other, slope_other = activate(hidden_other)
    gated_own, slope_own = activate(hidden_low)

    def both_halves(rows_own, rows_other, product):
        part_other = product(rows_other).astype(jnp.bfloat16)
        part_own = product(after(rows_own, part_other)).astype(jnp.bfloat16)
        recv_own = swap(part_other)
        recv_other = swap(part_own)
        return part_own, part_other, recv_own, recv_other

    part_own, part_other, recv_own, recv_other = both_halves(
        gated_own, gated_other, lambda rows: dot_nn(rows, w_down)
    )
    local_width = w_query.shape[1]
    width = w_up.shape[1]
    model = tokens.shape[1]

    def turned(rows, part, recv, pick, cot):
        return turn(
            rows, part, recv, gain_ffn, shift_ffn, w_colbert, pick, cot, local_width
        )

    output_low, unit_own, proj_own, pre_grad, pre_low, sums_ffn = turned(
        hidden, part_own, recv_own, unit_grad_own, cot_near
    )
    inner_own = (dot_nt(pre_low, w_down) * slope_own).astype(jnp.bfloat16)
    recv_other, inner_own = together(recv_other, inner_own)
    output_other, unit_other, proj_other, pre_far, pre_other, _ = turned(
        hidden_far, part_other, recv_other, unit_grad_other, cot_far
    )
    inner_other = (dot_nt(pre_other, w_down) * slope_other).astype(jnp.bfloat16)
    late = late_grad(
        qry_index[None].astype(jnp.int32),
        chips,
        (
            (hidden_low, hidden_other, inner_own, inner_other, True),
            (pre_low, pre_other, gated_own, gated_other, True),
            (output_low, output_other, proj_own, proj_other, False),
        ),
    )
    inner_own, inner_other, late = together(inner_own, inner_other, late)
    part_own, part_other, recv_own, recv_other = both_halves(
        inner_own, inner_other, lambda rows: dot_nt(rows, w_up)
    )
    late_sums = lax.psum_scatter(
        late, "pass", scatter_dimension=0, axis_index_groups=ring, tiled=True
    )

    def back_to_attn(pre, part, recv, unit, inverse):
        return attn_norm_back(pre, part, recv, gain_attn, unit, inverse, local_width)

    attn_pre, attn_low, sums_attn = back_to_attn(
        pre_grad, part_own, recv_own, unit_attn, inverse_attn
    )
    _, attn_other, _ = back_to_attn(
        pre_far, part_other, recv_other, unit_attn_far, inverse_attn_far
    )

    dctx_send = ctx_grad_packed(attn_low, attn_other, w_out)
    own_dctx = to_heads(dctx_send)
    out_mine, out_send = out_grad_pack(
        info, chips, after(attn_low, dctx_send), attn_other, context_low
    )
    own_dctx, out_mine, out_send = together(own_dctx, out_mine, out_send)
    mine, other, dq = attend_back(info, kv, key_turned, query, own_dctx, ctx_turned, lse)
    back_send = combine(mine, sibling(other), dq)
    back = to_heads(back_send)
    back_own, out_send, unit_other = together(back_send, out_send, unit_other)

    out_keep, out_send = halve(info, first_bit, out_mine, sibling(out_send))
    out_came = swap_over(out_send, "pass", 2)
    unit_other = after(unit_other, out_send)
    picked = dot_nn(one_hot, jnp.concatenate([unit_own, unit_other], axis=0))
    per_query = jnp.sum((query_float * picked).reshape(query_rows, -1), axis=1)
    score_block = per_query[:, None] * pick_col.astype(jnp.float32)[None, :]
    score_part = lax.dynamic_update_slice(
        jnp.zeros((query_rows * qry_count, seq_count), jnp.float32),
        score_block,
        (qry_index * query_rows, jnp.zeros((), jnp.int32)),
    )
    score_rows = jnp.pad(score_part.reshape(1, -1), ((0, 7), (0, local_width - score_part.size)))
    small = jnp.concatenate([sums_attn, sums_ffn, score_rows], axis=0)
    small = small + swap(small)
    small = small + sibling(small)
    head_grads = head_grad(info, tokens_all, back_own, sibling(back_own))
    back, head_grads, small, late_sums = together(back, head_grads, small, late_sums)
    head_recv = to_heads(head_grads)
    token_own, token_send = token_grad(back, w_query, w_key, w_value)
    token_recv = swap(token_send)
    colbert_all = lax.all_gather(
        late_sums[:, 2 * width :], "pass", axis=0, axis_index_groups=ring, tiled=True
    )
    out_keep = after(out_keep, token_recv)
    for step in range(1, bits):
        out_keep, out_send = halve(info, first_bit + step, out_keep, out_came)
        out_came = swap_over(out_send, "pass", 2 << step)
    for step in range(bits):
        small = small + swap_over(small, "pass", 2 << step)
    grad_out = out_sum(out_keep, out_came, local_width)
    grad_tokens = attn_pre + token_own + token_recv.astype(jnp.float32)
    grad_query, grad_key, grad_value = split_heads(after(head_recv, token_recv))
    grad_up = late_sums[:, :width].astype(jnp.float32)
    grad_down = late_sums[:, width : 2 * width].astype(jnp.float32).T
    grad_colbert = widen(after(colbert_all, grad_up, grad_down, grad_out))
    norms = small[:8].reshape(4, model)
    scores = small[8].reshape(-1)[: score_part.size].reshape(score_part.shape)
    return (
        output_low,
        scores,
        grad_tokens,
        grad_query,
        grad_key,
        grad_value,
        grad_out,
        grad_up,
        grad_down,
        grad_colbert,
        norms[0],
        norms[1],
        norms[2],
        norms[3],
    )


def solution(mesh):
    by_head = mesh.shape["qry"] == 2
    return jax.shard_map(
        local_by_head if by_head else local_general,
        mesh=mesh,
        in_specs=(
            P(("pass", "qry"), None),
            P(None, "qry"),
            P(None, "qry"),
            P(None, "qry"),
            P("qry", None),
            P(),
            P(),
            P(None, "qry"),
            P("qry", None),
            P(),
            P(),
            P(),
            P("qry", None),
            P("qry", None),
            P(),
            P(("pass", "qry"), None),
            P("qry", None),
        ),
        out_specs=(
            P(("pass", "qry"), None),
            P(),
            P(("pass", "qry"), None),
            P("pass", "qry"),
            P("pass", "qry"),
            P("pass", "qry"),
            P("qry", "pass"),
            P("pass", "qry"),
            P("qry", "pass"),
            P(),
            P(),
            P(),
            P(),
            P(),
        ),
        check_vma=False,
    )
```

```python
import functools
import math

import jax
import jax.numpy as jnp
from jax import lax
from jax.experimental import pallas as pl
from jax.experimental.pallas import tpu as pltpu
from jax.sharding import PartitionSpec as P

HD = 64
SPAN = 8
LANES = 128
VMEM_LIMIT = 24 << 20
WIDE_LIMIT = 55 << 20
LOG2E = math.log2(math.e)


def passed_along(value, axis, steps):
    count = lax.axis_size(axis)
    first, last = (max(0, -steps), min(count, count - steps))
    return lax.ppermute(value, axis, [(source, source + steps) for source in range(first, last)])


def layer_norm(values, gain, shift):
    row_mean = jnp.mean(values, axis=-1, keepdims=True)
    centred = values - row_mean
    variance = jnp.mean(centred * centred, axis=-1, keepdims=True)
    return centred * lax.rsqrt(variance + 1e-05) * gain + shift


def gelu_exact(values):
    return 0.5 * values * (1.0 + jax.scipy.special.erf(values * 0.7071067811865476))


def normalize_rows(proj_rows):
    return proj_rows * lax.rsqrt(jnp.sum(proj_rows * proj_rows, axis=1, keepdims=True) + 1e-06)


def head_split(array):
    return array.reshape(array.shape[0], array.shape[1] // HD, HD)


def block_scores(queries, key_rows):
    return jnp.einsum("qhd,khd->hqk", queries, key_rows, preferred_element_type=jnp.float32) * 0.125


def grad_block(queries, ctx_grad, log_total, row_delta, key_rows, value_rows):
    scaled = block_scores(queries, key_rows)
    probs = jnp.exp(scaled - log_total[:, :, None])
    dprob = jnp.einsum("qhd,khd->hqk", ctx_grad, value_rows, preferred_element_type=jnp.float32)
    dscore = (0.125 * probs * (dprob - row_delta[:, :, None])).astype(jnp.bfloat16)
    dquery = jnp.einsum("hqk,khd->qhd", dscore, key_rows, preferred_element_type=jnp.float32)
    dkey = jnp.einsum("hqk,qhd->khd", dscore, queries, preferred_element_type=jnp.float32)
    dvalue = jnp.einsum(
        "hqk,qhd->khd", probs.astype(jnp.bfloat16), ctx_grad, preferred_element_type=jnp.float32
    )
    return (dquery, jnp.stack([dkey, dvalue]))


def contract_rows(left, right):
    return lax.dot_general(
        left, right, (((0,), (0,)), ((), ())), preferred_element_type=jnp.float32
    )


def contract_cols(left, right):
    return lax.dot_general(
        left, right, (((1,), (1,)), ((), ())), preferred_element_type=jnp.float32
    )


def local_general(
    tokens,
    w_query,
    w_key,
    w_value,
    w_out,
    gain_attn,
    shift_attn,
    w_up,
    w_down,
    gain_ffn,
    shift_ffn,
    w_colbert,
    query_vecs,
    match_index,
    passage_of,
    cot_act,
    cot_scores,
):
    pass_count = lax.axis_size("pass")
    qry_count = lax.axis_size("qry")
    pass_index = lax.axis_index("pass")
    qry_index = lax.axis_index("qry")
    own_id = passage_of[pass_index]

    def source_valid(offset):
        source = pass_index - offset
        inside = (source >= 0) & (source < pass_count)
        return inside & (passage_of[jnp.clip(source, 0, pass_count - 1)] == own_id)

    gathered = lax.all_gather(tokens, "qry", axis=0, tiled=True)
    block_rows = gathered.shape[0]
    local_width = w_query.shape[1]
    w_qkv = jnp.concatenate([w_query, w_key, w_value], axis=1)
    qkv_rows = jnp.dot(gathered, w_qkv, preferred_element_type=jnp.float32).astype(jnp.bfloat16)
    query_flat = qkv_rows[:, :local_width]
    key_flat = qkv_rows[:, local_width : 2 * local_width]
    value_flat = qkv_rows[:, 2 * local_width :]
    queries = head_split(query_flat)
    heads = queries.shape[1]
    own_pair = jnp.stack([key_flat, value_flat])
    offsets = [distance for distance in range(1, SPAN)] + [-distance for distance in range(1, SPAN)]

    def fetch_keys():
        received = []
        for offset in offsets:
            received.append(passed_along(own_pair, "pass", offset))
        return received

    remote = fetch_keys()

    def stat_of(kv_pair):
        return jax.nn.logsumexp(block_scores(queries, head_split(kv_pair[0])), axis=2)

    log_total = stat_of(own_pair)
    for offset, kv_pair in zip(offsets, remote):
        log_total = lax.cond(
            source_valid(offset),
            lambda current, kv_pair=kv_pair: jnp.logaddexp(current, stat_of(kv_pair)),
            lambda current: current,
            log_total,
        )

    def weighted(kv_pair):
        probs = jnp.exp(
            block_scores(queries, head_split(kv_pair[0])) - log_total[:, :, None]
        ).astype(jnp.bfloat16)
        return jnp.einsum(
            "hqk,khd->qhd", probs, head_split(kv_pair[1]), preferred_element_type=jnp.float32
        )

    context = weighted(own_pair)
    for offset, kv_pair in zip(offsets, remote):
        context = lax.cond(
            source_valid(offset),
            lambda running, kv_pair=kv_pair: running + weighted(kv_pair),
            lambda running: running,
            context,
        )
    context_low = context.reshape(block_rows, local_width).astype(jnp.bfloat16)
    piece_rows = context_low
    attn_rows = lax.psum_scatter(
        jnp.dot(piece_rows, w_out, preferred_element_type=jnp.float32).astype(jnp.bfloat16),
        "qry",
        scatter_dimension=0,
        tiled=True,
    ).astype(jnp.float32)
    hidden, norm_attn_back = jax.vjp(
        layer_norm, tokens.astype(jnp.float32) + attn_rows, gain_attn, shift_attn
    )
    hidden_all = lax.all_gather(hidden.astype(jnp.bfloat16), "qry", axis=0, tiled=True)
    inner_pre = jnp.dot(hidden_all, w_up, preferred_element_type=jnp.float32)
    gated_float, gelu_back = jax.vjp(gelu_exact, inner_pre)
    gated_low = gated_float.astype(jnp.bfloat16)
    piece_rows = gated_low
    ffn_rows = lax.psum_scatter(
        jnp.dot(piece_rows, w_down, preferred_element_type=jnp.float32).astype(jnp.bfloat16),
        "qry",
        scatter_dimension=0,
        tiled=True,
    ).astype(jnp.float32)
    output, norm_ffn_back = jax.vjp(layer_norm, hidden + ffn_rows, gain_ffn, shift_ffn)
    output_low = output.astype(jnp.bfloat16)
    proj_rows = jnp.dot(output_low, w_colbert, preferred_element_type=jnp.float32)
    unit_vecs, unit_back = jax.vjp(normalize_rows, proj_rows)
    unit_all = lax.all_gather(unit_vecs.astype(jnp.bfloat16), "qry", axis=0, tiled=True)
    seq_count = match_index.shape[1]
    query_rows = cot_scores.shape[0]
    numbers = jnp.arange(seq_count, dtype=jnp.int32)
    pick_col = numbers == own_id
    span_count = jnp.sum((passage_of == own_id).astype(jnp.int32))
    first_index = jnp.sum((passage_of < own_id).astype(jnp.int32))
    length = span_count * block_rows
    raw_pick = jnp.sum(jnp.where(pick_col[None, :], match_index, 0), axis=1)
    local_row = raw_pick % length - (pass_index - first_index) * block_rows
    one_hot = (local_row[:, None] == jnp.arange(block_rows, dtype=jnp.int32)[None, :]).astype(
        jnp.bfloat16
    )
    picked = jnp.dot(one_hot, unit_all, preferred_element_type=jnp.float32)
    query_float = query_vecs.astype(jnp.float32)
    match_vals = jnp.sum(query_float * picked, axis=1)
    per_query = jnp.sum(match_vals.reshape(query_rows, -1), axis=1)
    score_block = per_query[:, None] * pick_col.astype(jnp.float32)[None, :]
    score_part = lax.dynamic_update_slice(
        jnp.zeros((query_rows * qry_count, seq_count), jnp.float32),
        score_block,
        (qry_index * query_rows, jnp.zeros((), jnp.int32)),
    )
    cot_pick = jnp.sum(jnp.where(pick_col[None, :], cot_scores, 0.0), axis=1)
    token_weight = jnp.repeat(cot_pick, query_vecs.shape[0] // query_rows)
    weighted_queries = (token_weight[:, None] * query_float).astype(jnp.bfloat16)
    piece_rows = one_hot
    unit_grad = lax.psum_scatter(
        contract_rows(piece_rows, weighted_queries).astype(jnp.bfloat16),
        "qry",
        scatter_dimension=0,
        tiled=True,
    ).astype(jnp.float32)
    (proj_grad,) = unit_back(unit_grad)
    proj_low = proj_grad.astype(jnp.bfloat16)
    grad_colbert = contract_rows(output_low, proj_low)
    out_grad = cot_act.astype(jnp.float32) + contract_cols(proj_low, w_colbert)
    pre_grad, grad_gain_ffn, grad_shift_ffn = norm_ffn_back(out_grad)
    ffn_all = lax.all_gather(pre_grad.astype(jnp.bfloat16), "qry", axis=0, tiled=True)
    gated_grad = contract_cols(ffn_all, w_down)
    grad_down = contract_rows(gated_low, ffn_all)
    (inner_grad,) = gelu_back(gated_grad)
    inner_low = inner_grad.astype(jnp.bfloat16)
    grad_up = contract_rows(hidden_all, inner_low)
    piece_rows = inner_low
    hidden_grad = pre_grad + lax.psum_scatter(
        contract_cols(piece_rows, w_up).astype(jnp.bfloat16), "qry", scatter_dimension=0, tiled=True
    ).astype(jnp.float32)
    attn_pre_grad, grad_gain_attn, grad_shift_attn = norm_attn_back(hidden_grad)
    attn_all = lax.all_gather(attn_pre_grad.astype(jnp.bfloat16), "qry", axis=0, tiled=True)
    grad_out = contract_rows(context_low, attn_all)
    ctx_grad = head_split(contract_cols(attn_all, w_out).astype(jnp.bfloat16))
    row_delta = jnp.einsum("qhd,qhd->hq", ctx_grad.astype(jnp.float32), context)
    remote_back = fetch_keys()
    dquery, dkv_own = grad_block(
        queries, ctx_grad, log_total, row_delta, head_split(key_flat), head_split(value_flat)
    )
    key_value_grad = dkv_own
    zero_query = jnp.zeros_like(dquery)
    zero_pair = jnp.zeros((2, block_rows, heads, HD), jnp.float32)
    for offset, kv_pair in zip(offsets, remote_back):
        query_part, pair_part = lax.cond(
            source_valid(offset),
            lambda incoming: grad_block(
                queries,
                ctx_grad,
                log_total,
                row_delta,
                head_split(incoming[0]),
                head_split(incoming[1]),
            ),
            lambda incoming: (zero_query, zero_pair),
            kv_pair,
        )
        dquery = dquery + query_part
        returned = passed_along(
            pair_part.reshape(2, block_rows, local_width).astype(jnp.bfloat16), "pass", -offset
        ).astype(jnp.float32)
        key_value_grad = key_value_grad + returned.reshape(2, block_rows, heads, HD)
    dqkv_low = jnp.concatenate(
        [
            dquery.reshape(block_rows, local_width),
            key_value_grad[0].reshape(block_rows, local_width),
            key_value_grad[1].reshape(block_rows, local_width),
        ],
        axis=1,
    ).astype(jnp.bfloat16)
    grad_qkv = contract_rows(gathered, dqkv_low)
    piece_rows = dqkv_low
    grad_tokens = attn_pre_grad + lax.psum_scatter(
        contract_cols(piece_rows, w_qkv).astype(jnp.bfloat16),
        "qry",
        scatter_dimension=0,
        tiled=True,
    ).astype(jnp.float32)
    summed = (
        lax.psum_scatter(
            grad_qkv[:, :local_width].astype(jnp.bfloat16), "pass", scatter_dimension=0, tiled=True
        ).astype(jnp.float32),
        lax.psum_scatter(
            grad_qkv[:, local_width : 2 * local_width].astype(jnp.bfloat16),
            "pass",
            scatter_dimension=0,
            tiled=True,
        ).astype(jnp.float32),
        lax.psum_scatter(
            grad_qkv[:, 2 * local_width :].astype(jnp.bfloat16),
            "pass",
            scatter_dimension=0,
            tiled=True,
        ).astype(jnp.float32),
        lax.psum_scatter(
            grad_out.astype(jnp.bfloat16), "pass", scatter_dimension=1, tiled=True
        ).astype(jnp.float32),
        lax.psum_scatter(
            grad_up.astype(jnp.bfloat16), "pass", scatter_dimension=0, tiled=True
        ).astype(jnp.float32),
        lax.psum_scatter(
            grad_down.astype(jnp.bfloat16), "pass", scatter_dimension=1, tiled=True
        ).astype(jnp.float32),
    )
    shared = lax.psum(
        (grad_colbert, grad_gain_attn, grad_shift_attn, grad_gain_ffn, grad_shift_ffn, score_part),
        ("pass", "qry"),
    )
    return (
        output_low,
        shared[5],
        grad_tokens,
        summed[0],
        summed[1],
        summed[2],
        summed[3],
        summed[4],
        summed[5],
        shared[0],
        shared[1],
        shared[2],
        shared[3],
        shared[4],
    )


def swap_over(value, axis, mask):
    count = lax.axis_size(axis)
    return lax.ppermute(value, axis, [(index, index ^ mask) for index in range(count)])


def ring_chips(chips):
    layers = chips // 2
    return [2 * z for z in range(layers)] + [2 * z + 1 for z in reversed(range(layers))]


def low_lanes(rows):
    return lax.broadcasted_iota(jnp.int32, (rows, LANES), 1) < HD


def split_lanes(first, second):
    low = low_lanes(first.shape[0])
    return (
        jnp.where(low, first, pltpu.roll(second, HD, 1)),
        jnp.where(low, pltpu.roll(first, HD, 1), second),
    )


def dot_nn(left, right):
    return jnp.dot(left, right, preferred_element_type=jnp.float32)


def dot_nt(left, right):
    return contract_cols(left, right)


def params(*semantics, limit=VMEM_LIMIT):
    return pltpu.CompilerParams(
        dimension_semantics=semantics or None, vmem_limit_bytes=limit
    )


def cost(flops, moved, transcendentals=0):
    return pl.CostEstimate(
        flops=int(flops), bytes_accessed=int(moved), transcendentals=int(transcendentals)
    )


def project_body(x_ref, wq_ref, wk_ref, wv_ref, out_ref):
    x = x_ref[...]
    rows = x.shape[0]
    half = rows // 2
    query = dot_nn(x, wq_ref[...])
    key = dot_nn(x, wk_ref[...])
    value = dot_nn(x, wv_ref[...])
    for pair in range(query.shape[1] // LANES):
        cols = slice(pair * LANES, (pair + 1) * LANES)
        first, second = split_lanes(key[:, cols], value[:, cols])
        out_ref[2 * pair, 0:rows] = first.astype(jnp.bfloat16)
        out_ref[2 * pair + 1, 0:rows] = second.astype(jnp.bfloat16)
        first, second = split_lanes(query[:half, cols], query[half:, cols])
        out_ref[2 * pair, rows : rows + half] = first.astype(jnp.bfloat16)
        out_ref[2 * pair + 1, rows : rows + half] = second.astype(jnp.bfloat16)


def project(x, wq, wk, wv):
    rows, depth = x.shape
    width = wq.shape[1]
    heads = width // HD
    steps = 2
    weight = pl.BlockSpec((depth, width // steps), lambda i: (0, i))
    return pl.pallas_call(
        project_body,
        grid=(steps,),
        in_specs=[pl.BlockSpec((rows, depth), lambda i: (0, 0)), weight, weight, weight],
        out_specs=pl.BlockSpec((heads // steps, rows * 3 // 2, LANES), lambda i: (i, 0, 0)),
        out_shape=jax.ShapeDtypeStruct((heads, rows * 3 // 2, LANES), jnp.bfloat16),
        compiler_params=params("arbitrary", limit=WIDE_LIMIT),
        cost_estimate=cost(2 * rows * depth * width * 3, 2 * (3 * depth * width + 4 * rows * depth)),
        name="project",
    )(x, wq, wk, wv)


def load_query(packed):
    wide = packed.astype(jnp.float32)
    low = low_lanes(wide.shape[0])
    top = jnp.where(low, wide, 0.0)
    bottom = jnp.where(low, pltpu.roll(wide, HD, 1), 0.0)
    return jnp.concatenate([top, bottom], axis=0).astype(jnp.bfloat16)


def pack_transposed(columns):
    half = columns.shape[1] // 2
    return jnp.concatenate([columns[:, :half], columns[:, half:]], axis=0).T


def square_sums(rows_low):
    group = lambda axis: lax.broadcasted_iota(jnp.int32, (LANES, LANES), axis) // HD
    ones = (group(0) == group(1)).astype(jnp.bfloat16)
    wide = rows_low.astype(jnp.float32)
    sums = dot_nn((wide * wide).astype(jnp.bfloat16), ones)
    return jnp.max(sums.reshape(sums.shape[0] // 8, 8, LANES), axis=0)


def over_blocks(first, count, step):
    for size in (8, 4, 2, 1):

        @pl.when(count & size != 0)
        def _(size=size):
            step(first + (count & ~(2 * size - 1)), size)


def load_block(near_ref, far_ref, chip, block_ref):
    half = block_ref.shape[0] // 2
    block_ref[:half] = near_ref[chip, 0:half]
    block_ref[half:] = far_ref[chip, 0:half]


def load_queries(near_ref, far_ref, chip, block_ref):
    half = block_ref.shape[0] // 2
    block_ref[:half] = load_query(near_ref[chip, half:])
    block_ref[half:] = load_query(far_ref[chip, half:])


def attend_body(
    info_ref, near_ref, far_ref, near_sib_ref, far_sib_ref, ctx_ref, ctxt_ref, lse_ref, kv_s, v1_s, q_s, total_s, score_s, top_s
):
    chips = near_ref.shape[0]
    blocks = 2 * chips
    rows = kv_s.shape[1]
    half = rows // 2
    parity = info_ref[2 * blocks]
    scale = 0.125 * LOG2E
    low = low_lanes(rows)
    key_top = query_top = jnp.zeros((8, LANES), jnp.float32)
    for chip in range(chips):
        for refs, which in (
            ((near_ref, far_ref), parity),
            ((near_sib_ref, far_sib_ref), 1 - parity),
        ):
            place = 2 * chip + which
            load_block(*refs, chip, kv_s.at[place])
            block = kv_s[place]
            v1_s[place] = jnp.where(low, 1.0, block.astype(jnp.float32)).astype(jnp.bfloat16)
            key_top = jnp.maximum(key_top, square_sums(block))
        load_queries(near_ref, far_ref, chip, q_s.at[chip])
        query_top = jnp.maximum(query_top, square_sums(q_s[chip]))
    key_top = jnp.max(jnp.where(low_lanes(8), key_top, 0.0))
    bound = jnp.max(query_top) * key_top * (1.02 * scale * scale)
    safe = bound < 3600.0

    @pl.when(safe)
    def _():
        def one_item(item, carry):
            query = q_s[item]
            total_s[item] = jnp.zeros((rows, LANES), jnp.float32)

            def step(block, n):
                keys = kv_s[pl.ds(block, n)].reshape(n * rows, LANES)
                values = v1_s[pl.ds(block, n)].reshape(n * rows, LANES)
                prob = jnp.exp2(dot_nt(query, keys) * scale).astype(jnp.bfloat16)
                total_s[item] += dot_nn(prob, values)

            place = 2 * item + parity
            over_blocks(info_ref[place], info_ref[blocks + place], step)
            top_s[item] = jnp.zeros((8, rows), jnp.float32)
            return carry

        lax.fori_loop(0, chips, one_item, 0)

    @pl.when(jnp.logical_not(safe))
    def _():
        def one_item(item, carry):
            query = q_s[item]
            place = 2 * item + parity
            first, count = info_ref[place], info_ref[blocks + place]

            def scores(step, top):
                score = dot_nt(query, kv_s[first + step]) * scale
                score_s[step] = score
                return jnp.maximum(top, score)

            top = lax.fori_loop(0, count, scores, jnp.full((rows, rows), -jnp.inf, jnp.float32))
            top = jnp.max(top, axis=1, keepdims=True)
            total_s[item] = jnp.zeros((rows, LANES), jnp.float32)

            def weigh(step, carry):
                prob = jnp.exp2(score_s[step] - top).astype(jnp.bfloat16)
                total_s[item] += dot_nn(prob, v1_s[first + step])
                return carry

            lax.fori_loop(0, count, weigh, 0)
            top_s[item] = jnp.broadcast_to(top, (rows, LANES)).T[0:8]
            return carry

        lax.fori_loop(0, chips, one_item, 0)

    narrow = low_lanes(half)
    for item in range(chips):
        total = total_s[item]
        turned = total.T
        weight = turned[0:8]
        lse_ref[item] = top_s[item] + jnp.log2(weight)
        ctxt_ref[item] = turned[HD:] / weight[0:1]
        inverse = 1.0 / jnp.where(low, total, 1.0)
        context = total * pltpu.roll(inverse, HD, 1)
        ctx_ref[item] = jnp.where(
            narrow, pltpu.roll(context[:half], HD, 1), context[half:]
        ).astype(jnp.bfloat16)


def whole():
    return pl.BlockSpec(memory_space=pltpu.VMEM)


def attend(info, *packs):
    chips, packed, _ = packs[0].shape
    rows = packed * 4 // 3
    blocks = 2 * chips
    return pl.pallas_call(
        attend_body,
        in_specs=[pl.BlockSpec(memory_space=pltpu.SMEM)] + [whole()] * 4,
        out_specs=[whole()] * 3,
        out_shape=[
            jax.ShapeDtypeStruct((chips, rows // 2, LANES), jnp.bfloat16),
            jax.ShapeDtypeStruct((chips, HD, rows), jnp.float32),
            jax.ShapeDtypeStruct((chips, 8, rows), jnp.float32),
        ],
        scratch_shapes=[
            pltpu.VMEM((blocks, rows, LANES), jnp.bfloat16),
            pltpu.VMEM((blocks, rows, LANES), jnp.bfloat16),
            pltpu.VMEM((chips, rows, LANES), jnp.bfloat16),
            pltpu.VMEM((chips, rows, LANES), jnp.float32),
            pltpu.VMEM((SPAN, rows, rows), jnp.float32),
            pltpu.VMEM((chips, 8, rows), jnp.float32),
        ],
        compiler_params=params(limit=WIDE_LIMIT),
        cost_estimate=cost(2 * 2 * 40 * rows * rows * LANES, 4 << 20, 40 * rows * rows),
        name="attend",
    )(info, *packs)


def prepare_body(info_ref, near_ref, far_ref, near_sib_ref, far_sib_ref, kv_ref, kt_ref, q_ref):
    chips = near_ref.shape[0]
    parity = info_ref[4 * chips]
    for chip in range(chips):
        for refs, which in (
            ((near_ref, far_ref), parity),
            ((near_sib_ref, far_sib_ref), 1 - parity),
        ):
            place = 2 * chip + which
            load_block(*refs, chip, kv_ref.at[place])
            kt_ref[place] = kv_ref[place].astype(jnp.float32).T[:HD].astype(jnp.bfloat16)
        load_queries(near_ref, far_ref, chip, q_ref.at[chip])


def prepare(info, *packs):
    chips, packed, _ = packs[0].shape
    rows = packed * 4 // 3
    return pl.pallas_call(
        prepare_body,
        in_specs=[pl.BlockSpec(memory_space=pltpu.SMEM)] + [whole()] * 4,
        out_specs=[whole()] * 3,
        out_shape=[
            jax.ShapeDtypeStruct((2 * chips, rows, LANES), jnp.bfloat16),
            jax.ShapeDtypeStruct((2 * chips, HD, rows), jnp.bfloat16),
            jax.ShapeDtypeStruct((chips, rows, LANES), jnp.bfloat16),
        ],
        compiler_params=params(),
        cost_estimate=cost(1 << 20, 4 << 20),
        name="prepare",
    )(info, *packs)


def attend_back_body(
    info_ref,
    kv_ref,
    kt_ref,
    q_ref,
    dctx_ref,
    ctxt_ref,
    lse_ref,
    mine_ref,
    other_ref,
    dq_ref,
    acc_s,
    both_s,
    delta_s,
    total_s,
):
    chips = q_ref.shape[0]
    blocks = 2 * chips
    rows = kv_ref.shape[1]
    half = rows // 2
    parity = info_ref[2 * blocks]
    scale = 0.125 * LOG2E
    low = low_lanes(half)
    for item in range(chips):
        packed = dctx_ref[item].astype(jnp.float32)
        both_s[item, :rows] = q_ref[item]
        both_s[item, rows : rows + half] = jnp.where(
            low, 0.0, pltpu.roll(packed, HD, 1)
        ).astype(jnp.bfloat16)
        both_s[item, rows + half :] = jnp.where(low, 0.0, packed).astype(jnp.bfloat16)
        turned = packed.T
        turned = jnp.concatenate([turned[:HD], turned[HD:]], axis=1)
        delta = jnp.sum(turned * ctxt_ref[item], axis=0, keepdims=True)
        delta_s[item] = jnp.broadcast_to(delta, (8, rows))
        acc_s[2 * item] = jnp.zeros((rows, LANES), jnp.float32)
        acc_s[2 * item + 1] = jnp.zeros((rows, LANES), jnp.float32)
        total_s[item] = jnp.zeros((HD, rows), jnp.float32)

    def one_item(item, carry):
        query = both_s[item, :rows]
        dctx = both_s[item, rows:]
        delta = delta_s[item, 0:1]
        lse = lse_ref[item, 0:1]

        def step(block, n):
            kv = kv_ref[pl.ds(block, n)].reshape(n * rows, LANES)
            prob = jnp.exp2(dot_nt(kv, query) * scale - lse)
            dscore = (prob * (dot_nt(kv, dctx) - delta)).astype(jnp.bfloat16)
            pair = jnp.concatenate([dscore, prob.astype(jnp.bfloat16)], axis=1)
            acc_s[pl.ds(block, n)] += dot_nn(pair, both_s[item]).reshape(n, rows, LANES)
            total = total_s[item]
            for part in range(n):
                total = total + dot_nn(kt_ref[block + part], dscore[part * rows : (part + 1) * rows])
            total_s[item] = total

        place = 2 * item + parity
        over_blocks(info_ref[place], info_ref[blocks + place], step)
        return carry

    lax.fori_loop(0, chips, one_item, 0)
    key_scale = jnp.where(low_lanes(rows), 0.125, 1.0)
    for item in range(chips):
        dq_ref[item] = pack_transposed(total_s[item] * 0.125).astype(jnp.bfloat16)
        mine_ref[item] = (acc_s[2 * item + parity] * key_scale).astype(jnp.bfloat16)
        other_ref[item] = (acc_s[2 * item + 1 - parity] * key_scale).astype(jnp.bfloat16)


def attend_back(info, kv, kt, query, dctx, ctxt, lse):
    chips, rows, _ = query.shape
    blocks = 2 * chips
    share = jax.ShapeDtypeStruct((chips, rows, LANES), jnp.bfloat16)
    return pl.pallas_call(
        attend_back_body,
        in_specs=[pl.BlockSpec(memory_space=pltpu.SMEM)] + [whole()] * 6,
        out_specs=[whole()] * 3,
        out_shape=[share, share, jax.ShapeDtypeStruct((chips, rows // 2, LANES), jnp.bfloat16)],
        scratch_shapes=[
            pltpu.VMEM((blocks, rows, LANES), jnp.float32),
            pltpu.VMEM((chips, 2 * rows, LANES), jnp.bfloat16),
            pltpu.VMEM((chips, 8, rows), jnp.float32),
            pltpu.VMEM((chips, HD, rows), jnp.float32),
        ],
        compiler_params=params(limit=WIDE_LIMIT),
        cost_estimate=cost(2 * 5 * 40 * rows * rows * LANES, 5 << 20, 40 * rows * rows),
        name="attend_back",
    )(info, kv, kt, query, dctx, ctxt, lse)


def combine_body(mine_ref, sib_ref, dq_ref, out_ref):
    chips, rows, _ = mine_ref.shape
    for chip in range(chips):
        total = mine_ref[chip].astype(jnp.float32) + sib_ref[chip].astype(jnp.float32)
        out_ref[chip, 0:rows] = total.astype(jnp.bfloat16)
        out_ref[chip, rows:] = dq_ref[chip]


def combine(mine, sib, dq):
    chips, rows, _ = mine.shape
    return pl.pallas_call(
        combine_body,
        in_specs=[whole()] * 3,
        out_specs=whole(),
        out_shape=jax.ShapeDtypeStruct((chips, rows * 3 // 2, LANES), jnp.bfloat16),
        compiler_params=params(),
        cost_estimate=cost(1 << 20, 2 << 20),
        name="combine",
    )(mine, sib, dq)


def out_norm_body(
    info_ref,
    in_ref,
    other_ref,
    w_ref,
    w_mine_ref,
    w_sib_ref,
    tok_ref,
    gain_ref,
    shift_ref,
    ctx_ref,
    *outs,
):
    *outs, far_s = outs
    heads, half, _ = in_ref.shape
    parity = info_ref[2 * 2 * in_ref.shape[0]]
    for pair in range(heads // 2):
        cols = slice(pair * LANES, (pair + 1) * LANES)
        top, bottom = split_lanes(
            in_ref[2 * pair].astype(jnp.float32), in_ref[2 * pair + 1].astype(jnp.float32)
        )
        ctx_ref[0:half, cols] = top.astype(jnp.bfloat16)
        ctx_ref[half:, cols] = bottom.astype(jnp.bfloat16)
        top, bottom = split_lanes(
            other_ref[2 * pair].astype(jnp.float32), other_ref[2 * pair + 1].astype(jnp.float32)
        )
        far_s[0:half, cols] = bottom.astype(jnp.bfloat16)
        far_s[half:, cols] = top.astype(jnp.bfloat16)
    first = parity == 0
    mine, sib = w_mine_ref[...], w_sib_ref[...]
    w_far = jnp.concatenate([jnp.where(first, mine, sib), jnp.where(first, sib, mine)], axis=0)
    rows = dot_nn(ctx_ref[...], w_ref[...]) + dot_nn(far_s[...], w_far)
    unit, inverse = norm_rows(tok_ref[...].astype(jnp.float32) + rows)
    hidden = unit * gain_ref[...] + shift_ref[...]
    inverse = jnp.broadcast_to(inverse, (2 * half, LANES))
    for index, value in enumerate((hidden, hidden.astype(jnp.bfloat16), unit, inverse)):
        outs[2 * index][...] = value[:half]
        outs[2 * index + 1][...] = value[half:]


def out_norm(info, packed, packed_other, w_out, w_mine, w_sib, tokens, gain, shift):
    heads, half, _ = packed.shape
    width, depth = w_out.shape
    wide = jax.ShapeDtypeStruct((half, depth), jnp.float32)
    low = jax.ShapeDtypeStruct((half, depth), jnp.bfloat16)
    narrow = jax.ShapeDtypeStruct((half, LANES), jnp.float32)
    return pl.pallas_call(
        out_norm_body,
        in_specs=[pl.BlockSpec(memory_space=pltpu.SMEM)] + [whole()] * 8,
        out_specs=[whole()] * 9,
        out_shape=[jax.ShapeDtypeStruct((2 * half, width), jnp.bfloat16)]
        + [wide, wide, low, low, wide, wide, narrow, narrow],
        scratch_shapes=[pltpu.VMEM((2 * half, width), jnp.bfloat16)],
        compiler_params=params(),
        cost_estimate=cost(8 * half * width * depth, 5 << 20),
        name="out_norm",
    )(info, packed, packed_other, w_out, w_mine, w_sib, tokens, gain[None], shift[None])


def ctx_grad_body(own_ref, other_ref, w_ref, out_ref):
    half = out_ref.shape[1]
    grad = dot_nt(jnp.concatenate([own_ref[...], other_ref[...]], axis=0), w_ref[...])
    for pair in range(grad.shape[1] // LANES):
        cols = slice(pair * LANES, (pair + 1) * LANES)
        first, second = split_lanes(grad[:half, cols], grad[half:, cols])
        out_ref[2 * pair] = first.astype(jnp.bfloat16)
        out_ref[2 * pair + 1] = second.astype(jnp.bfloat16)


def ctx_grad_packed(grad_own, grad_other, w_out):
    rows, depth = 2 * grad_own.shape[0], grad_own.shape[1]
    width = w_out.shape[0]
    return pl.pallas_call(
        ctx_grad_body,
        in_specs=[whole()] * 3,
        out_specs=whole(),
        out_shape=jax.ShapeDtypeStruct((width // HD, rows // 2, LANES), jnp.bfloat16),
        compiler_params=params(),
        cost_estimate=cost(2 * rows * width * depth, 2 << 20),
        name="ctx_grad",
    )(grad_own, grad_other, w_out)


def head_grad_body(info_ref, tok_ref, own_ref, sib_ref, out_ref, acc_s, grad_s):
    step = pl.program_id(0)
    steps = pl.num_programs(0)
    chips, packed, _ = own_ref.shape
    blocks = 2 * chips
    rows = packed * 2 // 3
    parity = info_ref[2 * blocks]
    group = chips // steps
    columns = []
    for index in range(group):
        place = step * group + index
        chip = jnp.where(place < chips // 2, 2 * place, 2 * chips - 1 - 2 * place)
        own, sib = own_ref[chip].astype(jnp.float32), sib_ref[chip].astype(jnp.float32)
        for core in range(2):
            block = jnp.where(parity == core, own, sib)
            dq = block[rows:].T
            dq = jnp.concatenate([dq[:HD], dq[HD:]], axis=1)
            columns.append(jnp.concatenate([block[:rows].T, dq], axis=0).astype(jnp.bfloat16))
    part = dot_nn(jnp.concatenate(columns, axis=1), tok_ref[...])

    @pl.when(step == 0)
    def _():
        acc_s[...] = part

    @pl.when(step > 0)
    def _():
        acc_s[...] += part

    @pl.when(step == steps - 1)
    def _():
        grad = acc_s[...]
        depth = grad.shape[1] // blocks
        wide = jnp.concatenate([grad, grad[2 * HD :]], axis=0)
        grad_s[...] = wide.T.reshape(blocks, depth, 2 * LANES)

        def pack(index, carry):
            part = grad_s[2 * index + parity]
            out_ref[index, 0:depth] = part[:, :LANES].astype(jnp.bfloat16)
            query = part[:, LANES:]
            mixed = jnp.where(low_lanes(depth // 2), query[: depth // 2], query[depth // 2 :])
            out_ref[index, depth : depth + depth // 2] = mixed.astype(jnp.bfloat16)
            return carry

        lax.fori_loop(0, chips, pack, 0)


def head_grad(info, tokens_all, own, sib):
    chips, packed, _ = own.shape
    blocks = 2 * chips
    rows = packed * 2 // 3
    depth = tokens_all.shape[1]
    piece = depth // blocks
    steps = 4
    full = lambda shape: pl.BlockSpec(shape, lambda i: (0,) * len(shape))
    return pl.pallas_call(
        head_grad_body,
        grid=(steps,),
        in_specs=[
            pl.BlockSpec(memory_space=pltpu.SMEM),
            pl.BlockSpec((blocks * rows // steps, depth), lambda i: (i, 0)),
            full(own.shape),
            full(sib.shape),
        ],
        out_specs=full((chips, piece + piece // 2, LANES)),
        out_shape=jax.ShapeDtypeStruct((chips, piece + piece // 2, LANES), jnp.bfloat16),
        scratch_shapes=[
            pltpu.VMEM((3 * HD, depth), jnp.float32),
            pltpu.VMEM((blocks, piece, 2 * LANES), jnp.float32),
        ],
        compiler_params=params("arbitrary", limit=2 * VMEM_LIMIT),
        cost_estimate=cost(2 * blocks * rows * depth * 3 * HD, blocks * rows * depth * 2),
        name="head_grad",
    )(info, tokens_all, own, sib)


def token_grad_body(in_ref, wq_ref, wk_ref, wv_ref, own_ref, send_ref, d_s):
    heads = in_ref.shape[0]
    rows = d_s.shape[1]
    half = rows // 2
    load = lambda head, lo, hi: in_ref[head, lo:hi].astype(jnp.float32)
    for pair in range(heads // 2):
        cols = slice(pair * LANES, (pair + 1) * LANES)
        a, b = 2 * pair, 2 * pair + 1
        key, value = split_lanes(load(a, 0, rows), load(b, 0, rows))
        d_s[1, :, cols] = key.astype(jnp.bfloat16)
        d_s[2, :, cols] = value.astype(jnp.bfloat16)
        top, bottom = split_lanes(load(a, rows, rows + half), load(b, rows, rows + half))
        d_s[0, :half, cols] = top.astype(jnp.bfloat16)
        d_s[0, half:, cols] = bottom.astype(jnp.bfloat16)
    total = dot_nt(d_s[0], wq_ref[...]) + dot_nt(d_s[1], wk_ref[...]) + dot_nt(d_s[2], wv_ref[...])
    own_ref[...] = total[:half]
    send_ref[...] = total[half:].astype(jnp.bfloat16)


def token_grad(packed, wq, wk, wv):
    depth, width = wq.shape
    rows = packed.shape[1] * 2 // 3
    return pl.pallas_call(
        token_grad_body,
        in_specs=[whole()] * 4,
        out_specs=[whole()] * 2,
        out_shape=[
            jax.ShapeDtypeStruct((rows // 2, depth), jnp.float32),
            jax.ShapeDtypeStruct((rows // 2, depth), jnp.bfloat16),
        ],
        scratch_shapes=[pltpu.VMEM((3, rows, width), jnp.bfloat16)],
        compiler_params=params(),
        cost_estimate=cost(6 * rows * depth * width, 5 << 20),
        name="token_grad",
    )(packed, wq, wk, wv)


def split_heads_body(in_ref, gq_ref, gk_ref, gv_ref):
    heads = in_ref.shape[0]
    piece = gq_ref.shape[0]
    last = piece + piece // 2
    load = lambda head, lo, hi: in_ref[head, lo:hi].astype(jnp.float32)
    for pair in range(heads // 2):
        cols = slice(pair * LANES, (pair + 1) * LANES)
        a, b = 2 * pair, 2 * pair + 1
        key, value = split_lanes(load(a, 0, piece), load(b, 0, piece))
        gk_ref[:, cols] = key
        gv_ref[:, cols] = value
        top, bottom = split_lanes(load(a, piece, last), load(b, piece, last))
        gq_ref[: piece // 2, cols] = top
        gq_ref[piece // 2 :, cols] = bottom


def split_heads(packed):
    heads, height, _ = packed.shape
    grad = jax.ShapeDtypeStruct((height * 2 // 3, heads * HD), jnp.float32)
    return pl.pallas_call(
        split_heads_body,
        in_specs=[whole()],
        out_specs=[whole()] * 3,
        out_shape=[grad] * 3,
        compiler_params=params(),
        cost_estimate=cost(1 << 18, 1 << 20),
        name="split_heads",
    )(packed)


def out_sum_body(keep_ref, came_ref, out_ref):
    piece = out_ref.shape[1]
    for tile in range(out_ref.shape[0] // LANES):
        rows = slice(tile * piece, (tile + 1) * piece)
        total = keep_ref[0, rows].astype(jnp.float32) + came_ref[0, rows].astype(jnp.float32)
        out_ref[tile * LANES : (tile + 1) * LANES] = total.T


def out_sum(keep, came, width):
    piece = keep.shape[1] * LANES // width
    return pl.pallas_call(
        out_sum_body,
        in_specs=[whole()] * 2,
        out_specs=whole(),
        out_shape=jax.ShapeDtypeStruct((width, piece), jnp.float32),
        compiler_params=params(),
        cost_estimate=cost(1 << 17, 1 << 19),
        name="out_sum",
    )(keep, came)


def late_grad_body(orders, tiles, first_ref, *refs):
    *arrays, out_ref, turned_s, tile_s, sems = refs
    tile = tile_s.shape[2]
    terms = [arrays[index : index + 4] for index in range(0, len(arrays), 4)]
    first = first_ref[0] == 0

    def ordered(own, other):
        return (jnp.where(first, own, other), jnp.where(first, other, own))

    def columns(place):
        return pl.ds(pl.multiple_of(place * tile, tile), tile)

    def copy(place):
        slot = place % 2
        return pltpu.make_async_copy(tile_s.at[slot], out_ref.at[:, columns(place)], sems.at[slot])

    start = 0
    for index, (own, other, own_right, other_right) in enumerate(terms):
        half, depth = own.shape
        size = depth // len(orders[index])
        for place, chip in enumerate(orders[index]):
            cols = slice(chip * size, (chip + 1) * size)
            rows = slice(place * size, (place + 1) * size)
            for which, piece in enumerate(ordered(own[:, cols], other[:, cols])):
                turned_s[rows, which * half : (which + 1) * half] = piece.T

        def step(number, carry, start=start, own_right=own_right, other_right=other_right):
            place = start + number
            cols = columns(number)
            right = jnp.concatenate(ordered(own_right[:, cols], other_right[:, cols]), axis=0)

            @pl.when(place >= 2)
            def _():
                copy(place - 2).wait()

            tile_s[place % 2] = dot_nn(turned_s[...], right).astype(jnp.bfloat16)
            copy(place).start()
            return carry

        lax.fori_loop(0, tiles[index], step, 0)
        start += tiles[index]
    for place in range(start - 2, start):
        copy(place).wait()


def late_grad(first, chips, terms):
    half, depth = terms[0][0].shape
    tile = 1024
    orders = [ring_chips(chips) if term[4] else list(range(chips)) for term in terms]
    arrays = [array for term in terms for array in term[:4]]
    tiles = [term[2].shape[1] // tile for term in terms]
    width = sum(tiles) * tile
    return pl.pallas_call(
        functools.partial(late_grad_body, orders, tiles),
        in_specs=[pl.BlockSpec(memory_space=pltpu.SMEM)] + [whole()] * len(arrays),
        out_specs=pl.BlockSpec(memory_space=pl.ANY),
        out_shape=jax.ShapeDtypeStruct((depth, width), jnp.bfloat16),
        scratch_shapes=[
            pltpu.VMEM((depth, 2 * half), jnp.bfloat16),
            pltpu.VMEM((2, depth, tile), jnp.bfloat16),
            pltpu.SemaphoreType.DMA((2,)),
        ],
        compiler_params=params(limit=WIDE_LIMIT),
        cost_estimate=cost(4 * half * depth * width, 2 * depth * width + (3 << 20)),
        name="late_grad",
    )(first, *arrays)


def halve_body(place, info_ref, mine_ref, came_ref, keep_ref, send_ref):
    bit = info_ref[place]
    for index in range(keep_ref.shape[0]):
        for ref, block in ((keep_ref, 2 * index + bit), (send_ref, 2 * index + 1 - bit)):
            total = mine_ref[block].astype(jnp.float32) + came_ref[block].astype(jnp.float32)
            ref[index] = total.astype(jnp.bfloat16)


def halve(info, place, mine, came):
    count, height, width = mine.shape
    share = jax.ShapeDtypeStruct((count // 2, height, width), jnp.bfloat16)
    return pl.pallas_call(
        functools.partial(halve_body, place),
        in_specs=[pl.BlockSpec(memory_space=pltpu.SMEM)] + [whole()] * 2,
        out_specs=[whole()] * 2,
        out_shape=[share] * 2,
        compiler_params=params(),
        cost_estimate=cost(1 << 18, 2 << 20),
        name="halve",
    )(info, mine, came)


def widen_body(in_ref, out_ref):
    out_ref[...] = in_ref[...].astype(jnp.float32)


def widen(values):
    rows, width = values.shape
    steps = 2
    block = pl.BlockSpec((rows // steps, width), lambda i: (i, 0))
    return pl.pallas_call(
        widen_body,
        grid=(steps,),
        in_specs=[block],
        out_specs=block,
        out_shape=jax.ShapeDtypeStruct((rows, width), jnp.float32),
        compiler_params=params("arbitrary", limit=WIDE_LIMIT),
        cost_estimate=cost(1 << 20, 6 << 20),
        name="widen",
    )(values)


def out_grad_body(info_ref, left_ref, other_ref, ctx_ref, mine_ref, send_ref, grad_s):
    blocks, piece, width = grad_s.shape
    chips = blocks // 2
    parity = info_ref[2 * blocks]
    left = jnp.concatenate([left_ref[...], other_ref[...]], axis=0)
    grad_s[...] = contract_rows(left, ctx_ref[...]).reshape(blocks, piece, width)
    for chip in range(chips):
        for ref, block in ((mine_ref, 2 * chip + parity), (send_ref, 2 * chip + 1 - parity)):
            part = grad_s[block].astype(jnp.bfloat16)
            for tile in range(width // LANES):
                cols = slice(tile * LANES, (tile + 1) * LANES)
                ref[chip, tile * piece : (tile + 1) * piece] = part[:, cols]


def out_grad_pack(info, chips, grad_own, grad_other, context_low):
    depth = grad_own.shape[1]
    rows, width = context_low.shape
    piece = depth // (2 * chips)
    height = piece * width // LANES
    share = jax.ShapeDtypeStruct((chips, height, LANES), jnp.bfloat16)
    return pl.pallas_call(
        out_grad_body,
        in_specs=[pl.BlockSpec(memory_space=pltpu.SMEM)] + [whole()] * 3,
        out_specs=[whole()] * 2,
        out_shape=[share] * 2,
        scratch_shapes=[pltpu.VMEM((2 * chips, piece, width), jnp.float32)],
        compiler_params=params(),
        cost_estimate=cost(2 * rows * depth * width, 2 << 20),
        name="out_grad",
    )(info, grad_own, grad_other, context_low)


def norm_rows(values):
    centred = values - jnp.mean(values, axis=-1, keepdims=True)
    inverse = lax.rsqrt(jnp.mean(centred * centred, axis=-1, keepdims=True) + 1e-05)
    return centred * inverse, inverse


def back_rows(grad, gain, unit, inverse):
    scaled = grad * gain
    along = jnp.mean(scaled * unit, axis=-1, keepdims=True)
    return (scaled - jnp.mean(scaled, axis=-1, keepdims=True) - unit * along) * inverse


def store_sums(ref, grad, unit):
    width = ref.shape[1]
    for index, total in enumerate((jnp.sum(grad * unit, axis=0), jnp.sum(grad, axis=0))):
        for part in range(2):
            row = 2 * index + part
            ref[row : row + 1] = total[None, part * width : (part + 1) * width]


def attn_norm_back_body(
    pre_ref, own_ref, recv_ref, gain_ref, unit_ref, inv_ref, grad_ref, low_ref, sums_ref
):
    grad = pre_ref[...] + (own_ref[...].astype(jnp.float32) + recv_ref[...].astype(jnp.float32))
    unit = unit_ref[...]
    back = back_rows(grad, gain_ref[...], unit, inv_ref[:, 0:1])
    grad_ref[...] = back
    low_ref[...] = back.astype(jnp.bfloat16)
    store_sums(sums_ref, grad, unit)


def attn_norm_back(pre, own, recv, gain, unit, inverse, width):
    rows, depth = pre.shape
    return pl.pallas_call(
        attn_norm_back_body,
        in_specs=[whole()] * 6,
        out_specs=[whole()] * 3,
        out_shape=[
            jax.ShapeDtypeStruct((rows, depth), jnp.float32),
            jax.ShapeDtypeStruct((rows, depth), jnp.bfloat16),
            jax.ShapeDtypeStruct((4, width), jnp.float32),
        ],
        compiler_params=params(),
        cost_estimate=cost(1 << 20, 2 << 20),
        name="attn_norm_back",
    )(pre, own, recv, gain[None], unit, inverse)


def turn_body(
    hid_ref,
    own_ref,
    recv_ref,
    gain_ref,
    shift_ref,
    w_ref,
    pick_ref,
    cot_ref,
    out_ref,
    unit_ref,
    proj_ref,
    pre_ref,
    low_ref,
    sums_ref,
):
    values = hid_ref[...] + (own_ref[...].astype(jnp.float32) + recv_ref[...].astype(jnp.float32))
    unit, inverse = norm_rows(values)
    gain = gain_ref[...]
    output = (unit * gain + shift_ref[...]).astype(jnp.bfloat16)
    out_ref[...] = output
    proj = dot_nn(output, w_ref[...])
    scale = lax.rsqrt(jnp.sum(proj * proj, axis=1, keepdims=True) + 1e-06)
    vec = proj * scale
    unit_ref[...] = vec.astype(jnp.bfloat16)
    pick = pick_ref[...]
    along = jnp.sum(vec * pick, axis=1, keepdims=True)
    proj_low = ((pick - vec * along) * scale).astype(jnp.bfloat16)
    proj_ref[...] = proj_low
    grad = cot_ref[...] + dot_nt(proj_low, w_ref[...])
    pre = back_rows(grad, gain, unit, inverse)
    pre_ref[...] = pre
    low_ref[...] = pre.astype(jnp.bfloat16)
    store_sums(sums_ref, grad, unit)


def turn(hidden, own, recv, gain, shift, w_colbert, pick, cot, width):
    rows, depth = hidden.shape
    low = jax.ShapeDtypeStruct((rows, depth), jnp.bfloat16)
    return pl.pallas_call(
        turn_body,
        in_specs=[whole()] * 8,
        out_specs=[whole()] * 6,
        out_shape=[
            low,
            low,
            low,
            jax.ShapeDtypeStruct((rows, depth), jnp.float32),
            low,
            jax.ShapeDtypeStruct((4, width), jnp.float32),
        ],
        compiler_params=params(),
        cost_estimate=cost(4 * rows * depth * depth, 5 << 20),
        name="turn",
    )(hidden, own, recv, gain[None], shift[None], w_colbert, pick, cot)


def gelu_with_slope(values):
    cdf = 0.5 * (1.0 + lax.erf(values * 0.7071067811865476))
    density = jnp.exp(-0.5 * values * values) * 0.3989422804014327
    return values * cdf, cdf + values * density


def local_by_head(
    tokens,
    w_query,
    w_key,
    w_value,
    w_out,
    gain_attn,
    shift_attn,
    w_up,
    w_down,
    gain_ffn,
    shift_ffn,
    w_colbert,
    query_vecs,
    match_index,
    passage_of,
    cot_act,
    cot_scores,
):
    pass_count = lax.axis_size("pass")
    qry_count = lax.axis_size("qry")
    pass_index = lax.axis_index("pass")
    qry_index = lax.axis_index("qry")
    chips = pass_count // 2
    own_rows = tokens.shape[0]
    block_rows = own_rows * qry_count
    same_core = [[index for index in range(pass_count) if index % 2 == core] for core in (0, 1)]
    ring = [[2 * chip + core for chip in ring_chips(chips) for core in (0, 1)]]
    parity = pass_index % 2
    own_id = passage_of[pass_index]

    def swap(value):
        return swap_over(value, "qry", 1)

    def sibling(value):
        return swap_over(value, "pass", 1)

    def to_heads(value):
        return lax.all_to_all(
            value, "pass", 0, 0, axis_index_groups=same_core, tiled=True
        )

    def after(value, *others):
        return lax.optimization_barrier((value,) + others)[0]

    def together(*values):
        return lax.optimization_barrier(values)

    near_send = project(tokens, w_query, w_key, w_value)
    near_pack = to_heads(near_send)
    tokens_other = swap(tokens)
    gathered = jnp.concatenate([tokens, tokens_other], axis=0)
    block_ids = passage_of.astype(jnp.int32)
    same = block_ids[:, None] == block_ids[None, :]
    starts = jnp.sum((block_ids[None, :] < block_ids[:, None]).astype(jnp.int32), axis=1)
    counts = jnp.sum(same.astype(jnp.int32), axis=1)
    chip = (pass_index // 2).astype(jnp.int32)
    bits = chips.bit_length() - 1
    info = jnp.concatenate(
        [starts, counts, parity[None].astype(jnp.int32)]
        + [((chip >> bit) & 1)[None] for bit in range(bits)]
    )
    first_bit = 2 * pass_count + 1

    seq_count = match_index.shape[1]
    query_rows = cot_scores.shape[0]
    pick_col = jnp.arange(seq_count, dtype=jnp.int32) == own_id
    span_count = jnp.sum((passage_of == own_id).astype(jnp.int32))
    first_index = jnp.sum((passage_of < own_id).astype(jnp.int32))
    raw_pick = jnp.sum(jnp.where(pick_col[None, :], match_index, 0), axis=1)
    local_row = raw_pick % (span_count * block_rows) - (pass_index - first_index) * block_rows
    inside = (local_row >= 0) & (local_row < block_rows)
    local_row = jnp.where(inside, (local_row + qry_index * own_rows) % block_rows, -1)
    one_hot = (local_row[:, None] == jnp.arange(block_rows, dtype=jnp.int32)[None, :]).astype(
        jnp.bfloat16
    )
    cot_pick = jnp.sum(jnp.where(pick_col[None, :], cot_scores, 0.0), axis=1)
    token_weight = jnp.repeat(cot_pick, query_vecs.shape[0] // query_rows)
    query_float = query_vecs.astype(jnp.float32)
    weighted_queries = (token_weight[:, None] * query_float).astype(jnp.bfloat16)
    unit_grad_part = contract_rows(one_hot, weighted_queries)
    turned_part = jnp.concatenate([unit_grad_part[own_rows:], unit_grad_part[:own_rows]], axis=0)
    unit_grad_send = turned_part.astype(jnp.bfloat16)

    far_send = project(after(tokens_other, near_send), w_query, w_key, w_value)
    near_pack, far_send = together(near_pack, far_send)
    far_pack = to_heads(far_send)
    near_sib = sibling(near_pack)
    piece = w_out.shape[0] // 2
    w_out_send = lax.dynamic_slice_in_dim(w_out, parity * piece, piece, axis=0)
    w_out_mine = swap(after(w_out_send, tokens_other))
    w_out_sib = sibling(w_out_mine)
    far_pack, near_sib, unit_grad_send, w_out_sib, gathered = together(
        far_pack, near_sib, unit_grad_send, w_out_sib, gathered
    )
    packs = (near_pack, far_pack, near_sib, sibling(far_pack))
    unit_grad_recv = swap(unit_grad_send)
    cot_other = swap(after(cot_act, unit_grad_send))
    ctx_pack, ctx_turned, lse = attend(info, *packs)
    unit_grad = unit_grad_part.astype(jnp.bfloat16).astype(jnp.float32) + unit_grad_recv.astype(
        jnp.float32
    )
    unit_grad_own, unit_grad_other = unit_grad[:own_rows], unit_grad[own_rows:]
    ctx_recv = to_heads(ctx_pack)
    ready = prepare(info, after(near_pack, ctx_pack), *packs[1:])
    cot_near = after(cot_act, ctx_pack).astype(jnp.float32)
    cot_far = after(cot_other, ctx_pack).astype(jnp.float32)
    ctx_recv, unit_grad_own, unit_grad_other, cot_near, cot_far, kv, key_turned, query = together(
        ctx_recv, unit_grad_own, unit_grad_other, cot_near, cot_far, *ready
    )
    tokens_all = lax.all_gather(
        after(gathered, far_pack), "pass", axis=0, axis_index_groups=ring, tiled=True
    )
    (
        context_low,
        hidden,
        hidden_far,
        hidden_low,
        hidden_other,
        unit_attn,
        unit_attn_far,
        inverse_attn,
        inverse_attn_far,
    ) = out_norm(
        info,
        ctx_recv,
        swap(ctx_recv),
        w_out,
        w_out_mine,
        w_out_sib,
        gathered,
        gain_attn,
        shift_attn,
    )

    def activate(rows):
        gated, slope = gelu_with_slope(dot_nn(rows, w_up))
        return lax.optimization_barrier((gated.astype(jnp.bfloat16), slope))

    gated_other, slope_other = activate(hidden_other)
    gated_own, slope_own = activate(hidden_low)

    def both_halves(rows_own, rows_other, product):
        part_other = product(rows_other).astype(jnp.bfloat16)
        part_own = product(after(rows_own, part_other)).astype(jnp.bfloat16)
        recv_own = swap(part_other)
        recv_other = swap(part_own)
        return part_own, part_other, recv_own, recv_other

    part_own, part_other, recv_own, recv_other = both_halves(
        gated_own, gated_other, lambda rows: dot_nn(rows, w_down)
    )
    local_width = w_query.shape[1]
    width = w_up.shape[1]
    model = tokens.shape[1]

    def turned(rows, part, recv, pick, cot):
        return turn(
            rows, part, recv, gain_ffn, shift_ffn, w_colbert, pick, cot, local_width
        )

    output_low, unit_own, proj_own, pre_grad, pre_low, sums_ffn = turned(
        hidden, part_own, recv_own, unit_grad_own, cot_near
    )
    inner_own = (dot_nt(pre_low, w_down) * slope_own).astype(jnp.bfloat16)
    recv_other, inner_own = together(recv_other, inner_own)
    output_other, unit_other, proj_other, pre_far, pre_other, _ = turned(
        hidden_far, part_other, recv_other, unit_grad_other, cot_far
    )
    inner_other = (dot_nt(pre_other, w_down) * slope_other).astype(jnp.bfloat16)
    late = late_grad(
        qry_index[None].astype(jnp.int32),
        chips,
        (
            (hidden_low, hidden_other, inner_own, inner_other, True),
            (pre_low, pre_other, gated_own, gated_other, True),
            (output_low, output_other, proj_own, proj_other, False),
        ),
    )
    inner_own, inner_other, late = together(inner_own, inner_other, late)
    part_own, part_other, recv_own, recv_other = both_halves(
        inner_own, inner_other, lambda rows: dot_nt(rows, w_up)
    )
    late_sums = lax.psum_scatter(
        late, "pass", scatter_dimension=0, axis_index_groups=ring, tiled=True
    )

    def back_to_attn(pre, part, recv, unit, inverse):
        return attn_norm_back(pre, part, recv, gain_attn, unit, inverse, local_width)

    attn_pre, attn_low, sums_attn = back_to_attn(
        pre_grad, part_own, recv_own, unit_attn, inverse_attn
    )
    _, attn_other, _ = back_to_attn(
        pre_far, part_other, recv_other, unit_attn_far, inverse_attn_far
    )

    dctx_send = ctx_grad_packed(attn_low, attn_other, w_out)
    own_dctx = to_heads(dctx_send)
    out_mine, out_send = out_grad_pack(
        info, chips, after(attn_low, dctx_send), attn_other, context_low
    )
    own_dctx, out_mine, out_send = together(own_dctx, out_mine, out_send)
    mine, other, dq = attend_back(info, kv, key_turned, query, own_dctx, ctx_turned, lse)
    back_send = combine(mine, sibling(other), dq)
    back = to_heads(back_send)
    back_own, out_send, unit_other = together(back_send, out_send, unit_other)

    out_keep, out_send = halve(info, first_bit, out_mine, sibling(out_send))
    out_came = swap_over(out_send, "pass", 2)
    unit_other = after(unit_other, out_send)
    picked = dot_nn(one_hot, jnp.concatenate([unit_own, unit_other], axis=0))
    per_query = jnp.sum((query_float * picked).reshape(query_rows, -1), axis=1)
    score_block = per_query[:, None] * pick_col.astype(jnp.float32)[None, :]
    score_part = lax.dynamic_update_slice(
        jnp.zeros((query_rows * qry_count, seq_count), jnp.float32),
        score_block,
        (qry_index * query_rows, jnp.zeros((), jnp.int32)),
    )
    score_rows = jnp.pad(score_part.reshape(1, -1), ((0, 7), (0, local_width - score_part.size)))
    small = jnp.concatenate([sums_attn, sums_ffn, score_rows], axis=0)
    small = small + swap(small)
    small = small + sibling(small)
    head_grads = head_grad(info, tokens_all, back_own, sibling(back_own))
    back, head_grads, small, late_sums = together(back, head_grads, small, late_sums)
    head_recv = to_heads(head_grads)
    token_own, token_send = token_grad(back, w_query, w_key, w_value)
    token_recv = swap(token_send)
    colbert_all = lax.all_gather(
        late_sums[:, 2 * width :], "pass", axis=0, axis_index_groups=ring, tiled=True
    )
    out_keep = after(out_keep, token_recv)
    for step in range(1, bits):
        out_keep, out_send = halve(info, first_bit + step, out_keep, out_came)
        out_came = swap_over(out_send, "pass", 2 << step)
    for step in range(bits):
        small = small + swap_over(small, "pass", 2 << step)
    grad_out = out_sum(out_keep, out_came, local_width)
    grad_tokens = attn_pre + token_own + token_recv.astype(jnp.float32)
    grad_query, grad_key, grad_value = split_heads(after(head_recv, token_recv))
    grad_up = late_sums[:, :width].astype(jnp.float32)
    grad_down = late_sums[:, width : 2 * width].astype(jnp.float32).T
    grad_colbert = widen(after(colbert_all, grad_up, grad_down, grad_out))
    norms = small[:8].reshape(4, model)
    scores = small[8].reshape(-1)[: score_part.size].reshape(score_part.shape)
    return (
        output_low,
        scores,
        grad_tokens,
        grad_query,
        grad_key,
        grad_value,
        grad_out,
        grad_up,
        grad_down,
        grad_colbert,
        norms[0],
        norms[1],
        norms[2],
        norms[3],
    )


def solution(mesh):
    by_head = mesh.shape["qry"] == 2
    return jax.shard_map(
        local_by_head if by_head else local_general,
        mesh=mesh,
        in_specs=(
            P(("pass", "qry"), None),
            P(None, "qry"),
            P(None, "qry"),
            P(None, "qry"),
            P("qry", None),
            P(),
            P(),
            P(None, "qry"),
            P("qry", None),
            P(),
            P(),
            P(),
            P("qry", None),
            P("qry", None),
            P(),
            P(("pass", "qry"), None),
            P("qry", None),
        ),
        out_specs=(
            P(("pass", "qry"), None),
            P(),
            P(("pass", "qry"), None),
            P("pass", "qry"),
            P("pass", "qry"),
            P("pass", "qry"),
            P("qry", "pass"),
            P("pass", "qry"),
            P("qry", "pass"),
            P(),
            P(),
            P(),
            P(),
            P(),
        ),
        check_vma=False,
    )
```
